32 devices in a mesh: tok: 2 (over x), patch: 16 (over z, y, core).
Axes of the slice: x: 2, y: 2, z: 4, core: 2. Of those that a mesh axis runs over, the one named last changes fastest.
Arguments:
- tokens: bfloat16 [16, 1536, 1024], P('patch', 'tok'), may hold values from -6 to 6
- patches: bfloat16 [1024, 1024], P(('tok', 'patch')), may hold values from -6 to 6
- cotangent: bfloat16 [16, 1536, 1024], P('patch', 'tok'), may hold values from -6 to 6
- lengths: int32 [16], replicated, may hold values from 1 to 1536, 18432 in all
- page_of: int32 [16], replicated, may hold values from 0 to 1
- page_counts: int32 [2], replicated, may hold values from 1 to 512, as said below
- self_gain: float32 [1024], replicated, may hold values from 0.5 to 1.5
- self_shift: float32 [1024], replicated, may hold values from -1 to 1
- query_weight: bfloat16 [1024, 1024], replicated, may hold values from -0.1875 to 0.1875
- query_bias: float32 [1024], replicated, may hold values from -1.5 to 1.5
- key_weight: bfloat16 [1024, 1024], replicated, may hold values from -0.1875 to 0.1875
- value_weight: bfloat16 [1024, 1024], replicated, may hold values from -0.1875 to 0.1875
- value_bias: float32 [1024], replicated, may hold values from -1.5 to 1.5
- output_weight: bfloat16 [1024, 1024], replicated, may hold values from -1.5 to 1.5
- output_bias: float32 [1024], replicated, may hold values from -1.5 to 1.5
- cross_gain: float32 [1024], replicated, may hold values from 0.5 to 1.5
- cross_shift: float32 [1024], replicated, may hold values from -1 to 1
- probe_weight: bfloat16 [1024, 1024], replicated, may hold values from -0.1875 to 0.1875
- probe_bias: float32 [1024], replicated, may hold values from -1.5 to 1.5
- source_key: bfloat16 [1024, 1024], replicated, may hold values from -0.1875 to 0.1875
- source_value: bfloat16 [1024, 1024], replicated, may hold values from -0.1875 to 0.1875
- source_bias: float32 [1024], replicated, may hold values from -1.5 to 1.5
- merge_weight: bfloat16 [1024, 1024], replicated, may hold values from -1.5 to 1.5
- merge_bias: float32 [1024], replicated, may hold values from -1.5 to 1.5
- feed_gain: float32 [1024], replicated, may hold values from 0.5 to 1.5
- feed_shift: float32 [1024], replicated, may hold values from -1 to 1
- expand_weight: bfloat16 [1024, 4096], replicated, may hold values from -0.1875 to 0.1875
- expand_bias: float32 [4096], replicated, may hold values from -1.5 to 1.5
- reduce_weight: bfloat16 [4096, 1024], replicated, may hold values from -0.09375 to 0.09375
- reduce_bias: float32 [1024], replicated, may hold values from -1.5 to 1.5
Outputs:
- block_output: bfloat16 [16, 1536, 1024], P('patch', 'tok')
- tokens_grad: float32 [16, 1536, 1024], P('patch', 'tok')
- patches_grad: float32 [1024, 1024], P(('tok', 'patch'))
- self_gain_grad: float32 [1024], P(('tok', 'patch'))
- self_shift_grad: float32 [1024], P(('tok', 'patch'))
- query_weight_grad: float32 [1024, 1024], P(('tok', 'patch'))
- query_bias_grad: float32 [1024], P(('tok', 'patch'))
- key_weight_grad: float32 [1024, 1024], P(('tok', 'patch'))
- value_weight_grad: float32 [1024, 1024], P(('tok', 'patch'))
- value_bias_grad: float32 [1024], P(('tok', 'patch'))
- output_weight_grad: float32 [1024, 1024], P(('tok', 'patch'))
- output_bias_grad: float32 [1024], P(('tok', 'patch'))
- cross_gain_grad: float32 [1024], P(('tok', 'patch'))
- cross_shift_grad: float32 [1024], P(('tok', 'patch'))
- probe_weight_grad: float32 [1024, 1024], P(('tok', 'patch'))
- probe_bias_grad: float32 [1024], P(('tok', 'patch'))
- source_key_grad: float32 [1024, 1024], P(('tok', 'patch'))
- source_value_grad: float32 [1024, 1024], P(('tok', 'patch'))
- source_bias_grad: float32 [1024], P(('tok', 'patch'))
- merge_weight_grad: float32 [1024, 1024], P(('tok', 'patch'))
- merge_bias_grad: float32 [1024], P(('tok', 'patch'))
- feed_gain_grad: float32 [1024], P(('tok', 'patch'))
- feed_shift_grad: float32 [1024], P(('tok', 'patch'))
- expand_weight_grad: float32 [1024, 4096], P(('tok', 'patch'))
- expand_bias_grad: float32 [4096], P(('tok', 'patch'))
- reduce_weight_grad: float32 [4096, 1024], P(('tok', 'patch'))
- reduce_bias_grad: float32 [1024], P(('tok', 'patch'))
The draws below stay inside these ranges and needn't reach their ends.
Inputs may be any that keep to these rules, and one draw needn't show every extreme that they name: The 16 lengths sum to 18432, and one equals 1536. `page_counts`: one page holds exactly 512 patches.
All inputs are finite; a program needn't handle non-finite values.
Results may differ from the reference program's by a relative error of at most 0.03.
Values may be sent and summed in bfloat16 or wider, within the bound.
No kernel may reach another device: no remote copies, remote signals or barrier semaphores. Data moves between devices by JAX's collectives and lax.ppermute only.
A program may use at most 320 MiB of HBM per device.

```python
import math
import jax
import jax.numpy as jnp
import numpy as np
from jax import lax

D = 1024
HEADS = 16
HDIM = 64
FF = 4096
PAGE_SLOTS = 512
LEN_MAX = 1536
SEQS = 16
PATCHES = 1024
PAGES = 2


def draw_page_counts(key, part):
    full_key = jax.random.fold_in(key, 11)
    rest_key = jax.random.fold_in(key, 23)
    full_page = jax.random.randint(full_key, (), 0, PAGES, dtype=jnp.int32)
    others = jax.random.randint(rest_key, (PAGES,), PAGE_SLOTS // 4, PAGE_SLOTS, dtype=jnp.int32)
    page_ids = jnp.arange(PAGES, dtype=jnp.int32)
    return jnp.where(page_ids == full_page, jnp.int32(PAGE_SLOTS), others).astype(jnp.int32)


def touch_ends(drawn, rng, smallest, top_value):
    place = [jax.random.randint(jax.random.fold_in(rng, axis), (), 0, length) for axis, length in enumerate(drawn.shape)]
    widest = drawn.shape.index(max(drawn.shape))
    next_to = place[:widest] + [(place[widest] + 1) % drawn.shape[widest]] + place[widest + 1:]
    return drawn.at[tuple(place)].set(smallest).at[tuple(next_to)].set(top_value)


def block_levels(rng, extent, pieces, low, high):
    loudness = 1.0
    for position, shards_of in pieces:
        heights = jax.random.uniform(jax.random.fold_in(jax.random.fold_in(rng, 6), position), (shards_of,), jnp.float32, low / len(pieces), high / len(pieces))
        loudness = loudness * jnp.repeat(jnp.exp(heights), extent[position] // shards_of).reshape((-1,) + (1,) * (len(extent) - 1 - position))
    return loudness


def profile(count, total, bound, slope):
    loads = [(1 << 20) // math.isqrt(rank ** slope) + 1 for rank in range(2, count + 1)]
    spare, counts = total - bound - (count - 1), [1] * (count - 1)
    while spare > 0:
        movable = [i for i in range(count - 1) if counts[i] < bound]
        pool, remaining = sum([loads[i] for i in movable]), spare
        for i in movable:
            addition = min(bound - counts[i], max(1, remaining * loads[i] // pool), spare)
            counts[i] = counts[i] + addition
            spare = spare - addition
    return np.array([bound] + counts)


def uneven(own_key, number_of, total, bound, skew):
    if number_of == 2:
        one = jax.random.randint(own_key, (), max(1, total - bound), min(bound, total - 1) + 1)
        return jnp.stack([one, total - one])
    tallies = jnp.asarray(profile(number_of, total, bound, skew), jnp.int32)
    pairs = (number_of - 1) // 2
    giver, taker = tallies[1:1 + 2 * pairs:2], tallies[2:2 + 2 * pairs:2]
    room = jnp.minimum(giver - 1, bound - taker)
    moved = jax.random.randint(jax.random.fold_in(own_key, 1), (pairs,), 0, 1 << 20) % (room + 1)
    tallies = tallies.at[1:1 + 2 * pairs:2].set(giver - moved).at[2:2 + 2 * pairs:2].set(taker + moved)
    return tallies[jax.random.permutation(jax.random.fold_in(own_key, 2), number_of)]


def normal_values(rng, extent, scale, limit, pieces=(), kind=jnp.bfloat16):
    drawn = scale * jax.random.normal(rng, extent, jnp.float32)
    if pieces:
        drawn = drawn * block_levels(rng, extent, pieces, -0.22, 0.18)
    return jnp.clip(drawn, -limit, limit).astype(kind)


def setup_inputs(seed: int = 0) -> dict:
    keys = jax.random.split(jax.random.key(seed), 31)
    tokens = normal_values(keys[0], (SEQS, LEN_MAX, D), 1.0, 6.0, ((0, 16), (1, 2)))
    patches = normal_values(keys[1], (PATCHES, D), 1.0, 6.0, ((0, 32),))
    cotangent = normal_values(keys[2], (SEQS, LEN_MAX, D), 1.0, 6.0, ((0, 16), (1, 2)))
    lengths = uneven(keys[3], SEQS, SEQS * LEN_MAX * 3 // 4, LEN_MAX, 1).astype(jnp.int32)
    page_of = touch_ends(jax.random.randint(keys[4], (SEQS,), 0, PAGES), jax.random.fold_in(keys[4], 1), 0, PAGES - 1).astype(jnp.int32)
    page_counts = draw_page_counts(jax.random.fold_in(keys[30], 71), 0)
    self_gain = jnp.clip(1.0 + 0.1 * jax.random.normal(keys[6], (D,), jnp.float32), 0.5, 1.5)
    self_shift = normal_values(keys[7], (D,), 0.2, 1.0, (), jnp.float32)
    query_weight = normal_values(keys[8], (D, D), D ** -0.5, 0.1875)
    query_bias = normal_values(keys[9], (D,), 0.3, 1.5, (), jnp.float32)
    key_weight = normal_values(keys[10], (D, D), D ** -0.5, 0.1875)
    value_weight = normal_values(keys[11], (D, D), D ** -0.5, 0.1875)
    value_bias = normal_values(keys[12], (D,), 0.3, 1.5, (), jnp.float32)
    output_weight = normal_values(keys[13], (D, D), (D // 64) ** -0.5, 1.5)
    output_bias = normal_values(keys[14], (D,), 0.3, 1.5, (), jnp.float32)
    cross_gain = jnp.clip(1.0 + 0.1 * jax.random.normal(keys[15], (D,), jnp.float32), 0.5, 1.5)
    cross_shift = normal_values(keys[16], (D,), 0.2, 1.0, (), jnp.float32)
    probe_weight = normal_values(keys[17], (D, D), D ** -0.5, 0.1875)
    probe_bias = normal_values(keys[18], (D,), 0.3, 1.5, (), jnp.float32)
    source_key = normal_values(keys[19], (D, D), D ** -0.5, 0.1875)
    source_value = normal_values(keys[20], (D, D), D ** -0.5, 0.1875)
    source_bias = normal_values(keys[21], (D,), 0.3, 1.5, (), jnp.float32)
    merge_weight = normal_values(keys[22], (D, D), (D // 64) ** -0.5, 1.5)
    merge_bias = normal_values(keys[23], (D,), 0.3, 1.5, (), jnp.float32)
    feed_gain = jnp.clip(1.0 + 0.1 * jax.random.normal(keys[24], (D,), jnp.float32), 0.5, 1.5)
    feed_shift = normal_values(keys[25], (D,), 0.2, 1.0, (), jnp.float32)
    expand_weight = normal_values(keys[26], (D, FF), D ** -0.5, 0.1875)
    expand_bias = normal_values(keys[27], (FF,), 0.3, 1.5, (), jnp.float32)
    reduce_weight = normal_values(keys[28], (FF, D), FF ** -0.5, 0.09375)
    reduce_bias = normal_values(keys[29], (D,), 0.3, 1.5, (), jnp.float32)
    return dict(tokens=tokens, patches=patches, cotangent=cotangent, lengths=lengths, page_of=page_of, page_counts=page_counts, self_gain=self_gain, self_shift=self_shift, query_weight=query_weight, query_bias=query_bias, key_weight=key_weight, value_weight=value_weight, value_bias=value_bias, output_weight=output_weight, output_bias=output_bias, cross_gain=cross_gain, cross_shift=cross_shift, probe_weight=probe_weight, probe_bias=probe_bias, source_key=source_key, source_value=source_value, source_bias=source_bias, merge_weight=merge_weight, merge_bias=merge_bias, feed_gain=feed_gain, feed_shift=feed_shift, expand_weight=expand_weight, expand_bias=expand_bias, reduce_weight=reduce_weight, reduce_bias=reduce_bias)


HIGH = lax.Precision.HIGHEST
NEG_FILL = -1e+30
EPS_NORM = 1e-05

@jax.custom_vjp
def low(v):
    return lax.optimization_barrier(v.astype(jnp.bfloat16)).astype(jnp.float32)

@jax.custom_vjp
def low_back(v):
    return v

def low_keep(v):
    return (low(v), None)

def low_pass(kept, grad):
    return (grad,)

def back_keep(v):
    return (v, None)

def back_low(kept, grad):
    return (low(grad),)
low.defvjp(low_keep, low_pass)
low_back.defvjp(back_keep, back_low)

def product(left, right):
    return jnp.dot(left, right, precision=HIGH)

def layer_norm(values, gain, shift):
    average = lax.optimization_barrier(jnp.mean(values, axis=-1, keepdims=True))
    centred = values - average
    spread = lax.optimization_barrier(jnp.mean(centred * centred, axis=-1, keepdims=True))
    return centred * lax.rsqrt(spread + EPS_NORM) * gain + shift

def attend(query, key_rows, value_rows, allowed):
    query_heads = query.reshape(query.shape[0], HEADS, HDIM)
    key_heads = key_rows.reshape(key_rows.shape[0], HEADS, HDIM)
    value_heads = value_rows.reshape(value_rows.shape[0], HEADS, HDIM)
    scores = low_back(jnp.einsum('qhd,khd->hqk', query_heads, key_heads, precision=HIGH))
    scores = jnp.where(allowed[None], scores, NEG_FILL)
    row_max = lax.optimization_barrier(jnp.max(scores, axis=-1, keepdims=True))
    exponent = jnp.exp(scores - row_max)
    soft_weights = low(exponent / lax.optimization_barrier(jnp.sum(exponent, axis=-1, keepdims=True)))
    mixed_heads = jnp.einsum('hqk,khd->qhd', soft_weights, value_heads, precision=HIGH)
    return mixed_heads.reshape(query.shape[0], HEADS * HDIM)

def layer(inputs, patch_rows, weights, lengths, page_of, page_counts):
    self_gain, self_shift, query_weight, query_bias, key_weight, value_weight, value_bias, output_weight, output_bias, cross_gain, cross_shift, probe_weight, probe_bias, source_key, source_value, source_bias, merge_weight, merge_bias, feed_gain, feed_shift, expand_weight, expand_bias, reduce_weight, reduce_bias = weights
    head_scale = HDIM ** (-0.5)
    places = jnp.arange(LEN_MAX, dtype=jnp.int32)
    slots = jnp.arange(PAGE_SLOTS, dtype=jnp.int32)
    page_ids = jnp.arange(PAGES, dtype=jnp.int32)
    flat = inputs.reshape(SEQS * LEN_MAX, D)
    hidden = low(layer_norm(flat, self_gain, self_shift))
    query = low(low_back((product(hidden, query_weight) + query_bias) * head_scale))
    self_keys = low(low_back(product(hidden, key_weight)))
    self_values = low(low_back(product(hidden, value_weight) + value_bias))

    def self_block(block_item):
        block_query, block_keys, block_values, length = block_item
        allowed = (places[None, :] <= places[:, None]) & (places[None, :] < length)
        return attend(block_query, block_keys, block_values, allowed)
    self_mixed = lax.map(jax.checkpoint(self_block), (query.reshape(SEQS, LEN_MAX, D), self_keys.reshape(SEQS, LEN_MAX, D), self_values.reshape(SEQS, LEN_MAX, D), lengths))
    self_mixed = low(low_back(self_mixed.reshape(SEQS * LEN_MAX, D)))
    after_one = flat + low_back(product(self_mixed, output_weight) + output_bias)
    hidden = low(layer_norm(after_one, cross_gain, cross_shift))
    probe = low(low_back((product(hidden, probe_weight) + probe_bias) * head_scale))
    patch_keys = low(product(patch_rows, source_key))
    patch_values = low(product(patch_rows, source_value) + source_bias)

    def cross_block(block_item):
        block_query, page_index = block_item
        page_start = (page_index * PAGE_SLOTS).astype(jnp.int32)
        page_keys = lax.dynamic_slice_in_dim(patch_keys, page_start, PAGE_SLOTS, 0)
        page_values = lax.dynamic_slice_in_dim(patch_values, page_start, PAGE_SLOTS, 0)
        filled = jnp.sum(jnp.where(page_ids == page_index, page_counts, 0))
        allowed = jnp.broadcast_to((slots < filled)[None, :], (LEN_MAX, PAGE_SLOTS))
        return attend(block_query, page_keys, page_values, allowed)
    cross_mixed = lax.map(jax.checkpoint(cross_block), (probe.reshape(SEQS, LEN_MAX, D), page_of))
    cross_mixed = low(low_back(cross_mixed.reshape(SEQS * LEN_MAX, D)))
    after_two = after_one + low_back(product(cross_mixed, merge_weight) + merge_bias)
    hidden = low(layer_norm(after_two, feed_gain, feed_shift))
    pre_act = low_back(product(hidden, expand_weight) + expand_bias)
    activated = low(jax.nn.gelu(pre_act, approximate=False))
    branch = low_back(product(activated, reduce_weight) + reduce_bias)
    valid = (places[None, :] < lengths[:, None]).astype(jnp.float32).reshape(SEQS * LEN_MAX, 1)
    return (valid * (after_two + branch)).reshape(SEQS, LEN_MAX, D)

def reference(tokens, patches, cotangent, lengths, page_of, page_counts, self_gain, self_shift, query_weight, query_bias, key_weight, value_weight, value_bias, output_weight, output_bias, cross_gain, cross_shift, probe_weight, probe_bias, source_key, source_value, source_bias, merge_weight, merge_bias, feed_gain, feed_shift, expand_weight, expand_bias, reduce_weight, reduce_bias):
    weights = (self_gain, self_shift, query_weight, query_bias, key_weight, value_weight, value_bias, output_weight, output_bias, cross_gain, cross_shift, probe_weight, probe_bias, source_key, source_value, source_bias, merge_weight, merge_bias, feed_gain, feed_shift, expand_weight, expand_bias, reduce_weight, reduce_bias)
    float_weights = tuple((member.astype(jnp.float32) for member in weights))

    def wrapped(inputs, patch_rows, float_params):
        return layer(inputs, patch_rows, float_params, lengths, page_of, page_counts)
    output, pullback = jax.vjp(wrapped, tokens.astype(jnp.float32), patches.astype(jnp.float32), float_weights)
    tokens_grad, patches_grad, param_grads = pullback(cotangent.astype(jnp.float32))
    return (output.astype(jnp.bfloat16), tokens_grad, patches_grad, param_grads[0], param_grads[1], param_grads[2], param_grads[3], param_grads[4], param_grads[5], param_grads[6], param_grads[7], param_grads[8], param_grads[9], param_grads[10], param_grads[11], param_grads[12], param_grads[13], param_grads[14], param_grads[15], param_grads[16], param_grads[17], param_grads[18], param_grads[19], param_grads[20], param_grads[21], param_grads[22], param_grads[23])
```

```python
import jax
import jax.numpy as jnp
from jax import lax
from jax.sharding import PartitionSpec as P

HDIM = 64
PAGE_SLOTS = 512


HIGH = lax.Precision.HIGHEST
NEG_FILL = -1e30
EPS_NORM = 1e-05
group_count = 4


def passed_along(value, axis, by):
    count = lax.axis_size(axis)
    pairs = [(i, i + by) for i in range(count) if 0 <= i + by < count]
    return lax.ppermute(value, axis, pairs)


def pick_entry(table, position):
    indices = jnp.arange(table.shape[0], dtype=jnp.int32)
    return jnp.sum(jnp.where(indices == position, table, 0))


def layer_norm(values, gain, shift):
    average = jnp.mean(values, axis=-1, keepdims=True)
    centred = values - average
    spread = jnp.mean(centred * centred, axis=-1, keepdims=True)
    inverse = lax.rsqrt(spread + EPS_NORM)
    normed = centred * inverse
    return (normed * gain + shift, normed, inverse)


def norm_backward(upstream, normed, inverse, gain):
    gain_part = jnp.sum(upstream * normed, axis=0)
    shift_part = jnp.sum(upstream, axis=0)
    scaled = upstream * gain
    centred = scaled - jnp.mean(scaled, axis=-1, keepdims=True)
    centred = centred - normed * jnp.mean(scaled * normed, axis=-1, keepdims=True)
    return (centred * inverse, gain_part, shift_part)


def product(left, right):
    return jnp.dot(left, right, preferred_element_type=jnp.float32)


def product_tn(left, right):
    return lax.dot_general(
        left, right, (((0,), (0,)), ((), ())), preferred_element_type=jnp.float32
    )


def product_nt(left, right):
    return lax.dot_general(
        left, right, (((1,), (1,)), ((), ())), preferred_element_type=jnp.float32
    )


def precise_tn(left, right):
    return lax.dot_general(
        left, right, (((0,), (0,)), ((), ())), precision=HIGH, preferred_element_type=jnp.float32
    )


def precise_nt(left, right):
    return lax.dot_general(
        left, right, (((1,), (1,)), ((), ())), precision=HIGH, preferred_element_type=jnp.float32
    )


def by_groups(matrix):
    row_count, model_width = matrix.shape
    return jnp.transpose(
        matrix.reshape(row_count, group_count, model_width // group_count), (1, 0, 2)
    )


def from_groups(stacked):
    return jnp.transpose(stacked, (1, 0, 2)).reshape(stacked.shape[1], -1)


def split_heads(matrix):
    return matrix.reshape(matrix.shape[0], matrix.shape[1] // HDIM, HDIM)


def group_scores(query, key_rows, allowed):
    scores = jnp.einsum(
        "qhd,khd->hqk",
        split_heads(query),
        split_heads(key_rows),
        preferred_element_type=jnp.float32,
    )
    return jnp.where(allowed[None], scores, NEG_FILL)


def group_forward(query, key_rows, value_rows, allowed):
    scores = group_scores(query, key_rows, allowed)
    row_max = jnp.max(scores, axis=-1, keepdims=True)
    exponent = jnp.exp(scores - row_max)
    row_total = jnp.sum(exponent, axis=-1, keepdims=True)
    soft_weights = (exponent / row_total).astype(jnp.bfloat16)
    mixed_heads = jnp.einsum(
        "hqk,khd->qhd", soft_weights, split_heads(value_rows), preferred_element_type=jnp.float32
    )
    return (mixed_heads.reshape(query.shape[0], -1), (row_max + jnp.log(row_total))[..., 0])


def attend_forward(query, key_rows, value_rows, allowed):

    def one_group(members):
        return group_forward(members[0], members[1], members[2], allowed)

    mixed_heads, log_total = lax.map(
        one_group, (by_groups(query), by_groups(key_rows), by_groups(value_rows))
    )
    return (from_groups(mixed_heads), log_total)


def group_backward(query, key_rows, value_rows, allowed, log_total, upstream):
    scores = group_scores(query, key_rows, allowed)
    soft_weights = jnp.exp(scores - log_total[..., None])
    upstream_heads = split_heads(upstream)
    grad_weights = jnp.einsum(
        "qhd,khd->hqk", upstream_heads, split_heads(value_rows), preferred_element_type=jnp.float32
    )
    grad_values = jnp.einsum(
        "hqk,qhd->khd",
        soft_weights.astype(jnp.bfloat16),
        upstream_heads,
        preferred_element_type=jnp.float32,
    )
    row_inner = jnp.sum(soft_weights * grad_weights, axis=-1, keepdims=True)
    grad_scores = (soft_weights * (grad_weights - row_inner)).astype(jnp.bfloat16)
    grad_query = jnp.einsum(
        "hqk,khd->qhd", grad_scores, split_heads(key_rows), preferred_element_type=jnp.float32
    )
    grad_keys = jnp.einsum(
        "hqk,qhd->khd", grad_scores, split_heads(query), preferred_element_type=jnp.float32
    )
    return (
        grad_query.reshape(query.shape[0], -1),
        grad_keys.reshape(key_rows.shape[0], -1),
        grad_values.reshape(value_rows.shape[0], -1),
    )


def attend_backward(query, key_rows, value_rows, allowed, log_total, upstream):

    def one_group(members):
        return group_backward(members[0], members[1], members[2], allowed, members[3], members[4])

    group_grads = lax.map(
        one_group,
        (
            by_groups(query),
            by_groups(key_rows),
            by_groups(value_rows),
            log_total,
            by_groups(upstream),
        ),
    )
    return (from_groups(group_grads[0]), from_groups(group_grads[1]), from_groups(group_grads[2]))


def exact_gelu(values):
    return jax.nn.gelu(values, approximate=False)


def other_of(value, axis, flip):
    pairs = [(i, i ^ flip) for i in range(lax.axis_size(axis))]
    return lax.ppermute(value, axis, pairs)


def digit_axes():
    patch_bits = lax.axis_size("patch").bit_length() - 1
    return [("tok", 0)] + [("patch", bit) for bit in reversed(range(patch_bits))]


def my_digit(axis, bit):
    return (lax.axis_index(axis) >> bit) & 1


def halve(stacked, place, axis, bit):
    mine = my_digit(axis, bit)
    leaving = lax.dynamic_index_in_dim(stacked, 1 - mine, place, keepdims=False)
    staying = lax.dynamic_index_in_dim(stacked, mine, place, keepdims=False)
    arrived = other_of(leaving, axis, 1 << bit)
    total = staying.astype(jnp.float32) + arrived.astype(jnp.float32)
    return total.astype(stacked.dtype)


def halve_all(stacked, order):
    axes = digit_axes()
    left = list(axes)
    for step in order:
        place = left.index(step)
        stacked = halve(stacked, place, *step)
        left.pop(place)
    return stacked


def split_order(first):
    rest = [step for step in reversed(digit_axes()) if step not in (("patch", 0), ("tok", 0))]
    if first == "tok":
        return [("tok", 0)] + rest
    return rest[:1] + [("tok", 0)] + rest[1:]


def scatter_columns(make_half, width, first):
    half = width // 2
    core = my_digit("patch", 0)
    leaving = make_half((1 - core) * half, half, None).astype(jnp.bfloat16)
    arrived = other_of(leaving, "patch", 1)
    total = make_half(core * half, half, arrived).astype(jnp.bfloat16)
    digits = len(digit_axes())
    rows = total.shape[0] >> digits
    stacked = total.reshape((2,) * digits + (rows, half))
    both = halve_all(stacked, split_order(first))
    own = lax.dynamic_index_in_dim(both, core, 0, keepdims=False)
    given = lax.dynamic_index_in_dim(both, 1 - core, 0, keepdims=False)
    taken = other_of(given, "patch", 1)
    low_half = jnp.where(core == 0, own, taken)
    high_half = jnp.where(core == 0, taken, own)
    return jnp.concatenate([low_half, high_half], axis=1).astype(jnp.float32)


def scatter_product(left, right, first):
    def make_half(start, size, added):
        part = product_tn(left, lax.dynamic_slice_in_dim(right, start, size, 1))
        return part if added is None else part + added.astype(jnp.float32)

    return scatter_columns(make_half, right.shape[1], first)


def scatter_vectors(vectors):
    digits = len(digit_axes())
    owners = 1 << digits
    widths = [vector.shape[0] // owners for vector in vectors]
    table = jnp.concatenate(
        [vector.reshape(owners, -1) for vector in vectors], axis=1
    )
    spare = -table.shape[1] % 128
    table = jnp.pad(table, ((0, 0), (0, spare)))
    stacked = table.reshape((2,) * digits + (table.shape[1],))
    mine = halve_all(stacked, [("patch", 0)] + split_order("tok"))
    pieces, start = [], 0
    for width in widths:
        pieces.append(mine[start : start + width])
        start += width
    return pieces


def local(
    tokens,
    patches,
    cotangent,
    lengths,
    page_of,
    page_counts,
    self_gain,
    self_shift,
    query_weight,
    query_bias,
    key_weight,
    value_weight,
    value_bias,
    output_weight,
    output_bias,
    cross_gain,
    cross_shift,
    probe_weight,
    probe_bias,
    source_key,
    source_value,
    source_bias,
    merge_weight,
    merge_bias,
    feed_gain,
    feed_shift,
    expand_weight,
    expand_bias,
    reduce_weight,
    reduce_bias,
):
    bf16, f32 = jnp.bfloat16, jnp.float32
    head_scale = HDIM ** (-0.5)
    tok_index = lax.axis_index("tok")
    sequence = lax.axis_index("patch")
    row_count = tokens.shape[1]
    model_width = tokens.shape[2]
    lead_tokens = passed_along(tokens[0], "tok", 1)
    gathered = lax.all_gather(patches, ("tok", "patch"), axis=0, tiled=True)
    inputs = tokens[0].astype(f32)
    length = pick_entry(lengths, sequence)
    page_index = pick_entry(page_of, sequence)
    filled = pick_entry(page_counts, page_index)
    page_start = page_index * PAGE_SLOTS
    places = tok_index * row_count + jnp.arange(row_count, dtype=jnp.int32)
    valid_rows = (places < length).astype(f32)[:, None]
    normed_one, unit_one, inverse_one = layer_norm(inputs, self_gain, self_shift)
    hidden_one = normed_one.astype(bf16)
    query = ((product(hidden_one, query_weight) + query_bias) * head_scale).astype(bf16)
    own_keys = product(hidden_one, key_weight).astype(bf16)
    own_values = (product(hidden_one, value_weight) + value_bias).astype(bf16)
    normed_lead, unit_lead, _ = layer_norm(lead_tokens.astype(f32), self_gain, self_shift)
    hidden_lead = normed_lead.astype(bf16)
    lead_keys = product(hidden_lead, key_weight).astype(bf16)
    lead_values = (product(hidden_lead, value_weight) + value_bias).astype(bf16)
    self_keys = jnp.concatenate([lead_keys, own_keys], axis=0)
    self_values = jnp.concatenate([lead_values, own_values], axis=0)
    key_places = (tok_index - 1) * row_count + jnp.arange(2 * row_count, dtype=jnp.int32)
    allowed_self = (
        (key_places[None, :] <= places[:, None])
        & (key_places[None, :] >= 0)
        & (key_places[None, :] < length)
    )
    self_out, self_total = attend_forward(query, self_keys, self_values, allowed_self)
    self_mixed = self_out.astype(bf16)
    after_one = inputs + product(self_mixed, output_weight) + output_bias
    normed_two, unit_two, inverse_two = layer_norm(after_one, cross_gain, cross_shift)
    hidden_two = normed_two.astype(bf16)
    probe = ((product(hidden_two, probe_weight) + probe_bias) * head_scale).astype(bf16)
    page_rows = lax.dynamic_slice_in_dim(gathered, page_start, PAGE_SLOTS, 0)
    page_keys = product(page_rows, source_key).astype(bf16)
    page_values = (product(page_rows, source_value) + source_bias).astype(bf16)
    slot_index = jnp.arange(PAGE_SLOTS, dtype=jnp.int32)
    allowed_cross = jnp.broadcast_to((slot_index < filled)[None, :], (row_count, PAGE_SLOTS))
    cross_out, cross_total = attend_forward(probe, page_keys, page_values, allowed_cross)
    cross_mixed = cross_out.astype(bf16)
    after_two = after_one + product(cross_mixed, merge_weight) + merge_bias
    normed_three, unit_three, inverse_three = layer_norm(after_two, feed_gain, feed_shift)
    hidden_three = normed_three.astype(bf16)
    pre_act = product(hidden_three, expand_weight) + expand_bias
    activated_full, gelu_pull = jax.vjp(exact_gelu, pre_act)
    activated = activated_full.astype(bf16)
    branch = product(activated, reduce_weight) + reduce_bias
    block_output = (valid_rows * (after_two + branch)).astype(bf16)
    grad_two = valid_rows * cotangent[0].astype(f32)
    grad_ffn = grad_two.astype(bf16)
    reduce_weight_grad = scatter_product(activated, grad_ffn, "patch")
    reduce_bias_part = jnp.sum(grad_ffn.astype(f32), axis=0)
    grad_pre = gelu_pull(product_nt(grad_ffn, reduce_weight))[0].astype(bf16)
    expand_weight_grad = scatter_product(hidden_three, grad_pre, "tok")
    expand_bias_part = jnp.sum(grad_pre.astype(f32), axis=0)
    norm_grad, feed_gain_part, feed_shift_part = norm_backward(
        product_nt(grad_pre, expand_weight), unit_three, inverse_three, feed_gain
    )
    grad_two = grad_two + norm_grad
    grad_merge = grad_two.astype(bf16)
    merge_weight_grad = scatter_product(cross_mixed, grad_merge, "patch")
    merge_bias_part = jnp.sum(grad_merge.astype(f32), axis=0)
    grad_cross_out = product_nt(grad_merge, merge_weight).astype(bf16)
    probe_raw, page_key_grad, page_value_grad = attend_backward(
        probe, page_keys, page_values, allowed_cross, cross_total, grad_cross_out
    )
    pair_grads = jnp.concatenate([page_key_grad, page_value_grad], axis=1).astype(bf16)
    source_grads = scatter_product(page_rows, pair_grads, "tok")
    source_bias_part = jnp.sum(page_value_grad, axis=0)
    source_pair = jnp.concatenate([source_key, source_value], axis=1)
    patch_total = patches.shape[0] * lax.axis_size(("tok", "patch"))

    def patch_half(start, size, added):
        part = product_nt(pair_grads, lax.dynamic_slice_in_dim(source_pair, start, size, 0))
        placed = lax.dynamic_update_slice_in_dim(
            jnp.zeros((patch_total, size), bf16), part.astype(bf16), page_start, 0
        ).astype(f32)
        return placed if added is None else placed + added.astype(f32)

    patches_grad = scatter_columns(patch_half, model_width, "patch")
    probe_grad = probe_raw.astype(bf16)
    probe_weight_grad = scatter_product(hidden_two, probe_grad, "patch") * head_scale
    probe_bias_part = jnp.sum(probe_grad.astype(f32), axis=0) * head_scale
    norm_grad, cross_gain_part, cross_shift_part = norm_backward(
        product_nt(probe_grad, probe_weight) * head_scale, unit_two, inverse_two, cross_gain
    )
    grad_one = grad_two + norm_grad
    grad_self = grad_one.astype(bf16)
    output_weight_grad = scatter_product(self_mixed, grad_self, "patch")
    output_bias_part = jnp.sum(grad_self.astype(f32), axis=0)
    grad_self_out = product_nt(grad_self, output_weight).astype(bf16)
    query_raw, keys_raw, values_raw = attend_backward(
        query, self_keys, self_values, allowed_self, self_total, grad_self_out
    )
    key_grad = keys_raw.astype(bf16)
    value_grad = values_raw.astype(bf16)
    query_grad = (query_raw * head_scale).astype(bf16)
    lead_upstream = product_nt(key_grad[:row_count], key_weight) + product_nt(
        value_grad[:row_count], value_weight
    )
    returned = passed_along(lead_upstream.astype(bf16), "tok", -1).astype(f32)
    own_upstream = (
        product_nt(query_grad, query_weight)
        + product_nt(key_grad[row_count:], key_weight)
        + product_nt(value_grad[row_count:], value_weight)
    )
    both_hidden = jnp.concatenate([hidden_lead, hidden_one], axis=0)
    pair_weight_grad = scatter_product(
        both_hidden, jnp.concatenate([key_grad, value_grad], axis=1), "tok"
    )
    query_weight_grad = scatter_product(hidden_one, query_grad, "patch")
    query_bias_part = jnp.sum(query_grad.astype(f32), axis=0)
    value_bias_part = jnp.sum(value_grad.astype(f32), axis=0)
    self_gain_part = jnp.sum(own_upstream * unit_one, axis=0) + jnp.sum(
        lead_upstream * unit_lead, axis=0
    )
    self_shift_part = jnp.sum(own_upstream, axis=0) + jnp.sum(lead_upstream, axis=0)
    norm_grad, _, _ = norm_backward(own_upstream + returned, unit_one, inverse_one, self_gain)
    tokens_grad = grad_one + norm_grad
    sums = scatter_vectors(
        [
            self_gain_part,
            self_shift_part,
            query_bias_part,
            value_bias_part,
            output_bias_part,
            cross_gain_part,
            cross_shift_part,
            probe_bias_part,
            source_bias_part,
            merge_bias_part,
            feed_gain_part,
            feed_shift_part,
            expand_bias_part,
            reduce_bias_part,
        ]
    )
    return (
        block_output[None],
        tokens_grad[None],
        patches_grad,
        sums[0],
        sums[1],
        query_weight_grad,
        sums[2],
        pair_weight_grad[:, :model_width],
        pair_weight_grad[:, model_width:],
        sums[3],
        output_weight_grad,
        sums[4],
        sums[5],
        sums[6],
        probe_weight_grad,
        sums[7],
        source_grads[:, :model_width],
        source_grads[:, model_width:],
        sums[8],
        merge_weight_grad,
        sums[9],
        sums[10],
        sums[11],
        expand_weight_grad,
        sums[12],
        reduce_weight_grad,
        sums[13],
    )


def solution(mesh):
    placed = (
        P("patch", "tok", None),
        P(("tok", "patch"), None),
        P("patch", "tok", None),
        P(),
        P(),
        P(),
        P(),
        P(),
        P(),
        P(),
        P(),
        P(),
        P(),
        P(),
        P(),
        P(),
        P(),
        P(),
        P(),
        P(),
        P(),
        P(),
        P(),
        P(),
        P(),
        P(),
        P(),
        P(),
        P(),
        P(),
    )
    return jax.shard_map(
        local,
        mesh=mesh,
        in_specs=placed,
        out_specs=(
            P("patch", "tok", None),
            P("patch", "tok", None),
            P(("tok", "patch"), None),
            P(("tok", "patch")),
            P(("tok", "patch")),
            P(("tok", "patch"), None),
            P(("tok", "patch")),
            P(("tok", "patch"), None),
            P(("tok", "patch"), None),
            P(("tok", "patch")),
            P(("tok", "patch"), None),
            P(("tok", "patch")),
            P(("tok", "patch")),
            P(("tok", "patch")),
            P(("tok", "patch"), None),
            P(("tok", "patch")),
            P(("tok", "patch"), None),
            P(("tok", "patch"), None),
            P(("tok", "patch")),
            P(("tok", "patch"), None),
            P(("tok", "patch")),
            P(("tok", "patch")),
            P(("tok", "patch")),
            P(("tok", "patch"), None),
            P(("tok", "patch")),
            P(("tok", "patch"), None),
            P(("tok", "patch")),
        ),
        check_vma=False,
    )
```

```python
import jax
import jax.numpy as jnp
from jax import lax
from jax.experimental import pallas as pl
from jax.experimental.pallas import tpu as pltpu
from jax.sharding import PartitionSpec as P

HDIM = 64
PAIR = 2 * HDIM
PAGE_SLOTS = 512
NEG_FILL = -1e30
EPS_NORM = 1e-05
LANES = 128
HIGH = lax.Precision.HIGHEST
MIB = 1 << 20
bf16, f32 = jnp.bfloat16, jnp.float32
Shape = jax.ShapeDtypeStruct


def nn(left, right):
    return lax.dot_general(
        left, right, (((1,), (0,)), ((), ())), preferred_element_type=f32
    )


def nt(left, right, precision=None):
    return lax.dot_general(
        left, right, (((1,), (1,)), ((), ())), precision=precision, preferred_element_type=f32
    )


def tn(left, right):
    return lax.dot_general(
        left, right, (((0,), (0,)), ((), ())), preferred_element_type=f32
    )


def column_sums(values):
    return jnp.sum(values.astype(f32), axis=0, keepdims=True)


def norm_unit(values):
    average = jnp.mean(values, axis=-1, keepdims=True)
    centred = values - average
    spread = jnp.mean(centred * centred, axis=-1, keepdims=True)
    inverse = lax.rsqrt(spread + EPS_NORM)
    return centred * inverse, inverse


def norm_pull(upstream, unit, inverse, gain):
    scaled = upstream * gain
    centred = scaled - jnp.mean(scaled, axis=-1, keepdims=True)
    centred = centred - unit * jnp.mean(scaled * unit, axis=-1, keepdims=True)
    return centred * inverse


def gelu_pair(values):
    share = 0.5 * (1.0 + lax.erf(values * (2.0**-0.5)))
    slope = share + values * (jnp.exp(-0.5 * values * values) * 0.3989422804014327)
    return values * share, slope


def by_core(core, value, rows):
    count, width = value.shape
    split = value.reshape(count // (2 * rows), 2, rows, width)
    first, second = split[:, 0], split[:, 1]
    pair = (jnp.where(core == 0, second, first), jnp.where(core == 0, first, second))
    return [one.reshape(count // 2, width).astype(bf16) for one in pair]


def head_lanes(head):
    lane = lax.broadcasted_iota(jnp.int32, (1, PAIR), 1)
    return (lane >= head * HDIM) & (lane < (head + 1) * HDIM)


def only(value, head):
    return jnp.where(head_lanes(head), value, jnp.zeros_like(value))


def settings(limit=48):
    return pltpu.CompilerParams(
        dimension_semantics=("arbitrary",), vmem_limit_bytes=limit * MIB
    )


def forward_rows(q_ref, parts, out_ref, total_ref, start, count, pair):
    outs, totals = [], []
    for head in range(2):
        query = only(q_ref[pl.ds(start, count), :], head)
        scores = []
        for keys, _, first, rows, mask in parts:
            score = nt(query, keys[pl.ds(first, rows), :])
            if isinstance(mask, str):
                row = lax.broadcasted_iota(jnp.int32, score.shape, 0)
                column = lax.broadcasted_iota(jnp.int32, score.shape, 1)
                score = jnp.where(column <= row, score, NEG_FILL)
            elif mask is not None:
                score = score + mask
            scores.append(score)
        row_max = scores[0].max(-1, keepdims=True)
        for score in scores[1:]:
            row_max = jnp.maximum(row_max, score.max(-1, keepdims=True))
        row_total, out = 0.0, 0.0
        for score, (_, values, first, rows, _) in zip(scores, parts):
            exponent = jnp.exp(score - row_max)
            row_total = row_total + exponent.sum(-1, keepdims=True)
            out = out + nn(exponent.astype(bf16), values[pl.ds(first, rows), :])
        outs.append(out / row_total)
        totals.append(row_max + jnp.log(row_total))
    out_ref[pl.ds(start, count), :] = jnp.where(head_lanes(0), outs[0], outs[1]).astype(bf16)
    lane = lax.broadcasted_iota(jnp.int32, (1, LANES), 1)
    held = total_ref[pl.ds(start, count), :]
    held = jnp.where(lane == 2 * pair, totals[0], held)
    total_ref[pl.ds(start, count), :] = jnp.where(lane == 2 * pair + 1, totals[1], held)


def self_forward(query, lead_keys, lead_values, own_keys, own_values, trailing, count=256):
    rows, width = query.shape

    def body(flag, q_ref, lk, lv, ok, ov, out_ref, total_ref):
        pair = pl.program_id(0)

        @pl.when(pair == 0)
        def _():
            total_ref[...] = jnp.zeros_like(total_ref)

        def go(with_lead):
            for start in range(0, rows, count):
                parts = [(lk, lv, 0, rows, None)] if with_lead else []
                if start:
                    parts.append((ok, ov, 0, start, None))
                parts.append((ok, ov, start, count, "causal"))
                forward_rows(q_ref, parts, out_ref, total_ref, start, count, pair)

        @pl.when(flag[0] == 1)
        def _():
            go(True)

        @pl.when(flag[0] == 0)
        def _():
            go(False)

    block = pl.BlockSpec((rows, PAIR), lambda p, flag: (0, p))
    return pl.pallas_call(
        body,
        out_shape=(Shape((rows, width), bf16), Shape((rows, LANES), f32)),
        grid_spec=pltpu.PrefetchScalarGridSpec(
            num_scalar_prefetch=1,
            grid=(width // PAIR,),
            in_specs=[block] * 5,
            out_specs=[block, pl.BlockSpec((rows, LANES), lambda p, flag: (0, 0))],
        ),
        compiler_params=settings(),
        name="self_forward",
    )(trailing, query, lead_keys, lead_values, own_keys, own_values)


def cross_forward(query, keys, values, filled, count=256):
    rows, width = query.shape
    slots = keys.shape[0]

    def body(filled_ref, q_ref, k_ref, v_ref, out_ref, total_ref):
        pair = pl.program_id(0)

        @pl.when(pair == 0)
        def _():
            total_ref[...] = jnp.zeros_like(total_ref)

        slot = lax.broadcasted_iota(jnp.int32, (1, slots), 1)
        bias = jnp.where(slot < filled_ref[0], 0.0, NEG_FILL)
        for start in range(0, rows, count):
            parts = [(k_ref, v_ref, 0, slots, bias)]
            forward_rows(q_ref, parts, out_ref, total_ref, start, count, pair)

    block = pl.BlockSpec((rows, PAIR), lambda p, f: (0, p))
    page = pl.BlockSpec((slots, PAIR), lambda p, f: (0, p))
    return pl.pallas_call(
        body,
        out_shape=(Shape((rows, width), bf16), Shape((rows, LANES), f32)),
        grid_spec=pltpu.PrefetchScalarGridSpec(
            num_scalar_prefetch=1,
            grid=(width // PAIR,),
            in_specs=[block, page, page],
            out_specs=[block, pl.BlockSpec((rows, LANES), lambda p, f: (0, 0))],
        ),
        compiler_params=settings(),
        name="cross_forward",
    )(filled, query, keys, values)


def row_stats(total_ref, out_ref, grad_ref, pair):
    row = lax.broadcasted_iota(jnp.int32, (8, LANES), 0)
    lane = lax.broadcasted_iota(jnp.int32, (8, LANES), 1)
    choose = ((lane == 2 * pair + row) & (row < 2)).astype(f32)
    totals = nt(choose, total_ref[...], HIGH)
    inner = out_ref[...].astype(f32) * grad_ref[...].astype(f32)
    share = ((lane // HDIM == row) & (row < 2)).astype(f32)
    return totals, nt(share, inner, HIGH)


def backward_keys(q_ref, g_ref, keys, values, first, rows, start, stats, mask, acc, fresh):
    totals, inner = stats
    count = q_ref.shape[0] - start
    key_rows, value_rows = keys[pl.ds(first, rows), :], values[pl.ds(first, rows), :]
    key_grad = jnp.zeros((rows, PAIR), f32)
    value_grad = jnp.zeros((rows, PAIR), f32)
    for head in range(2):
        query = only(q_ref[pl.ds(start, count), :], head)
        upstream = only(g_ref[pl.ds(start, count), :], head)
        score = nt(key_rows, query)
        if isinstance(mask, str):
            row = lax.broadcasted_iota(jnp.int32, score.shape, 0)
            column = lax.broadcasted_iota(jnp.int32, score.shape, 1)
            score = jnp.where(row <= column, score, NEG_FILL)
        elif mask is not None:
            score = score + mask
        soft = jnp.exp(score - totals[head : head + 1, start:])
        grad_soft = nt(value_rows, upstream)
        grad_score = (soft * (grad_soft - inner[head : head + 1, start:])).astype(bf16)
        value_grad = value_grad + nn(soft.astype(bf16), upstream)
        key_grad = key_grad + nn(grad_score, query)
        part = tn(grad_score, only(key_rows, head))
        if fresh and head == 0:
            acc[pl.ds(start, count), :] = part
        else:
            acc[pl.ds(start, count), :] += part
    return key_grad.astype(bf16), value_grad.astype(bf16)


def lead_backward(query, keys, values, out, total, grad, trailing, first, pairs, block=256):
    rows = query.shape[0]

    def body(flag, q_ref, k_ref, v_ref, out_ref, total_ref, g_ref, dq_ref, dk_ref, dv_ref):
        @pl.when(flag[0] == 1)
        def _():
            stats = row_stats(total_ref, out_ref, g_ref, pl.program_id(0) + first)
            for at in range(0, rows, block):
                dk, dv = backward_keys(
                    q_ref, g_ref, k_ref, v_ref, at, block, 0, stats, None, dq_ref, at == 0
                )
                dk_ref[pl.ds(at, block), :] = dk
                dv_ref[pl.ds(at, block), :] = dv

        @pl.when(flag[0] == 0)
        def _():
            for ref in (dq_ref, dk_ref, dv_ref):
                ref[...] = jnp.zeros_like(ref)

    source = pl.BlockSpec((rows, PAIR), lambda p, flag: (0, p + first))
    target = pl.BlockSpec((rows, PAIR), lambda p, flag: (0, p))
    fixed = pl.BlockSpec((rows, LANES), lambda p, flag: (0, 0))
    return pl.pallas_call(
        body,
        out_shape=[Shape((rows, pairs * PAIR), kind) for kind in (f32, bf16, bf16)],
        grid_spec=pltpu.PrefetchScalarGridSpec(
            num_scalar_prefetch=1,
            grid=(pairs,),
            in_specs=[source] * 4 + [fixed, source],
            out_specs=[target] * 3,
        ),
        compiler_params=settings(),
        name="lead_backward",
    )(trailing, query, keys, values, out, total, grad)


def own_backward(query, keys, values, out, total, grad, begun, first, pairs, block=256):
    rows = query.shape[0]

    def body(q_ref, k_ref, v_ref, out_ref, total_ref, g_ref, begun_ref, dq_ref, dk_ref, dv_ref, acc):
        acc[...] = begun_ref[...]
        stats = row_stats(total_ref, out_ref, g_ref, pl.program_id(0) + first)
        for at in range(0, rows, block):
            dk, dv = backward_keys(
                q_ref, g_ref, k_ref, v_ref, at, block, at, stats, "causal", acc, False
            )
            dk_ref[pl.ds(at, block), :] = dk
            dv_ref[pl.ds(at, block), :] = dv
        dq_ref[...] = (acc[...] * (HDIM**-0.5)).astype(bf16)

    source = pl.BlockSpec((rows, PAIR), lambda p: (0, p + first))
    target = pl.BlockSpec((rows, PAIR), lambda p: (0, p))
    fixed = pl.BlockSpec((rows, LANES), lambda p: (0, 0))
    return pl.pallas_call(
        body,
        out_shape=[Shape((rows, pairs * PAIR), bf16)] * 3,
        grid=(pairs,),
        in_specs=[source] * 4 + [fixed, source, target],
        out_specs=[target] * 3,
        scratch_shapes=[pltpu.VMEM((rows, PAIR), f32)],
        compiler_params=settings(),
        name="own_backward",
    )(query, keys, values, out, total, grad, begun)


def cross_backward(query, keys, values, out, total, grad, filled, first, pairs, block=256):
    rows, slots = query.shape[0], keys.shape[0]

    def body(
        filled_ref, q_ref, k_ref, v_ref, out_ref, total_ref, g_ref, dq_ref, dk_ref, dv_ref, acc
    ):
        stats = row_stats(total_ref, out_ref, g_ref, pl.program_id(0) + first)
        for at in range(0, slots, block):
            slot = lax.broadcasted_iota(jnp.int32, (block, 1), 0) + at
            bias = jnp.where(slot < filled_ref[0], 0.0, NEG_FILL)
            dk, dv = backward_keys(
                q_ref, g_ref, k_ref, v_ref, at, block, 0, stats, bias, acc, at == 0
            )
            dk_ref[pl.ds(at, block), :] = dk
            dv_ref[pl.ds(at, block), :] = dv
        dq_ref[...] = (acc[...] * (HDIM**-0.5)).astype(bf16)

    source = pl.BlockSpec((rows, PAIR), lambda p, f: (0, p + first))
    page = pl.BlockSpec((slots, PAIR), lambda p, f: (0, p + first))
    target = pl.BlockSpec((rows, PAIR), lambda p, f: (0, p))
    page_target = pl.BlockSpec((slots, PAIR), lambda p, f: (0, p))
    fixed = pl.BlockSpec((rows, LANES), lambda p, f: (0, 0))
    return pl.pallas_call(
        body,
        out_shape=[Shape((rows, pairs * PAIR), bf16)] + [Shape((slots, pairs * PAIR), bf16)] * 2,
        grid_spec=pltpu.PrefetchScalarGridSpec(
            num_scalar_prefetch=1,
            grid=(pairs,),
            in_specs=[source, page, page, source, fixed, source],
            out_specs=[target, page_target, page_target],
            scratch_shapes=[pltpu.VMEM((rows, PAIR), f32)],
        ),
        compiler_params=settings(),
        name="cross_backward",
    )(filled, query, keys, values, out, total, grad)


def feed_forward(after_one, mixed, merge, cotangent, vectors, expand, bias, reduce, info, owners):
    rows, width = after_one.shape
    hidden = expand.shape[1]
    block, tall = 512, 384
    steps, half = hidden // block, width // 2
    starts = range(0, rows, tall)

    def body(
        info_ref, after_ref, mixed_ref, merge_ref, cot_ref, vec_ref, we_ref, be_ref, wr_ref,
        out_ref, two_ref, cross_ref, rs_ref, ro_ref, es_ref, eo_ref, ms_ref, mo_ref, eb_ref,
        sums_ref, after, h, h_flip, g, branch, up, act, gp,
    ):
        step = pl.program_id(0)
        core, place, length = info_ref[0], info_ref[1], info_ref[2]

        def valid(start):
            row = lax.broadcasted_iota(jnp.int32, (tall, 1), 0) + (start + place)
            return (row < length).astype(f32)

        @pl.when(step == 0)
        def _():
            total = jnp.zeros((1, width), f32)
            for start in starts:
                at = pl.ds(start, tall)
                x = after_ref[at, :] + nn(mixed_ref[at, :], merge_ref[...]) + vec_ref[0:1, :]
                after[at, :] = x
                unit, _ = norm_unit(x)
                low = (unit * vec_ref[1:2, :] + vec_ref[2:3, :]).astype(bf16)
                h[at, :] = low
                h_flip[:, at] = low.T
                grad = (valid(start) * cot_ref[at, :].astype(f32)).astype(bf16)
                g[at, :] = grad
                total = total + column_sums(grad)
                branch[at, :] = jnp.zeros((tall, width), f32)
                up[at, :] = jnp.zeros((tall, width), f32)
            sums_ref[0:1, :] = total

        we, wr = we_ref[...], wr_ref[...]
        for start in starts:
            at = pl.ds(start, tall)
            low, slope = gelu_pair(nn(h[at, :], we) + be_ref[...])
            low = low.astype(bf16)
            act[at, :] = low
            branch[at, :] += nn(low, wr)
            grad = (nt(g[at, :], wr) * slope).astype(bf16)
            gp[at, :] = grad
            up[at, :] += nt(grad, we)
        rs_ref[...], ro_ref[...] = by_core(core, tn(act[...], g[...]), hidden // owners)
        es_ref[...], eo_ref[...] = by_core(core, nn(h_flip[...], gp[...]), width // owners)
        eb_ref[...] = nn(jnp.ones((8, rows), bf16), gp[...])

        @pl.when(step == steps - 1)
        def _():
            gains = jnp.zeros((1, width), f32)
            shifts, merges = gains, gains
            for start in starts:
                at = pl.ds(start, tall)
                x, ok = after[at, :], valid(start)
                out_ref[at, :] = (ok * (x + branch[at, :] + vec_ref[3:4, :])).astype(bf16)
                unit, inverse = norm_unit(x)
                upstream = up[at, :]
                gains = gains + jnp.sum(upstream * unit, axis=0, keepdims=True)
                shifts = shifts + jnp.sum(upstream, axis=0, keepdims=True)
                pulled = norm_pull(upstream, unit, inverse, vec_ref[1:2, :])
                two = ok * cot_ref[at, :].astype(f32) + pulled
                two_ref[at, :] = two
                low = two.astype(bf16)
                g[at, :] = low
                merges = merges + column_sums(low)
                cross_ref[at, :] = nt(low, merge_ref[...]).astype(bf16)
            ms_ref[...], mo_ref[...] = by_core(core, tn(mixed_ref[...], g[...]), width // owners)
            sums_ref[1:2, :], sums_ref[2:3, :], sums_ref[3:4, :] = gains, shifts, merges

    def once(shape):
        return pl.BlockSpec(shape, lambda i, info: (0, 0), pipeline_mode=pl.Buffered(1))

    def fixed(shape):
        return pl.BlockSpec(shape, lambda i, info: (0, 0))

    by_row = pl.BlockSpec((block // 2, width), lambda i, info: (i, 0))
    by_column = pl.BlockSpec((half, block), lambda i, info: (0, i))
    full, low = (rows, width), (rows, width)
    return pl.pallas_call(
        body,
        out_shape=[
            Shape(full, bf16), Shape(full, f32), Shape(full, bf16),
            Shape((hidden // 2, width), bf16), Shape((hidden // 2, width), bf16),
            Shape((half, hidden), bf16), Shape((half, hidden), bf16),
            Shape((half, width), bf16), Shape((half, width), bf16),
            Shape((8, hidden), f32), Shape((8, width), f32),
        ],
        grid_spec=pltpu.PrefetchScalarGridSpec(
            num_scalar_prefetch=1,
            grid=(steps,),
            in_specs=[
                once(full), once(full), once((width, width)), once(full), once((8, width)),
                pl.BlockSpec((width, block), lambda i, info: (0, i)),
                pl.BlockSpec((1, block), lambda i, info: (0, i)),
                pl.BlockSpec((block, width), lambda i, info: (i, 0)),
            ],
            out_specs=[
                fixed(full), fixed(full), fixed(full), by_row, by_row, by_column, by_column,
                fixed((half, width)), fixed((half, width)),
                pl.BlockSpec((8, block), lambda i, info: (0, i)),
                fixed((8, width)),
            ],
            scratch_shapes=[
                pltpu.VMEM(full, f32), pltpu.VMEM(low, bf16), pltpu.VMEM((width, rows), bf16),
                pltpu.VMEM(low, bf16), pltpu.VMEM(full, f32), pltpu.VMEM(full, f32),
                pltpu.VMEM((rows, block), bf16), pltpu.VMEM((rows, block), bf16),
            ],
        ),
        compiler_params=settings(60),
        name="feed_forward",
    )(info, after_one, mixed, merge, cotangent, vectors, expand, bias, reduce)


def streamed(name, body, info, inputs, outs, scratch=()):
    n, m = len(inputs), len(outs)

    def kernel(info_ref, *refs):
        ins, dests = refs[:n], refs[n : n + m]
        held, made = refs[n + m : 2 * n + m], refs[2 * n + m : 2 * n + 2 * m]
        in_sem, out_sem = refs[2 * n + 2 * m : 2 * n + 2 * m + 2]
        rest = refs[2 * n + 2 * m + 2 :]
        loads = [pltpu.make_async_copy(ins[i], held[i], in_sem.at[i]) for i in range(n)]
        for load in loads:
            load.start()
        waited, stores = set(), {}

        def need(i):
            if i not in waited:
                loads[i].wait()
                waited.add(i)
            return held[i]

        def give(i, send=False):
            if send:
                stores[i] = pltpu.make_async_copy(made[i], dests[i], out_sem.at[i])
                stores[i].start()
            return made[i]

        body(info_ref, need, give, *rest)
        for i in range(m):
            stores[i].wait()

    anywhere = pl.BlockSpec(memory_space=pl.ANY)
    return pl.pallas_call(
        kernel,
        out_shape=[Shape(shape, kind) for shape, kind in outs],
        grid_spec=pltpu.PrefetchScalarGridSpec(
            num_scalar_prefetch=1,
            grid=(1,),
            in_specs=[anywhere] * n,
            out_specs=[anywhere] * m,
            scratch_shapes=[pltpu.VMEM(value.shape, value.dtype) for value in inputs]
            + [pltpu.VMEM(shape, kind) for shape, kind in outs]
            + [pltpu.SemaphoreType.DMA((n,)), pltpu.SemaphoreType.DMA((m,))]
            + list(scratch),
        ),
        compiler_params=settings(60),
        name=name,
    )(info, *inputs)


def probe_backward(info, probe_low, probe_high, probe_weight, after_one, two, output_weight, mixed, vectors, owners):
    rows, width = after_one.shape
    half, tall = width // 2, 256

    def body(info_ref, need, give, hidden, low_grad):
        core = info_ref[0]
        left, right = need(0), need(1)
        weight = need(2)
        vec = need(7)
        x_ref, two_ref = need(3), need(4)
        gains = jnp.zeros((1, width), f32)
        shifts, outs = gains, gains
        for start in range(0, rows, tall):
            at = pl.ds(start, tall)
            up = nt(left[at, :], weight[:, :half]) + nt(right[at, :], weight[:, half:])
            unit, inverse = norm_unit(x_ref[at, :])
            hidden[at, :] = (unit * vec[0:1, :] + vec[1:2, :]).astype(bf16)
            gains = gains + jnp.sum(up * unit, axis=0, keepdims=True)
            shifts = shifts + jnp.sum(up, axis=0, keepdims=True)
            one = two_ref[at, :] + norm_pull(up, unit, inverse, vec[0:1, :])
            give(0)[at, :] = one
            low = one.astype(bf16)
            low_grad[at, :] = low
            outs = outs + column_sums(low)
            if start == 0:
                need(5)
            give(1)[at, :] = nt(low, need(5)[...]).astype(bf16)
        give(0, True)
        give(1, True)
        sums = give(4)
        sums[...] = jnp.zeros_like(sums)
        sums[0:1, :], sums[1:2, :], sums[2:3, :] = gains, shifts, outs
        sums[3:4, :half] = column_sums(left[...])
        sums[3:4, half:] = column_sums(right[...])
        give(4, True)
        mixed_ref = need(6)
        columns = (
            (0, half, hidden, left[...]),
            (half, width, hidden, right[...]),
            (width, 2 * width, mixed_ref, low_grad[...]),
        )
        for begin, end, source, grads in columns:
            pair = by_core(core, tn(source[...], grads), width // owners)
            give(2)[:, begin:end], give(3)[:, begin:end] = pair
        give(2, True)
        give(3, True)

    return streamed(
        "probe_backward",
        body,
        info,
        [probe_low, probe_high, probe_weight, after_one, two, output_weight, mixed, vectors],
        [
            ((rows, width), f32), ((rows, width), bf16),
            ((half, 2 * width), bf16), ((half, 2 * width), bf16), ((8, width), f32),
        ],
        [pltpu.VMEM((rows, width), bf16), pltpu.VMEM((rows, width), bf16)],
    )


def page_backward(
    info, key_low, key_high, value_low, value_high, page_rows, key_weight, value_weight, owners,
    patch_total,
):
    slots, width = page_rows.shape
    half = width // 2
    deep = patch_total // 2

    def body(info_ref, need, give):
        core, page = info_ref[0], info_ref[3]
        kl, kh, vl, vh = need(0)[...], need(1)[...], need(2)[...], need(3)[...]
        rows_ref = need(4)
        for i, grads in enumerate((kl, kh, vl, vh)):
            pair = by_core(core, tn(rows_ref[...], grads), width // owners)
            at = pl.ds(i * half, half)
            give(0)[:, at], give(1)[:, at] = pair
        give(0, True)
        give(1, True)
        wk, wv = need(5), need(6)
        total = nt(kl, wk[:, :half]) + nt(kh, wk[:, half:])
        total = total + nt(vl, wv[:, :half]) + nt(vh, wv[:, half:])
        pair = by_core(core, total, patch_total // owners)
        at = pl.ds(pl.multiple_of(page * (slots // 2), slots // 2), slots // 2)
        for which in range(2):
            give(2 + which)[...] = jnp.zeros((deep, width), bf16)
            give(2 + which)[at, :] = pair[which]
            give(2 + which, True)
        sums = give(4)
        sums[...] = jnp.zeros_like(sums)
        sums[0:1, :half] = column_sums(vl)
        sums[0:1, half:] = column_sums(vh)
        give(4, True)

    return streamed(
        "page_backward",
        body,
        info,
        [key_low, key_high, value_low, value_high, page_rows, key_weight, value_weight],
        [
            ((half, 2 * width), bf16), ((half, 2 * width), bf16),
            ((deep, width), bf16), ((deep, width), bf16), ((8, width), f32),
        ],
    )


def lead_upstream(info, keys, values, key_weight, value_weight, lead_tokens, vectors):
    rows, width = lead_tokens.shape
    half, tall = width // 2, 256

    def body(info_ref, need, give, hidden):
        kl, kh, vl, vh = need(0), need(1), need(2), need(3)
        wk, wv = need(4), need(5)
        x_ref, vec = need(6), need(7)
        gains = jnp.zeros((1, width), f32)
        shifts = gains
        for start in range(0, rows, tall):
            at = pl.ds(start, tall)
            up = nt(kl[at, :], wk[:, :half]) + nt(kh[at, :], wk[:, half:])
            up = up + nt(vl[at, :], wv[:, :half]) + nt(vh[at, :], wv[:, half:])
            give(0)[at, :] = up.astype(bf16)
            unit, _ = norm_unit(x_ref[at, :].astype(f32))
            hidden[at, :] = (unit * vec[0:1, :] + vec[1:2, :]).astype(bf16)
            gains = gains + jnp.sum(up * unit, axis=0, keepdims=True)
            shifts = shifts + jnp.sum(up, axis=0, keepdims=True)
        give(0, True)
        sums = give(2)
        sums[...] = jnp.zeros_like(sums)
        sums[0:1, :], sums[1:2, :] = gains, shifts
        sums[2:3, :half], sums[2:3, half:] = column_sums(vl[...]), column_sums(vh[...])
        give(2, True)
        for i, ref in enumerate((kl, kh, vl, vh)):
            give(1)[:, i * half : (i + 1) * half] = tn(hidden[...], ref[...]).astype(bf16)
        give(1, True)

    return streamed(
        "lead_upstream",
        body,
        info,
        [*keys, *values, key_weight, value_weight, lead_tokens, vectors],
        [((rows, width), bf16), ((width, 2 * width), bf16), ((8, width), f32)],
        [pltpu.VMEM((rows, width), bf16)],
    )


def projection_grads(info, hidden, query_grad, key_grad, value_grad, lead_part, high, owners):
    rows, width = hidden.shape
    half = width // 2
    column = half if high else 0

    def body(info_ref, need, give):
        core = info_ref[0]
        h = need(0)
        for i in range(3):
            total = tn(h[...], need(1 + i)[...])
            if i:
                base = (i - 1) * width + column
                total = total + need(4)[:, base : base + half].astype(f32)
            at = pl.ds(i * half, half)
            give(0)[:, at], give(1)[:, at] = by_core(core, total, width // owners)
        give(0, True)
        give(1, True)

    return streamed(
        "projection_grads",
        body,
        info,
        [hidden, query_grad, key_grad, value_grad, lead_part],
        [((half, 3 * half), bf16), ((half, 3 * half), bf16)],
    )


def first_norm_backward(info, queries, keys, values, weights, tokens, one, returned, vectors):
    rows, width = tokens.shape
    half, tall = width // 2, 256

    def body(info_ref, need, give):
        grads = [need(i) for i in range(6)]
        wq, wk, wv = need(6), need(7), need(8)
        x_ref, vec = need(9), need(10)
        one_ref, back_ref = need(11), need(12)
        gains = jnp.zeros((1, width), f32)
        shifts = gains
        for start in range(0, rows, tall):
            at = pl.ds(start, tall)
            up = 0.0
            for i, weight in enumerate((wq, wk, wv)):
                up = up + nt(grads[2 * i][at, :], weight[:, :half])
                up = up + nt(grads[2 * i + 1][at, :], weight[:, half:])
            unit, inverse = norm_unit(x_ref[at, :].astype(f32))
            gains = gains + jnp.sum(up * unit, axis=0, keepdims=True)
            shifts = shifts + jnp.sum(up, axis=0, keepdims=True)
            up = up + back_ref[at, :].astype(f32)
            give(0)[at, :] = one_ref[at, :] + norm_pull(up, unit, inverse, vec[0:1, :])
        give(0, True)
        sums = give(1)
        sums[...] = jnp.zeros_like(sums)
        sums[0:1, :], sums[1:2, :] = gains, shifts
        sums[2:3, :half], sums[2:3, half:] = column_sums(grads[0][...]), column_sums(grads[1][...])
        sums[3:4, :half], sums[3:4, half:] = column_sums(grads[4][...]), column_sums(grads[5][...])
        give(1, True)

    return streamed(
        "first_norm_backward",
        body,
        info,
        [*queries, *keys, *values, *weights, tokens, vectors, one, returned],
        [((rows, width), f32), ((8, width), f32)],
    )


def digit_axes():
    patch_bits = lax.axis_size("patch").bit_length() - 1
    return [("tok", 0)] + [("patch", bit) for bit in reversed(range(patch_bits))]


def my_digit(axis, bit):
    return (lax.axis_index(axis) >> bit) & 1


def tied(*values):
    return lax.optimization_barrier(values)


FIRST_DIGIT = 4


class Sum:
    def __init__(self, sent, kept, tok_first):
        every = digit_axes()
        self.free = every[:-1]
        bits = every[-2:0:-1]
        loose, last = bits[: max(len(bits) - 2, 0)], bits[max(len(bits) - 2, 0) :]
        singles = [every[:1]] + [[one] for one in loose]
        if not tok_first:
            singles = singles[1:] + singles[:1]
        self.stages = singles + [last]
        self.at = 0
        self.terms = [(self.chunks(kept), self.free)]
        self.leaving = [self.chunks(sent)]
        self.hops = [[("patch", 0)]]
        self.mine = None
        self.result = None

    def chunks(self, value):
        count = 1 << len(self.free)
        size = 1
        for n in value.shape[:-1]:
            size *= n
        return value.reshape(count, size // count, value.shape[-1])

    def send(self):
        self.arrived = [hop(value, steps) for value, steps in zip(self.leaving, self.hops)]

    def absorb(self, arrived):
        if self.mine is not None:
            self.result = sum((one[0].astype(f32) for one in arrived), self.mine[0])
            self.leaving = None
            return []
        self.terms += [(self.chunks(one), self.free) for one in arrived]
        digits = self.stages[self.at]
        self.at += 1
        self.free = [one for one in self.free if one not in digits]
        self.hops, jobs = [], []
        last = self.at == len(self.stages)
        for flips in range(0 if last else 1, 1 << len(digits)):
            flipped = [one for i, one in enumerate(digits) if flips >> i & 1]
            choices = []
            for chunk in range(1 << len(self.free)):
                bits = {
                    one: chunk >> (len(self.free) - 1 - i) & 1 for i, one in enumerate(self.free)
                }
                choices.append((bits, flipped))
            jobs.append((self.terms, choices, bf16 if flips else f32))
            if flips:
                self.hops.append(flipped)
        return jobs

    def take(self, made):
        if self.at == len(self.stages):
            self.mine = made[0]
            made = made[1:]
        self.leaving = list(made)


def hop(value, steps):
    axis = steps[0][0]
    flip = sum(1 << bit for _, bit in steps)
    return lax.ppermute(value, axis, [(i, i ^ flip) for i in range(lax.axis_size(axis))])


def added_up(info, jobs):
    digits = digit_axes()
    arrays, known = [], {}
    for terms, _, _ in jobs:
        for value, _ in terms:
            if id(value) not in known:
                known[id(value)] = len(arrays)
                arrays.append(value)
    loads = sum(len(terms) * len(choices) for terms, choices, _ in jobs)

    def body(info_ref, *refs):
        n, m = len(arrays), len(jobs)
        ins, dests = refs[:n], refs[n : n + m]
        held, made = refs[n + m : n + 2 * m], refs[n + 2 * m : n + 3 * m]
        in_sem, out_sem = refs[n + 3 * m], refs[n + 3 * m + 1]
        mine = {one: info_ref[FIRST_DIGIT + i] for i, one in enumerate(digits)}
        copies, count = [], 0
        for job, (terms, choices, _) in enumerate(jobs):
            for t, (value, free) in enumerate(terms):
                for c, (bits, flipped) in enumerate(choices):
                    index = 0
                    for one in free:
                        digit = bits[one] if one in bits else mine[one]
                        digit = 1 - digit if one in flipped else digit
                        index = 2 * index + digit
                    copy = pltpu.make_async_copy(
                        ins[known[id(value)]].at[index], held[job].at[t, c], in_sem.at[count]
                    )
                    copy.start()
                    copies.append((job, copy))
                    count += 1
        stores = []
        for job, (terms, choices, kind) in enumerate(jobs):
            for which, copy in copies:
                if which == job:
                    copy.wait()
            rows = held[job].shape[2]
            slab = min(rows, 16)
            per = rows // slab

            def step(i, _, job=job, terms=terms, kind=kind, slab=slab, per=per):
                chunk, at = i // per, pl.ds(pl.multiple_of(i % per * slab, slab), slab)
                total = held[job][0, chunk, at, :].astype(f32)
                for t in range(1, len(terms)):
                    total = total + held[job][t, chunk, at, :].astype(f32)
                made[job][chunk, at, :] = total.astype(kind)
                return 0

            lax.fori_loop(0, len(choices) * per, step, 0)
            stores.append(pltpu.make_async_copy(made[job], dests[job], out_sem.at[job]))
            stores[-1].start()
        for store in stores:
            store.wait()

    anywhere = pl.BlockSpec(memory_space=pl.ANY)
    shapes = [((len(choices),) + terms[0][0].shape[1:], kind) for terms, choices, kind in jobs]
    held = [
        pltpu.VMEM((len(terms), len(choices)) + terms[0][0].shape[1:], bf16)
        for terms, choices, _ in jobs
    ]
    return pl.pallas_call(
        body,
        out_shape=[Shape(shape, kind) for shape, kind in shapes],
        grid_spec=pltpu.PrefetchScalarGridSpec(
            num_scalar_prefetch=1,
            grid=(1,),
            in_specs=[anywhere] * len(arrays),
            out_specs=[anywhere] * len(jobs),
            scratch_shapes=held
            + [pltpu.VMEM(shape, kind) for shape, kind in shapes]
            + [pltpu.SemaphoreType.DMA((loads,)), pltpu.SemaphoreType.DMA((len(jobs),))],
        ),
        compiler_params=settings(60),
        name="added_up",
    )(info, *arrays)


def advance(info, chain, moving=(), fresh=()):
    moving = [one for one in moving if one.leaving is not None]
    chain, arrived = tied(chain, [one.arrived for one in moving])
    jobs, owners = [], []
    for one, values in zip(moving, arrived):
        new = one.absorb(values)
        owners.append((one, len(new)))
        jobs += new
    if jobs:
        made = added_up(info, jobs)
        for one, count in owners:
            if count:
                one.take(made[:count])
                made = made[count:]
    going = [one for one in moving + list(fresh) if one.leaving is not None]
    chain, leaving = tied(chain, [one.leaving for one in going])
    for one, values in zip(going, leaving):
        one.leaving = values
        one.send()
    return chain


def scatter_vectors(vectors):
    digits = digit_axes()
    owners = 1 << len(digits)
    widths = [vector.shape[0] // owners for vector in vectors]
    table = jnp.concatenate([vector.reshape(owners, -1) for vector in vectors], axis=1)
    table = jnp.pad(table, ((0, 0), (0, -table.shape[1] % 128)))
    mine = table.reshape((2,) * len(digits) + (table.shape[1],))
    left = list(digits)
    for step in digits[::-1]:
        place = left.index(step)
        left.pop(place)
        digit = my_digit(*step)
        keep = lax.dynamic_index_in_dim(mine, digit, place, keepdims=False)
        give = lax.dynamic_index_in_dim(mine, 1 - digit, place, keepdims=False)
        mine = keep + hop(give, [step])
    pieces, start = [], 0
    for width in widths:
        pieces.append(mine[start : start + width])
        start += width
    return pieces


def pick_entry(table, position):
    indices = jnp.arange(table.shape[0], dtype=jnp.int32)
    return jnp.sum(jnp.where(indices == position, table, 0))


def layer_norm(values, gain, shift):
    unit, _ = norm_unit(values)
    return (unit * gain + shift).astype(bf16)


def rows_of(*vectors):
    rows = jnp.stack(vectors, axis=0)
    return jnp.pad(rows, ((0, 8 - len(vectors)), (0, 0)))


def local(
    tokens,
    patches,
    cotangent,
    lengths,
    page_of,
    page_counts,
    self_gain,
    self_shift,
    query_weight,
    query_bias,
    key_weight,
    value_weight,
    value_bias,
    output_weight,
    output_bias,
    cross_gain,
    cross_shift,
    probe_weight,
    probe_bias,
    source_key,
    source_value,
    source_bias,
    merge_weight,
    merge_bias,
    feed_gain,
    feed_shift,
    expand_weight,
    expand_bias,
    reduce_weight,
    reduce_bias,
):
    head_scale = HDIM ** (-0.5)
    tok_index = lax.axis_index("tok").astype(jnp.int32)
    sequence = lax.axis_index("patch")
    core = my_digit("patch", 0).astype(jnp.int32)
    row_count, model_width = tokens.shape[1:]
    lead_tokens = lax.ppermute(tokens[0], "tok", [(0, 1)])
    gathered = lax.all_gather(patches, ("tok", "patch"), axis=0, tiled=True)
    inputs = tokens[0].astype(f32)
    page_index = pick_entry(page_of, sequence)
    filled = pick_entry(page_counts, page_index).reshape(1)
    trailing = tok_index.reshape(1)
    page_start = page_index * PAGE_SLOTS
    digits = [my_digit(*one).astype(jnp.int32) for one in digit_axes()]
    owners = 1 << len(digits)
    info = jnp.stack(
        [core, tok_index * row_count, pick_entry(lengths, sequence), page_index] + digits
    )
    self_vectors = rows_of(self_gain, self_shift)
    cross_vectors = rows_of(cross_gain, cross_shift)
    feed_vectors = rows_of(merge_bias, feed_gain, feed_shift, reduce_bias)

    hidden_one = layer_norm(inputs, self_gain, self_shift)
    query = ((nn(hidden_one, query_weight) + query_bias) * head_scale).astype(bf16)
    own_keys = nn(hidden_one, key_weight).astype(bf16)
    own_values = (nn(hidden_one, value_weight) + value_bias).astype(bf16)
    lead_tokens, query, own_keys, own_values = tied(lead_tokens, query, own_keys, own_values)
    hidden_lead = layer_norm(lead_tokens.astype(f32), self_gain, self_shift)
    lead_keys = nn(hidden_lead, key_weight).astype(bf16)
    lead_values = (nn(hidden_lead, value_weight) + value_bias).astype(bf16)
    self_mixed, self_total = self_forward(
        query, lead_keys, lead_values, own_keys, own_values, trailing
    )
    after_one = inputs + nn(self_mixed, output_weight) + output_bias
    hidden_two = layer_norm(after_one, cross_gain, cross_shift)
    probe = ((nn(hidden_two, probe_weight) + probe_bias) * head_scale).astype(bf16)
    page_rows = lax.dynamic_slice_in_dim(gathered, page_start, PAGE_SLOTS, 0)
    page_keys = nn(page_rows, source_key).astype(bf16)
    page_values = (nn(page_rows, source_value) + source_bias).astype(bf16)
    cross_mixed, cross_total = cross_forward(probe, page_keys, page_values, filled)

    fed = feed_forward(
        after_one, cross_mixed, merge_weight, cotangent[0], feed_vectors, expand_weight,
        expand_bias[None], reduce_weight, info, owners,
    )
    block_output, grad_two, grad_cross_out = fed[:3]
    feed_sums, expand_bias_sums = fed[10], fed[9]
    reduce_sum = Sum(fed[3], fed[4], False)
    expand_sum = Sum(fed[5], fed[6], True)
    merge_sum = Sum(fed[7], fed[8], False)

    half_pairs = model_width // PAIR // 2
    cross_args = (probe, page_keys, page_values, cross_mixed, cross_total)
    grad_cross_out = advance(info, grad_cross_out, [], [expand_sum, reduce_sum, merge_sum])
    low = cross_backward(*cross_args, grad_cross_out, filled, 0, half_pairs)
    low, grad_cross_out = advance(info, (low, grad_cross_out), [expand_sum, reduce_sum, merge_sum])
    high = cross_backward(*cross_args, grad_cross_out, filled, half_pairs, half_pairs)
    patch_total = patches.shape[0] * lax.axis_size(("tok", "patch"))
    paged = page_backward(
        info, low[1], high[1], low[2], high[2], page_rows, source_key, source_value, owners,
        patch_total,
    )
    source_sum = Sum(paged[0], paged[1], True)
    patch_sum = Sum(paged[2], paged[3], False)
    low, high = advance(info, (low, high), [], [source_sum, patch_sum])
    probed = probe_backward(
        info, low[0], high[0], probe_weight, after_one, grad_two, output_weight, self_mixed,
        cross_vectors, owners,
    )
    grad_one, grad_self_out, probe_sums = probed[0], probed[1], probed[4]
    middle_sum = Sum(probed[2], probed[3], False)
    self_args = (query, lead_keys, lead_values, self_mixed, self_total)
    own_args = (query, own_keys, own_values, self_mixed, self_total)
    first = [expand_sum, reduce_sum, merge_sum]
    second = [source_sum, patch_sum]
    grad_self_out = advance(info, grad_self_out, first + second, [middle_sum])
    second = second + [middle_sum]
    lead_low = lead_backward(*self_args, grad_self_out, trailing, 0, half_pairs)
    lead_low, grad_self_out = advance(info, (lead_low, grad_self_out), first + [middle_sum])
    lead_high = lead_backward(*self_args, grad_self_out, trailing, half_pairs, half_pairs)
    led = lead_upstream(
        info, (lead_low[1], lead_high[1]), (lead_low[2], lead_high[2]), key_weight,
        value_weight, lead_tokens, self_vectors,
    )
    led_grad, led_part, lead_sums = led
    led_grad, led_part, grad_self_out = advance(
        info, (led_grad, led_part, grad_self_out), second
    )
    returned = lax.ppermute(led_grad, "tok", [(1, 0)])
    own_low = own_backward(*own_args, grad_self_out, lead_low[0], 0, half_pairs)
    parts = projection_grads(info, hidden_one, *own_low, led_part, False, owners)
    low_sum = Sum(*parts, False)
    own_low, grad_self_out = advance(info, (own_low, grad_self_out), first + second, [low_sum])
    own_high = own_backward(*own_args, grad_self_out, lead_high[0], half_pairs, half_pairs)
    own_high, led_part = advance(info, (own_high, led_part), second + [low_sum])
    parts = projection_grads(info, hidden_one, *own_high, led_part, True, owners)
    high_sum = Sum(*parts, True)
    own_low, own_high = advance(info, (own_low, own_high), [], [high_sum])
    tokens_grad, first_sums = first_norm_backward(
        info, (own_low[0], own_high[0]), (own_low[1], own_high[1]), (own_low[2], own_high[2]),
        (query_weight, key_weight, value_weight), tokens[0], grad_one, returned, self_vectors,
    )
    rest = first + second + [low_sum, high_sum]
    first_sums = advance(info, first_sums, rest)
    sums = scatter_vectors(
        [
            first_sums[0] + lead_sums[0],
            first_sums[1] + lead_sums[1],
            first_sums[2],
            first_sums[3] + lead_sums[2],
            probe_sums[2],
            probe_sums[0],
            probe_sums[1],
            probe_sums[3],
            paged[4][0],
            feed_sums[3],
            feed_sums[1],
            feed_sums[2],
            expand_bias_sums[0],
            feed_sums[0],
        ]
    )
    while any(one.leaving is not None for one in rest):
        advance(info, jnp.zeros((), f32), rest)
    half = model_width // 2
    source_grads = source_sum.result
    projections = [
        jnp.concatenate([one.result[:, i * half : (i + 1) * half] for one in (low_sum, high_sum)], axis=1)
        for i in range(3)
    ]
    return (
        block_output[None],
        tokens_grad[None],
        patch_sum.result,
        sums[0],
        sums[1],
        projections[0],
        sums[2],
        projections[1],
        projections[2],
        sums[3],
        middle_sum.result[:, model_width:],
        sums[4],
        sums[5],
        sums[6],
        middle_sum.result[:, :model_width],
        sums[7],
        source_grads[:, :model_width],
        source_grads[:, model_width:],
        sums[8],
        merge_sum.result,
        sums[9],
        sums[10],
        sums[11],
        expand_sum.result,
        sums[12],
        reduce_sum.result,
        sums[13],
    )


def solution(mesh):
    placed = (
        P("patch", "tok", None),
        P(("tok", "patch"), None),
        P("patch", "tok", None),
        P(),
        P(),
        P(),
        P(),
        P(),
        P(),
        P(),
        P(),
        P(),
        P(),
        P(),
        P(),
        P(),
        P(),
        P(),
        P(),
        P(),
        P(),
        P(),
        P(),
        P(),
        P(),
        P(),
        P(),
        P(),
        P(),
        P(),
    )
    return jax.shard_map(
        local,
        mesh=mesh,
        in_specs=placed,
        out_specs=(
            P("patch", "tok", None),
            P("patch", "tok", None),
            P(("tok", "patch"), None),
            P(("tok", "patch")),
            P(("tok", "patch")),
            P(("tok", "patch"), None),
            P(("tok", "patch")),
            P(("tok", "patch"), None),
            P(("tok", "patch"), None),
            P(("tok", "patch")),
            P(("tok", "patch"), None),
            P(("tok", "patch")),
            P(("tok", "patch")),
            P(("tok", "patch")),
            P(("tok", "patch"), None),
            P(("tok", "patch")),
            P(("tok", "patch"), None),
            P(("tok", "patch"), None),
            P(("tok", "patch")),
            P(("tok", "patch"), None),
            P(("tok", "patch")),
            P(("tok", "patch")),
            P(("tok", "patch")),
            P(("tok", "patch"), None),
            P(("tok", "patch")),
            P(("tok", "patch"), None),
            P(("tok", "patch")),
        ),
        check_vma=False,
    )
```

```python
import jax
import jax.numpy as jnp
from jax import lax
from jax.experimental import pallas as pl
from jax.experimental.pallas import tpu as pltpu
from jax.sharding import PartitionSpec as P

HDIM = 64
PAIR = 2 * HDIM
PAGE_SLOTS = 512
NEG_FILL = -1e30
EPS_NORM = 1e-05
LANES = 128
PIECE = 512
HIGH = lax.Precision.HIGHEST
MIB = 1 << 20
bf16, f32 = jnp.bfloat16, jnp.float32
Shape = pltpu.HBM


def nn(left, right):
    return lax.dot_general(
        left, right, (((1,), (0,)), ((), ())), preferred_element_type=f32
    )


def nt(left, right, precision=None):
    return lax.dot_general(
        left, right, (((1,), (1,)), ((), ())), precision=precision, preferred_element_type=f32
    )


def tn(left, right):
    return lax.dot_general(
        left, right, (((0,), (0,)), ((), ())), preferred_element_type=f32
    )


def column_sums(values):
    return jnp.sum(values.astype(f32), axis=0, keepdims=True)


def norm_unit(values):
    average = jnp.mean(values, axis=-1, keepdims=True)
    centred = values - average
    spread = jnp.mean(centred * centred, axis=-1, keepdims=True)
    inverse = lax.rsqrt(spread + EPS_NORM)
    return centred * inverse, inverse


def norm_pull(upstream, unit, inverse, gain):
    scaled = upstream * gain
    centred = scaled - jnp.mean(scaled, axis=-1, keepdims=True)
    centred = centred - unit * jnp.mean(scaled * unit, axis=-1, keepdims=True)
    return centred * inverse


def gelu_pair(values):
    share = 0.5 * (1.0 + lax.erf(values * (2.0**-0.5)))
    slope = share + values * (jnp.exp(-0.5 * values * values) * 0.3989422804014327)
    return values * share, slope


def by_core(core, value, each, fine):
    count, width = value.shape
    split = value.reshape(count // (2 * each), 2, each, width)
    found = []
    for own in range(2):
        one = jnp.where((core == 0) == (own == 0), split[:, 1], split[:, 0])
        one = one.reshape(count // (2 * each), each // fine, fine, width)
        columns = [one[..., at : at + PIECE] for at in range(0, width, PIECE)]
        one = columns[0] if len(columns) == 1 else jnp.concatenate(columns, axis=1)
        found.append(one.astype(bf16))
    return found


def head_lanes(head):
    lane = lax.broadcasted_iota(jnp.int32, (1, PAIR), 1)
    return (lane >= head * HDIM) & (lane < (head + 1) * HDIM)


def only(value, head):
    return jnp.where(head_lanes(head), value, jnp.zeros_like(value))


TINY = pl.CostEstimate(flops=1, bytes_accessed=1, transcendentals=0)


def settings(limit=48):
    return pltpu.CompilerParams(
        dimension_semantics=("arbitrary",), vmem_limit_bytes=limit * MIB
    )


def scores_of(key_rows, query, start, mask):
    score = nt(key_rows, query[start:])
    if isinstance(mask, str):
        rows = score.shape[0]
        row = lax.broadcasted_iota(jnp.int32, (rows, rows), 0)
        column = lax.broadcasted_iota(jnp.int32, (rows, rows), 1)
        corner = jnp.where(row <= column, score[:, :rows], NEG_FILL)
        if score.shape[1] == rows:
            return corner
        return jnp.concatenate([corner, score[:, rows:]], axis=1)
    return score if mask is None else score + mask


def from_start(whole, start, part, combine):
    if whole is None:
        return part
    if start == 0:
        return combine(whole, part)
    return jnp.concatenate([whole[:, :start], combine(whole[:, start:], part)], axis=1)


def forward_pair(q_ref, k_ref, v_ref, blocks, begun, out_ref, total_ref):
    values = v_ref[...].T
    outs = []
    for head in range(2):
        lanes = slice(head * HDIM, (head + 1) * HDIM)
        query = only(q_ref[...], head)
        earlier = None if begun is None else begun[1][0, head : head + 1, :]
        row_max, scores = earlier, []
        for first, rows, start, mask in blocks:
            score = scores_of(k_ref[pl.ds(first, rows), :], query, start, mask)
            row_max = from_start(row_max, start, score.max(0, keepdims=True), jnp.maximum)
            scores.append(score)
        total, out = None, None
        if begun is not None:
            total = jnp.exp(earlier - row_max)
            out = begun[0][lanes] * total
        for score, (first, rows, start, _) in zip(scores, blocks):
            exponent = jnp.exp(score - row_max[:, start:])
            total = from_start(total, start, exponent.sum(0, keepdims=True), jnp.add)
            part = nn(values[lanes, first : first + rows], exponent.astype(bf16))
            out = from_start(out, start, part, jnp.add)
        outs.append(out / total)
        total_ref[0, head : head + 1, :] = row_max + jnp.log(total)
    out_ref[...] = jnp.concatenate(outs, axis=0).T.astype(bf16)


def backward_pair(q_ref, k_ref, v_ref, out_ref, total_ref, g_ref, blocks, acc, fresh, dk_ref, dv_ref):
    queries, upstreams, keys = q_ref[...].T, g_ref[...].T, k_ref[...].T
    product = upstreams.astype(f32) * out_ref[...].T.astype(f32)
    for first, rows, start, mask in blocks:
        key_rows, value_rows = k_ref[pl.ds(first, rows), :], v_ref[pl.ds(first, rows), :]
        key_grads, value_grads = [], []
        for head in range(2):
            lanes = slice(head * HDIM, (head + 1) * HDIM)
            inner = product[lanes, start:].sum(0, keepdims=True)
            score = scores_of(key_rows, only(q_ref[...], head), start, mask)
            soft = jnp.exp(score - total_ref[0, head : head + 1, start:])
            grad_soft = nt(value_rows, only(g_ref[...], head)[start:])
            grad_score = (soft * (grad_soft - inner)).astype(bf16)
            value_grads.append(nt(upstreams[lanes, start:], soft.astype(bf16)))
            key_grads.append(nt(queries[lanes, start:], grad_score))
            part = nn(keys[lanes, first : first + rows], grad_score)
            if fresh and first == 0:
                acc[lanes, start:] = part
            else:
                acc[lanes, start:] += part
        dk_ref[pl.ds(first, rows), :] = jnp.concatenate(key_grads, axis=0).T.astype(bf16)
        dv_ref[pl.ds(first, rows), :] = jnp.concatenate(value_grads, axis=0).T.astype(bf16)


def causal_blocks(rows, size=256):
    return [(at, size, at, "causal") for at in range(0, rows, size)]


def totals_shape(rows, width):
    return (width // PAIR, 2, rows)


def own_forward(query, keys, values):
    rows, width = query.shape

    def body(q_ref, k_ref, v_ref, out_ref, total_ref):
        forward_pair(q_ref, k_ref, v_ref, causal_blocks(rows), None, out_ref, total_ref)

    block = pl.BlockSpec((rows, PAIR), lambda p: (0, p))
    total = pl.BlockSpec((1, 2, rows), lambda p: (p, 0, 0))
    return pl.pallas_call(
        body,
        out_shape=(Shape((rows, width), bf16), Shape(totals_shape(rows, width), f32)),
        grid=(width // PAIR,),
        in_specs=[block] * 3,
        out_specs=[block, total],
        cost_estimate=TINY,
        compiler_params=settings(),
        name="own_forward",
    )(query, keys, values)


def lead_forward(query, keys, values, begun, begun_total, trailing):
    rows, width = query.shape

    def body(flag, q_ref, k_ref, v_ref, begun_ref, old_ref, out_ref, total_ref):
        @pl.when(flag[0] == 1)
        def _():
            begun = (begun_ref[...].T.astype(f32), old_ref)
            blocks = [(0, rows, 0, None)]
            forward_pair(q_ref, k_ref, v_ref, blocks, begun, out_ref, total_ref)

        @pl.when(flag[0] == 0)
        def _():
            out_ref[...] = begun_ref[...]
            total_ref[...] = old_ref[...]

    block = pl.BlockSpec((rows, PAIR), lambda p, flag: (0, p))
    total = pl.BlockSpec((1, 2, rows), lambda p, flag: (p, 0, 0))
    return pl.pallas_call(
        body,
        out_shape=(Shape((rows, width), bf16), Shape(totals_shape(rows, width), f32)),
        grid_spec=pltpu.PrefetchScalarGridSpec(
            num_scalar_prefetch=1,
            grid=(width // PAIR,),
            in_specs=[block] * 4 + [total],
            out_specs=[block, total],
        ),
        cost_estimate=TINY,
        compiler_params=settings(),
        name="lead_forward",
    )(trailing, query, keys, values, begun, begun_total)


def slot_bias(filled_ref, slots):
    slot = lax.broadcasted_iota(jnp.int32, (slots, 1), 0)
    return jnp.where(slot < filled_ref[0], 0.0, NEG_FILL)


def cross_forward(query, keys, values, filled):
    rows, width = query.shape
    slots = keys.shape[0]

    def body(filled_ref, q_ref, k_ref, v_ref, out_ref, total_ref):
        blocks = [(0, slots, 0, slot_bias(filled_ref, slots))]
        forward_pair(q_ref, k_ref, v_ref, blocks, None, out_ref, total_ref)

    block = pl.BlockSpec((rows, PAIR), lambda p, f: (0, p))
    page = pl.BlockSpec((slots, PAIR), lambda p, f: (0, p))
    total = pl.BlockSpec((1, 2, rows), lambda p, f: (p, 0, 0))
    return pl.pallas_call(
        body,
        out_shape=(Shape((rows, width), bf16), Shape(totals_shape(rows, width), f32)),
        grid_spec=pltpu.PrefetchScalarGridSpec(
            num_scalar_prefetch=1,
            grid=(width // PAIR,),
            in_specs=[block, page, page],
            out_specs=[block, total],
        ),
        cost_estimate=TINY,
        compiler_params=settings(),
        name="cross_forward",
    )(filled, query, keys, values)


def lead_backward(query, keys, values, out, total, grad, trailing, first, pairs, size=384):
    rows = query.shape[0]

    def body(flag, q_ref, k_ref, v_ref, out_ref, total_ref, g_ref, dq_ref, dk_ref, dv_ref):
        @pl.when(flag[0] == 1)
        def _():
            blocks = [(at, size, 0, None) for at in range(0, rows, size)]
            backward_pair(
                q_ref, k_ref, v_ref, out_ref, total_ref, g_ref, blocks, dq_ref, True, dk_ref, dv_ref
            )

        @pl.when(flag[0] == 0)
        def _():
            for ref in (dq_ref, dk_ref, dv_ref):
                ref[...] = jnp.zeros_like(ref)

    source = pl.BlockSpec((rows, PAIR), lambda p, flag: (0, p + first))
    target = pl.BlockSpec((rows, PAIR), lambda p, flag: (0, p))
    totals = pl.BlockSpec((1, 2, rows), lambda p, flag: (p + first, 0, 0))
    return pl.pallas_call(
        body,
        out_shape=[Shape((pairs * PAIR, rows), f32)] + [Shape((rows, pairs * PAIR), bf16)] * 2,
        grid_spec=pltpu.PrefetchScalarGridSpec(
            num_scalar_prefetch=1,
            grid=(pairs,),
            in_specs=[source] * 4 + [totals, source],
            out_specs=[pl.BlockSpec((PAIR, rows), lambda p, flag: (p, 0)), target, target],
        ),
        cost_estimate=TINY,
        compiler_params=settings(),
        name="lead_backward",
    )(trailing, query, keys, values, out, total, grad)


def own_backward(query, keys, values, out, total, grad, begun, first, pairs):
    rows = query.shape[0]

    def body(q_ref, k_ref, v_ref, out_ref, total_ref, g_ref, begun_ref, dq_ref, dk_ref, dv_ref, acc):
        acc[...] = begun_ref[...]
        backward_pair(
            q_ref, k_ref, v_ref, out_ref, total_ref, g_ref, causal_blocks(rows), acc, False,
            dk_ref, dv_ref,
        )
        dq_ref[...] = (acc[...] * (HDIM**-0.5)).T.astype(bf16)

    source = pl.BlockSpec((rows, PAIR), lambda p: (0, p + first))
    target = pl.BlockSpec((rows, PAIR), lambda p: (0, p))
    totals = pl.BlockSpec((1, 2, rows), lambda p: (p + first, 0, 0))
    return pl.pallas_call(
        body,
        out_shape=[Shape((rows, pairs * PAIR), bf16)] * 3,
        grid=(pairs,),
        in_specs=[source] * 4 + [totals, source, pl.BlockSpec((PAIR, rows), lambda p: (p, 0))],
        out_specs=[target] * 3,
        scratch_shapes=[pltpu.VMEM((PAIR, rows), f32)],
        cost_estimate=TINY,
        compiler_params=settings(),
        name="own_backward",
    )(query, keys, values, out, total, grad, begun)


def cross_backward(query, keys, values, out, total, grad, filled, first, pairs):
    rows, slots = query.shape[0], keys.shape[0]

    def body(
        filled_ref, q_ref, k_ref, v_ref, out_ref, total_ref, g_ref, dq_ref, dk_ref, dv_ref, acc
    ):
        blocks = [(0, slots, 0, slot_bias(filled_ref, slots))]
        backward_pair(
            q_ref, k_ref, v_ref, out_ref, total_ref, g_ref, blocks, acc, True, dk_ref, dv_ref
        )
        dq_ref[...] = (acc[...] * (HDIM**-0.5)).T.astype(bf16)

    source = pl.BlockSpec((rows, PAIR), lambda p, f: (0, p + first))
    page = pl.BlockSpec((slots, PAIR), lambda p, f: (0, p + first))
    target = pl.BlockSpec((rows, PAIR), lambda p, f: (0, p))
    page_target = pl.BlockSpec((slots, PAIR), lambda p, f: (0, p))
    totals = pl.BlockSpec((1, 2, rows), lambda p, f: (p + first, 0, 0))
    return pl.pallas_call(
        body,
        out_shape=[Shape((rows, pairs * PAIR), bf16)] + [Shape((slots, pairs * PAIR), bf16)] * 2,
        grid_spec=pltpu.PrefetchScalarGridSpec(
            num_scalar_prefetch=1,
            grid=(pairs,),
            in_specs=[source, page, page, source, totals, source],
            out_specs=[target, page_target, page_target],
            scratch_shapes=[pltpu.VMEM((PAIR, rows), f32)],
        ),
        cost_estimate=TINY,
        compiler_params=settings(),
        name="cross_backward",
    )(filled, query, keys, values, out, total, grad)


def feed_forward(after_one, mixed, merge, cotangent, vectors, expand, bias, reduce, info, owners):
    rows, width = after_one.shape
    hidden = expand.shape[1]
    block, tall = PIECE, 384
    steps, fine, others = hidden // block, width // owners, owners // 2
    tall_pieces = hidden // owners // fine * (width // PIECE)
    starts = range(0, rows, tall)

    def body(
        info_ref, after_ref, mixed_ref, merge_ref, cot_ref, vec_ref, we_ref, be_ref, wr_ref,
        out_ref, two_ref, cross_ref, rs_ref, ro_ref, es_ref, eo_ref, ms_ref, mo_ref, eb_ref,
        sums_ref, after, h, h_flip, g, branch, up, act, gp,
    ):
        step = pl.program_id(0)
        core, place, length = info_ref[0], info_ref[1], info_ref[2]

        def valid(start):
            row = lax.broadcasted_iota(jnp.int32, (tall, 1), 0) + (start + place)
            return (row < length).astype(f32)

        @pl.when(step == 0)
        def _():
            total = jnp.zeros((1, width), f32)
            for start in starts:
                at = pl.ds(start, tall)
                x = after_ref[at, :] + nn(mixed_ref[at, :], merge_ref[...]) + vec_ref[0:1, :]
                after[at, :] = x
                unit, _ = norm_unit(x)
                low = (unit * vec_ref[1:2, :] + vec_ref[2:3, :]).astype(bf16)
                h[at, :] = low
                h_flip[:, at] = low.T
                grad = (valid(start) * cot_ref[at, :].astype(f32)).astype(bf16)
                g[at, :] = grad
                total = total + column_sums(grad)
                branch[at, :] = jnp.zeros((tall, width), f32)
                up[at, :] = jnp.zeros((tall, width), f32)
            sums_ref[0:1, :] = total

        we, wr = we_ref[...], wr_ref[...]
        for start in starts:
            at = pl.ds(start, tall)
            low, slope = gelu_pair(nn(h[at, :], we) + be_ref[...])
            low = low.astype(bf16)
            act[at, :] = low
            branch[at, :] += nn(low, wr)
            grad = (nt(g[at, :], wr) * slope).astype(bf16)
            gp[at, :] = grad
            up[at, :] += nt(grad, we)
        rs_ref[...], ro_ref[...] = by_core(core, tn(act[...], g[...]), hidden // owners, fine)
        es_ref[...], eo_ref[...] = by_core(core, nn(h_flip[...], gp[...]), fine, fine)
        eb_ref[...] = nn(jnp.ones((8, rows), bf16), gp[...])

        @pl.when(step == steps - 1)
        def _():
            gains = jnp.zeros((1, width), f32)
            shifts, merges = gains, gains
            for start in starts:
                at = pl.ds(start, tall)
                x, ok = after[at, :], valid(start)
                out_ref[at, :] = (ok * (x + branch[at, :] + vec_ref[3:4, :])).astype(bf16)
                unit, inverse = norm_unit(x)
                upstream = up[at, :]
                gains = gains + jnp.sum(upstream * unit, axis=0, keepdims=True)
                shifts = shifts + jnp.sum(upstream, axis=0, keepdims=True)
                pulled = norm_pull(upstream, unit, inverse, vec_ref[1:2, :])
                two = ok * cot_ref[at, :].astype(f32) + pulled
                two_ref[at, :] = two
                low = two.astype(bf16)
                g[at, :] = low
                merges = merges + column_sums(low)
                cross_ref[at, :] = nt(low, merge_ref[...]).astype(bf16)
            ms_ref[...], mo_ref[...] = by_core(core, tn(mixed_ref[...], g[...]), fine, fine)
            sums_ref[1:2, :], sums_ref[2:3, :], sums_ref[3:4, :] = gains, shifts, merges

    def once(shape):
        return pl.BlockSpec(shape, lambda i, info: (0, 0), pipeline_mode=pl.Buffered(1))

    def fixed(shape):
        return pl.BlockSpec(shape, lambda i, info: (0,) * len(shape))

    rows_each = others // steps
    by_row = pl.BlockSpec((rows_each, tall_pieces, fine, PIECE), lambda i, info: (i, 0, 0, 0))
    by_column = pl.BlockSpec((others, 1, fine, PIECE), lambda i, info: (0, i, 0, 0))
    merged = (others, width // PIECE, fine, PIECE)
    full, low = (rows, width), (rows, width)
    return pl.pallas_call(
        body,
        out_shape=[
            Shape(full, bf16), Shape(full, f32), Shape(full, bf16),
            *[Shape((others, tall_pieces, fine, PIECE), bf16)] * 2,
            *[Shape((others, steps, fine, PIECE), bf16)] * 2,
            *[Shape(merged, bf16)] * 2,
            Shape((8, hidden), f32), Shape((8, width), f32),
        ],
        grid_spec=pltpu.PrefetchScalarGridSpec(
            num_scalar_prefetch=1,
            grid=(steps,),
            in_specs=[
                once(full), once(full), once((width, width)), once(full), once((8, width)),
                pl.BlockSpec((width, block), lambda i, info: (0, i)),
                pl.BlockSpec((1, block), lambda i, info: (0, i)),
                pl.BlockSpec((block, width), lambda i, info: (i, 0)),
            ],
            out_specs=[
                fixed(full), fixed(full), fixed(full), by_row, by_row, by_column, by_column,
                fixed(merged), fixed(merged),
                pl.BlockSpec((8, block), lambda i, info: (0, i)),
                fixed((8, width)),
            ],
            scratch_shapes=[
                pltpu.VMEM(full, f32), pltpu.VMEM(low, bf16), pltpu.VMEM((width, rows), bf16),
                pltpu.VMEM(low, bf16), pltpu.VMEM(full, f32), pltpu.VMEM(full, f32),
                pltpu.VMEM((rows, block), bf16), pltpu.VMEM((rows, block), bf16),
            ],
        ),
        cost_estimate=TINY,
        compiler_params=settings(60),
        name="feed_forward",
    )(info, after_one, mixed, merge, cotangent, vectors, expand, bias, reduce)


def streamed(name, body, info, inputs, outs, scratch=()):
    n, m = len(inputs), len(outs)

    def kernel(info_ref, *refs):
        ins, dests = refs[:n], refs[n : n + m]
        held, made = refs[n + m : 2 * n + m], refs[2 * n + m : 2 * n + 2 * m]
        in_sem, out_sem = refs[2 * n + 2 * m : 2 * n + 2 * m + 2]
        rest = refs[2 * n + 2 * m + 2 :]
        loads = [pltpu.make_async_copy(ins[i], held[i], in_sem.at[i]) for i in range(n)]
        for load in loads:
            load.start()
        waited, stores = set(), {}

        def need(i):
            if i not in waited:
                loads[i].wait()
                waited.add(i)
            return held[i]

        def give(i, send=False):
            if send:
                stores[i] = pltpu.make_async_copy(made[i], dests[i], out_sem.at[i])
                stores[i].start()
            return made[i]

        body(info_ref, need, give, *rest)
        for i in range(m):
            stores[i].wait()

    anywhere = pl.BlockSpec(memory_space=pltpu.HBM)
    return pl.pallas_call(
        kernel,
        out_shape=[Shape(shape, kind) for shape, kind in outs],
        grid_spec=pltpu.PrefetchScalarGridSpec(
            num_scalar_prefetch=1,
            grid=(1,),
            in_specs=[anywhere] * n,
            out_specs=[anywhere] * m,
            scratch_shapes=[pltpu.VMEM(value.shape, value.dtype) for value in inputs]
            + [pltpu.VMEM(shape, kind) for shape, kind in outs]
            + [pltpu.SemaphoreType.DMA((n,)), pltpu.SemaphoreType.DMA((m,))]
            + list(scratch),
        ),
        cost_estimate=TINY,
        compiler_params=settings(60),
        name=name,
    )(info, *inputs)


def probe_backward(info, probe_low, probe_high, probe_weight, after_one, two, output_weight, mixed, vectors, owners):
    rows, width = after_one.shape
    half, tall, fine = width // 2, 256, width // owners

    def body(info_ref, need, give, hidden, low_grad):
        core = info_ref[0]
        left, right = need(0), need(1)
        weight = need(2)
        vec = need(7)
        x_ref, two_ref = need(3), need(4)
        gains = jnp.zeros((1, width), f32)
        shifts, outs = gains, gains
        for start in range(0, rows, tall):
            at = pl.ds(start, tall)
            up = nt(left[at, :], weight[:, :half]) + nt(right[at, :], weight[:, half:])
            unit, inverse = norm_unit(x_ref[at, :])
            hidden[at, :] = (unit * vec[0:1, :] + vec[1:2, :]).astype(bf16)
            gains = gains + jnp.sum(up * unit, axis=0, keepdims=True)
            shifts = shifts + jnp.sum(up, axis=0, keepdims=True)
            one = two_ref[at, :] + norm_pull(up, unit, inverse, vec[0:1, :])
            give(0)[at, :] = one
            low = one.astype(bf16)
            low_grad[at, :] = low
            outs = outs + column_sums(low)
            if start == 0:
                need(5)
            give(1)[at, :] = nt(low, need(5)[...]).astype(bf16)
        give(0, True)
        give(1, True)
        sums = give(4)
        sums[...] = jnp.zeros_like(sums)
        sums[0:1, :], sums[1:2, :], sums[2:3, :] = gains, shifts, outs
        sums[3:4, :half] = column_sums(left[...])
        sums[3:4, half:] = column_sums(right[...])
        give(4, True)
        mixed_ref = need(6)
        columns = (
            (0, 1, hidden, left[...]),
            (1, 2, hidden, right[...]),
            (2, 4, mixed_ref, low_grad[...]),
        )
        for begin, end, source, grads in columns:
            pair = by_core(core, tn(source[...], grads), fine, fine)
            give(2)[:, begin:end], give(3)[:, begin:end] = pair
        give(2, True)
        give(3, True)

    return streamed(
        "probe_backward",
        body,
        info,
        [probe_low, probe_high, probe_weight, after_one, two, output_weight, mixed, vectors],
        [
            ((rows, width), f32), ((rows, width), bf16),
            ((owners // 2, 4, fine, PIECE), bf16), ((owners // 2, 4, fine, PIECE), bf16),
            ((8, width), f32),
        ],
        [pltpu.VMEM((rows, width), bf16), pltpu.VMEM((rows, width), bf16)],
    )


def page_backward(
    info, key_low, key_high, value_low, value_high, page_rows, key_weight, value_weight, owners,
    patch_total,
):
    slots, width = page_rows.shape
    half, fine = width // 2, width // owners
    patch_shape = (owners // 2, patch_total // owners // fine * (width // PIECE), fine, PIECE)

    def body(info_ref, need, give):
        core, page = info_ref[0], info_ref[3]
        kl, kh, vl, vh = need(0)[...], need(1)[...], need(2)[...], need(3)[...]
        rows_ref = need(4)
        for i, grads in enumerate((kl, kh, vl, vh)):
            pair = by_core(core, tn(rows_ref[...], grads), fine, fine)
            give(0)[:, i : i + 1], give(1)[:, i : i + 1] = pair
        give(0, True)
        give(1, True)
        wk, wv = need(5), need(6)
        total = nt(kl, wk[:, :half]) + nt(kh, wk[:, half:])
        total = total + nt(vl, wv[:, :half]) + nt(vh, wv[:, half:])
        pair = by_core(core, total, patch_total // owners, fine)
        each = pair[0].shape[0]
        at = pl.ds(pl.multiple_of(page * each, each), each)
        for which in range(2):
            give(2 + which)[...] = jnp.zeros(patch_shape, bf16)
            give(2 + which)[at] = pair[which]
            give(2 + which, True)
        sums = give(4)
        sums[...] = jnp.zeros_like(sums)
        sums[0:1, :half] = column_sums(vl)
        sums[0:1, half:] = column_sums(vh)
        give(4, True)

    return streamed(
        "page_backward",
        body,
        info,
        [key_low, key_high, value_low, value_high, page_rows, key_weight, value_weight],
        [
            ((owners // 2, 4, fine, PIECE), bf16), ((owners // 2, 4, fine, PIECE), bf16),
            (patch_shape, bf16), (patch_shape, bf16), ((8, width), f32),
        ],
    )


def lead_upstream(info, keys, values, key_weight, value_weight, lead_tokens, vectors):
    rows, width = lead_tokens.shape
    half, tall = width // 2, 256

    def body(info_ref, need, give, hidden):
        kl, kh, vl, vh = need(0), need(1), need(2), need(3)
        wk, wv = need(4), need(5)
        x_ref, vec = need(6), need(7)
        gains = jnp.zeros((1, width), f32)
        shifts = gains
        for start in range(0, rows, tall):
            at = pl.ds(start, tall)
            up = nt(kl[at, :], wk[:, :half]) + nt(kh[at, :], wk[:, half:])
            up = up + nt(vl[at, :], wv[:, :half]) + nt(vh[at, :], wv[:, half:])
            give(0)[at, :] = up.astype(bf16)
            unit, _ = norm_unit(x_ref[at, :].astype(f32))
            hidden[at, :] = (unit * vec[0:1, :] + vec[1:2, :]).astype(bf16)
            gains = gains + jnp.sum(up * unit, axis=0, keepdims=True)
            shifts = shifts + jnp.sum(up, axis=0, keepdims=True)
        give(0, True)
        sums = give(2)
        sums[...] = jnp.zeros_like(sums)
        sums[0:1, :], sums[1:2, :] = gains, shifts
        sums[2:3, :half], sums[2:3, half:] = column_sums(vl[...]), column_sums(vh[...])
        give(2, True)
        for i, ref in enumerate((kl, kh, vl, vh)):
            give(1)[:, i * half : (i + 1) * half] = tn(hidden[...], ref[...]).astype(bf16)
        give(1, True)

    return streamed(
        "lead_upstream",
        body,
        info,
        [*keys, *values, key_weight, value_weight, lead_tokens, vectors],
        [((rows, width), bf16), ((width, 2 * width), bf16), ((8, width), f32)],
        [pltpu.VMEM((rows, width), bf16)],
    )


def projection_grads(info, hidden, query_grad, key_grad, value_grad, lead_part, high, owners):
    rows, width = hidden.shape
    half, fine = width // 2, width // owners
    column = half if high else 0

    def body(info_ref, need, give):
        core = info_ref[0]
        h = need(0)
        for i in range(3):
            total = tn(h[...], need(1 + i)[...])
            if i:
                base = (i - 1) * width + column
                total = total + need(4)[:, base : base + half].astype(f32)
            pair = by_core(core, total, fine, fine)
            give(0)[:, i : i + 1], give(1)[:, i : i + 1] = pair
        give(0, True)
        give(1, True)

    return streamed(
        "projection_grads",
        body,
        info,
        [hidden, query_grad, key_grad, value_grad, lead_part],
        [((owners // 2, 3, fine, PIECE), bf16)] * 2,
    )


def first_norm_backward(info, queries, keys, values, weights, tokens, one, returned, vectors, first, count, held):
    rows, width = tokens.shape
    half, tall = width // 2, count // 2
    n = 0 if held is None else 1

    def body(info_ref, *refs):
        grads = refs[:6]
        wq, wk, wv, x_ref, vec, one_ref, back_ref = refs[6:13]
        out_ref, sums = refs[13 + n :]
        gains = jnp.zeros((1, width), f32)
        shifts = gains
        for start in range(0, count, tall):
            at = pl.ds(start, tall)
            up = 0.0
            for i, weight in enumerate((wq, wk, wv)):
                up = up + nt(grads[2 * i][at, :], weight[:, :half])
                up = up + nt(grads[2 * i + 1][at, :], weight[:, half:])
            unit, inverse = norm_unit(x_ref[at, :].astype(f32))
            gains = gains + jnp.sum(up * unit, axis=0, keepdims=True)
            shifts = shifts + jnp.sum(up, axis=0, keepdims=True)
            up = up + back_ref[at, :].astype(f32)
            out_ref[at, :] = one_ref[at, :] + norm_pull(up, unit, inverse, vec[0:1, :])
        sums[...] = jnp.zeros_like(sums)
        sums[0:1, :], sums[1:2, :] = gains, shifts
        sums[2:3, :half], sums[2:3, half:] = column_sums(grads[0][...]), column_sums(grads[1][...])
        sums[3:4, :half], sums[3:4, half:] = column_sums(grads[4][...]), column_sums(grads[5][...])

    block = first // count
    narrow = pl.BlockSpec((count, half), lambda i, info: (block, 0))
    wide = pl.BlockSpec((count, width), lambda i, info: (block, 0))
    whole = pl.BlockSpec((width, width), lambda i, info: (0, 0))
    eight = pl.BlockSpec((8, width), lambda i, info: (0, 0))
    return pl.pallas_call(
        body,
        out_shape=[Shape((rows, width), f32), Shape((8, width), f32)],
        grid_spec=pltpu.PrefetchScalarGridSpec(
            num_scalar_prefetch=1,
            grid=(1,),
            in_specs=[narrow] * 6 + [whole] * 3 + [wide, eight, wide, wide]
            + [pl.BlockSpec(memory_space=pltpu.HBM)] * n,
            out_specs=[wide, eight],
        ),
        input_output_aliases={14: 0} if n else {},
        cost_estimate=TINY,
        compiler_params=settings(),
        name="first_norm_backward",
    )(
        info, *queries, *keys, *values, *weights, tokens, vectors, one, returned,
        *([] if held is None else [held]),
    )


def digit_axes():
    patch_bits = lax.axis_size("patch").bit_length() - 1
    return [("tok", 0)] + [("patch", bit) for bit in reversed(range(patch_bits))]


def my_digit(axis, bit):
    return (lax.axis_index(axis) >> bit) & 1


def tied(*values):
    return lax.optimization_barrier(values)


FIRST_DIGIT = 4


class Part:
    def __init__(self, kept, tok_first, shape, start=0, pieces=None):
        self.tok_first, self.shape = tok_first, shape
        self.pieces = pieces or kept.shape[1]
        self.terms = [(kept, owner_digits(), start)]


def owner_digits():
    return digit_axes()[:-1]


def stages_of(tok_first):
    every = digit_axes()
    bits = every[-2:0:-1]
    loose, last = bits[: max(len(bits) - 2, 0)], bits[max(len(bits) - 2, 0) :]
    singles = [[one] for one in loose]
    return ([every[:1]] + singles if tok_first else singles + [every[:1]]) + [last]


class Sum:
    def __init__(self, *sent):
        self.parts = [part for _, parts in sent for part in parts]
        self.at = 0
        self.leaving = [array for array, _ in sent]
        self.hops = [[("patch", 0)]] * len(sent)
        self.groups = [parts for _, parts in sent]
        self.mine = self.results = None

    def send(self):
        self.arrived = [hop(value, steps) for value, steps in zip(self.leaving, self.hops)]

    def free(self, part, at):
        settled = [one for stage in stages_of(part.tok_first)[:at] for one in stage]
        return [one for one in owner_digits() if one not in settled]

    def absorb(self, arrived):
        if self.mine is not None:
            self.results = finished([part for part in self.parts], self.mine, arrived)
            self.leaving = None
            return []
        for value, group in zip(arrived, self.groups):
            start = 0
            for part in group:
                part.terms = part.terms + [(value, self.free(part, self.at), start)]
                start += part.pieces
        stages = [stages_of(part.tok_first) for part in self.parts]
        last = self.at == len(stages[0]) - 1
        ways = [stage[self.at] for stage in stages]
        self.at += 1
        jobs, self.hops, self.groups = [], [], []
        for digits in [way for i, way in enumerate(ways) if way not in ways[:i]]:
            group = [part for part, way in zip(self.parts, ways) if way == digits]
            free = self.free(group[0], self.at)
            for flips in range(0 if last else 1, 1 << len(digits)):
                flipped = [one for i, one in enumerate(digits) if flips >> i & 1]
                choices = []
                for chunk in range(1 << len(free)):
                    bits = {one: chunk >> (len(free) - 1 - i) & 1 for i, one in enumerate(free)}
                    choices.append((bits, flipped))
                terms = [(part.terms, part.pieces) for part in group]
                jobs.append((terms, choices, bf16 if flips else f32))
                if flips:
                    self.hops.append(flipped)
                    self.groups.append(group)
        return jobs

    def take(self, made):
        if self.at == len(stages_of(True)):
            self.mine = made[0]
            made = made[1:]
        self.leaving = list(made)


def hop(value, steps):
    axis = steps[0][0]
    flip = sum(1 << bit for _, bit in steps)
    return lax.ppermute(value, axis, [(i, i ^ flip) for i in range(lax.axis_size(axis))])


def finished(parts, mine, arrived):
    def body(mine_ref, *refs):
        came, outs = refs[: len(arrived)], refs[len(arrived) :]
        piece = 0
        for part, out in zip(parts, outs):
            fine = mine_ref.shape[2]
            tall = out.shape[0] // fine
            for p in range(part.pieces):
                total = mine_ref[0, piece]
                for ref in came:
                    total = total + ref[0, piece].astype(f32)
                row, column = p % tall * fine, p // tall * PIECE
                out[row : row + fine, column : column + PIECE] = total
                piece += 1

    return pl.pallas_call(
        body,
        out_shape=[Shape(part.shape, f32) for part in parts],
        cost_estimate=TINY,
        compiler_params=pltpu.CompilerParams(vmem_limit_bytes=40 * MIB),
        name="finished",
    )(mine, *arrived)


def added_up(info, jobs):
    digits = digit_axes()
    arrays, known = [], {}
    for parts, _, _ in jobs:
        for terms, _ in parts:
            for value, _, _ in terms:
                if id(value) not in known:
                    known[id(value)] = len(arrays)
                    arrays.append(value)
    fine = arrays[0].shape[2]
    units = [(job, part) for job in range(len(jobs)) for part in range(len(jobs[job][0]))]
    loads = sum(len(jobs[job][0][part][0]) * len(jobs[job][1]) for job, part in units)

    def body(info_ref, *refs):
        n, m, k = len(arrays), len(jobs), len(units)
        ins, dests = refs[:n], refs[n : n + m]
        held, made = refs[n + m : n + m + k], refs[n + m + k : n + 2 * m + k]
        in_sem, out_sem = refs[n + 2 * m + k :]
        mine = {one: info_ref[FIRST_DIGIT + i] for i, one in enumerate(digits)}
        copies, count = [], 0
        for unit, (job, part) in enumerate(units):
            terms, pieces = jobs[job][0][part]
            copies.append([])
            for t, (value, free, start) in enumerate(terms):
                for c, (bits, flipped) in enumerate(jobs[job][1]):
                    index = 0
                    for one in free:
                        digit = bits[one] if one in bits else mine[one]
                        digit = 1 - digit if one in flipped else digit
                        index = 2 * index + digit
                    copy = pltpu.make_async_copy(
                        ins[known[id(value)]].at[index, pl.ds(start, pieces)],
                        held[unit].at[t, c],
                        in_sem.at[count],
                    )
                    copy.start()
                    copies[-1].append(copy)
                    count += 1
        offsets = [0] * m
        left = [len(jobs[job][0]) for job in range(m)]
        stores = []
        for unit, (job, part) in enumerate(units):
            terms, pieces = jobs[job][0][part]
            for copy in copies[unit]:
                copy.wait()
            offset = offsets[job]

            batch = max(one for one in range(1, 9) if pieces % one == 0)
            per = pieces // batch

            def step(i, _, unit=unit, job=job, count=len(terms), per=per, batch=batch, offset=offset):
                chunk = i // per
                for p in range(batch):
                    piece = i % per * batch + p
                    total = held[unit][0, chunk, piece].astype(f32)
                    for t in range(1, count):
                        total = total + held[unit][t, chunk, piece].astype(f32)
                    made[job][chunk, offset + piece] = total.astype(jobs[job][2])
                return 0

            lax.fori_loop(0, len(jobs[job][1]) * per, step, 0)
            offsets[job] += pieces
            left[job] -= 1
            if not left[job]:
                stores.append(pltpu.make_async_copy(made[job], dests[job], out_sem.at[job]))
                stores[-1].start()
        for store in stores:
            store.wait()

    anywhere = pl.BlockSpec(memory_space=pltpu.HBM)
    shapes = [
        ((len(choices), sum(pieces for _, pieces in parts), fine, PIECE), kind)
        for parts, choices, kind in jobs
    ]
    held = [
        pltpu.VMEM(
            (len(jobs[job][0][part][0]), len(jobs[job][1]), jobs[job][0][part][1], fine, PIECE), bf16
        )
        for job, part in units
    ]
    return pl.pallas_call(
        body,
        out_shape=[Shape(shape, kind) for shape, kind in shapes],
        grid_spec=pltpu.PrefetchScalarGridSpec(
            num_scalar_prefetch=1,
            grid=(1,),
            in_specs=[anywhere] * len(arrays),
            out_specs=[anywhere] * len(jobs),
            scratch_shapes=held
            + [pltpu.VMEM(shape, kind) for shape, kind in shapes]
            + [pltpu.SemaphoreType.DMA((loads,)), pltpu.SemaphoreType.DMA((len(jobs),))],
        ),
        cost_estimate=TINY,
        compiler_params=settings(60),
        name="added_up",
    )(info, *arrays)


def advance(info, chain, moving=(), fresh=()):
    moving = [one for one in moving if one.leaving is not None]
    chain, arrived = tied(chain, [one.arrived for one in moving])
    jobs, owners = [], []
    for one, values in zip(moving, arrived):
        new = one.absorb(values)
        owners.append((one, len(new)))
        jobs += new
    if jobs:
        made = added_up(info, jobs)
        for one, count in owners:
            if count:
                one.take(made[:count])
                made = made[count:]
    going = [one for one in moving + list(fresh) if one.leaving is not None]
    chain, leaving = tied(chain, [one.leaving for one in going])
    for one, values in zip(going, leaving):
        one.leaving = values
        one.send()
    return chain


def vector_table(feed, expand_bias, probe, page, lead, first_low, first_high):
    width = feed.shape[1]

    def body(feed_ref, bias_ref, probe_ref, page_ref, lead_ref, low_ref, high_ref, out):
        rows = [
            low_ref[0:1, :] + high_ref[0:1, :] + lead_ref[0:1, :],
            low_ref[1:2, :] + high_ref[1:2, :] + lead_ref[1:2, :],
            low_ref[2:3, :] + high_ref[2:3, :],
            low_ref[3:4, :] + high_ref[3:4, :] + lead_ref[2:3, :],
            probe_ref[2:3, :],
            probe_ref[0:1, :],
            probe_ref[1:2, :],
            probe_ref[3:4, :],
            page_ref[0:1, :],
            feed_ref[3:4, :],
            feed_ref[1:2, :],
            feed_ref[2:3, :],
            feed_ref[0:1, :],
        ]
        out[...] = jnp.zeros_like(out)
        for i, row in enumerate(rows):
            out[i : i + 1, :] = row
        out[16 : 16 + bias_ref.shape[0], :] = bias_ref[...]

    return pl.pallas_call(
        body,
        out_shape=jax.ShapeDtypeStruct((24, width), f32),
        cost_estimate=TINY,
        name="vector_table",
    )(feed, expand_bias, probe, page, lead, first_low, first_high)


def scatter_rows(table, width, first, last):
    digits = digit_axes()
    fine = width >> len(digits)
    for axis, bit in digits[first:last]:
        half = table.shape[1] // 2
        if half % LANES:
            table = table + hop(table, [(axis, bit)])
        else:
            digit = my_digit(axis, bit)
            keep = lax.dynamic_slice_in_dim(table, digit * half, half, 1)
            give = lax.dynamic_slice_in_dim(table, (1 - digit) * half, half, 1)
            table = keep + hop(give, [(axis, bit)])
    if last < len(digits):
        return table
    inside = 0
    for axis, bit in digits[(table.shape[1] // fine).bit_length() * -1 + 1 :]:
        inside = 2 * inside + my_digit(axis, bit)
    return lax.dynamic_slice_in_dim(table, inside * fine, fine, 1)


def pick_entry(table, position):
    indices = jnp.arange(table.shape[0], dtype=jnp.int32)
    return jnp.sum(jnp.where(indices == position, table, 0))


def layer_norm(values, gain, shift):
    unit, _ = norm_unit(values)
    return (unit * gain + shift).astype(bf16)


def rows_of(*vectors):
    rows = jnp.stack(vectors, axis=0)
    return jnp.pad(rows, ((0, 8 - len(vectors)), (0, 0)))


def local(
    tokens,
    patches,
    cotangent,
    lengths,
    page_of,
    page_counts,
    self_gain,
    self_shift,
    query_weight,
    query_bias,
    key_weight,
    value_weight,
    value_bias,
    output_weight,
    output_bias,
    cross_gain,
    cross_shift,
    probe_weight,
    probe_bias,
    source_key,
    source_value,
    source_bias,
    merge_weight,
    merge_bias,
    feed_gain,
    feed_shift,
    expand_weight,
    expand_bias,
    reduce_weight,
    reduce_bias,
):
    head_scale = HDIM ** (-0.5)
    tok_index = lax.axis_index("tok").astype(jnp.int32)
    sequence = lax.axis_index("patch")
    core = my_digit("patch", 0).astype(jnp.int32)
    row_count, model_width = tokens.shape[1:]
    lead_tokens = lax.ppermute(tokens[0], "tok", [(0, 1)])
    gathered = lax.all_gather(patches, ("tok", "patch"), axis=0, tiled=True)
    inputs = tokens[0].astype(f32)
    page_index = pick_entry(page_of, sequence)
    filled = pick_entry(page_counts, page_index).reshape(1)
    trailing = tok_index.reshape(1)
    page_start = page_index * PAGE_SLOTS
    digits = [my_digit(*one).astype(jnp.int32) for one in digit_axes()]
    owners = 1 << len(digits)
    info = jnp.stack(
        [core, tok_index * row_count, pick_entry(lengths, sequence), page_index] + digits
    )
    self_vectors = rows_of(self_gain, self_shift)
    cross_vectors = rows_of(cross_gain, cross_shift)
    feed_vectors = rows_of(merge_bias, feed_gain, feed_shift, reduce_bias)

    hidden_one = layer_norm(inputs, self_gain, self_shift)
    query = ((nn(hidden_one, query_weight) + query_bias) * head_scale).astype(bf16)
    own_keys = nn(hidden_one, key_weight).astype(bf16)
    own_values = (nn(hidden_one, value_weight) + value_bias).astype(bf16)
    own_mixed, own_total = own_forward(query, own_keys, own_values)
    lead_tokens, own_mixed = tied(lead_tokens, own_mixed)
    hidden_lead = layer_norm(lead_tokens.astype(f32), self_gain, self_shift)
    lead_keys = nn(hidden_lead, key_weight).astype(bf16)
    lead_values = (nn(hidden_lead, value_weight) + value_bias).astype(bf16)
    self_mixed, self_total = lead_forward(
        query, lead_keys, lead_values, own_mixed, own_total, trailing
    )
    after_one = inputs + nn(self_mixed, output_weight) + output_bias
    hidden_two = layer_norm(after_one, cross_gain, cross_shift)
    probe = ((nn(hidden_two, probe_weight) + probe_bias) * head_scale).astype(bf16)
    page_rows = lax.dynamic_slice_in_dim(gathered, page_start, PAGE_SLOTS, 0)
    page_keys = nn(page_rows, source_key).astype(bf16)
    page_values = (nn(page_rows, source_value) + source_bias).astype(bf16)
    cross_mixed, cross_total = cross_forward(probe, page_keys, page_values, filled)

    fed = feed_forward(
        after_one, cross_mixed, merge_weight, cotangent[0], feed_vectors, expand_weight,
        expand_bias[None], reduce_weight, info, owners,
    )
    block_output, grad_two, grad_cross_out = fed[:3]
    feed_sums, expand_bias_sums = fed[10], fed[9]
    fine, model = model_width // owners, (model_width // owners, model_width)
    half_model = (fine, model_width // 2)
    first = Sum(
        (fed[5], [Part(fed[6], True, (fine, expand_weight.shape[1]))]),
        (fed[3], [Part(fed[4], False, (expand_weight.shape[1] // owners, model_width))]),
        (fed[7], [Part(fed[8], False, model)]),
    )

    half_pairs = model_width // PAIR // 2
    cross_args = (probe, page_keys, page_values, cross_mixed, cross_total)
    grad_cross_out = advance(info, grad_cross_out, [], [first])
    low = cross_backward(*cross_args, grad_cross_out, filled, 0, half_pairs)
    low, grad_cross_out = advance(info, (low, grad_cross_out), [first])
    high = cross_backward(*cross_args, grad_cross_out, filled, half_pairs, half_pairs)
    patch_total = patches.shape[0] * lax.axis_size(("tok", "patch"))
    paged = page_backward(
        info, low[1], high[1], low[2], high[2], page_rows, source_key, source_value, owners,
        patch_total,
    )
    probed = probe_backward(
        info, low[0], high[0], probe_weight, after_one, grad_two, output_weight, self_mixed,
        cross_vectors, owners,
    )
    grad_one, grad_self_out, probe_sums = probed[0], probed[1], probed[4]
    second = Sum(
        (paged[0], [Part(paged[1], True, (fine, 2 * model_width))]),
        (paged[2], [Part(paged[3], False, (patches.shape[0], model_width))]),
        (probed[2], [Part(probed[3], False, (fine, 2 * model_width))]),
    )
    self_args = (query, lead_keys, lead_values, self_mixed, self_total)
    own_args = (query, own_keys, own_values, self_mixed, self_total)
    grad_self_out = advance(info, grad_self_out, [first], [second])
    lead_low = lead_backward(*self_args, grad_self_out, trailing, 0, half_pairs)
    lead_low, grad_self_out = advance(info, (lead_low, grad_self_out), [first, second])
    lead_high = lead_backward(*self_args, grad_self_out, trailing, half_pairs, half_pairs)
    led_grad, led_part, lead_sums = lead_upstream(
        info, (lead_low[1], lead_high[1]), (lead_low[2], lead_high[2]), key_weight,
        value_weight, lead_tokens, self_vectors,
    )
    led_grad, led_part, grad_self_out = advance(
        info, (led_grad, led_part, grad_self_out), [first, second]
    )
    own_low = own_backward(*own_args, grad_self_out, lead_low[0], 0, half_pairs)
    own_low, led_grad = advance(info, (own_low, led_grad), [second])
    returned = lax.ppermute(led_grad, "tok", [(1, 0)])
    parts = projection_grads(info, hidden_one, *own_low, led_part, False, owners)
    third = Sum((parts[0], [Part(parts[1], i == 1, half_model, i, 1) for i in range(3)]))
    own_low, grad_self_out = advance(info, (own_low, grad_self_out), [], [third])
    own_high = own_backward(*own_args, grad_self_out, lead_high[0], half_pairs, half_pairs)
    own_high, led_part = advance(info, (own_high, led_part), [second, third])
    parts = projection_grads(info, hidden_one, *own_high, led_part, True, owners)
    fourth = Sum((parts[0], [Part(parts[1], i != 1, half_model, i, 1) for i in range(3)]))
    own_low, own_high, returned = advance(
        info, (own_low, own_high, returned), [third], [fourth]
    )
    first_norm = (
        info, (own_low[0], own_high[0]), (own_low[1], own_high[1]), (own_low[2], own_high[2]),
        (query_weight, key_weight, value_weight), tokens[0], grad_one, returned, self_vectors,
    )
    top = first_norm_backward(*first_norm, 0, row_count // 2, None)
    top = advance(info, top, [third, fourth])
    rest = first_norm_backward(*first_norm, row_count // 2, row_count // 2, top[0])
    tokens_grad = rest[0]
    top_sums, rest_sums = advance(info, (top[1], rest[1]), [third, fourth])
    bias_rows = expand_bias_sums[0].reshape(owners, -1, fine)
    bias_rows = jnp.transpose(bias_rows, (1, 0, 2)).reshape(-1, model_width)
    table = vector_table(
        feed_sums, bias_rows, probe_sums, paged[4], lead_sums, top_sums, rest_sums
    )
    table = scatter_rows(table, model_width, 0, 3)
    table = advance(info, table, [third, fourth])
    sums = scatter_rows(table, model_width, 3, len(digits))
    totals = [first, second, third, fourth]
    while any(one.leaving is not None for one in totals):
        sums = advance(info, sums, totals)
    expand_grad, reduce_grad, merge_grad = first.results
    source_grads, patches_grad, middle_grads = second.results
    projections = [
        jnp.concatenate([one.results[i] for one in (third, fourth)], axis=1) for i in range(3)
    ]
    return (
        block_output[None],
        tokens_grad[None],
        patches_grad,
        sums[0],
        sums[1],
        projections[0],
        sums[2],
        projections[1],
        projections[2],
        sums[3],
        middle_grads[:, model_width:],
        sums[4],
        sums[5],
        sums[6],
        middle_grads[:, :model_width],
        sums[7],
        source_grads[:, :model_width],
        source_grads[:, model_width:],
        sums[8],
        merge_grad,
        sums[9],
        sums[10],
        sums[11],
        expand_grad,
        sums[16 : 16 + expand_bias.shape[0] // model_width].reshape(-1),
        reduce_grad,
        sums[12],
    )


def solution(mesh):
    placed = (
        P("patch", "tok", None),
        P(("tok", "patch"), None),
        P("patch", "tok", None),
        P(),
        P(),
        P(),
        P(),
        P(),
        P(),
        P(),
        P(),
        P(),
        P(),
        P(),
        P(),
        P(),
        P(),
        P(),
        P(),
        P(),
        P(),
        P(),
        P(),
        P(),
        P(),
        P(),
        P(),
        P(),
        P(),
        P(),
    )
    return jax.shard_map(
        local,
        mesh=mesh,
        in_specs=placed,
        out_specs=(
            P("patch", "tok", None),
            P("patch", "tok", None),
            P(("tok", "patch"), None),
            P(("tok", "patch")),
            P(("tok", "patch")),
            P(("tok", "patch"), None),
            P(("tok", "patch")),
            P(("tok", "patch"), None),
            P(("tok", "patch"), None),
            P(("tok", "patch")),
            P(("tok", "patch"), None),
            P(("tok", "patch")),
            P(("tok", "patch")),
            P(("tok", "patch")),
            P(("tok", "patch"), None),
            P(("tok", "patch")),
            P(("tok", "patch"), None),
            P(("tok", "patch"), None),
            P(("tok", "patch")),
            P(("tok", "patch"), None),
            P(("tok", "patch")),
            P(("tok", "patch")),
            P(("tok", "patch")),
            P(("tok", "patch"), None),
            P(("tok", "patch")),
            P(("tok", "patch"), None),
            P(("tok", "patch")),
        ),
        check_vma=False,
    )
```

```python
import jax
import jax.numpy as jnp
from jax import lax
from jax.experimental import pallas as pl
from jax.experimental.pallas import tpu as pltpu
from jax.sharding import PartitionSpec as P

HDIM = 64
PAIR = 2 * HDIM
PAGE_SLOTS = 512
NEG_FILL = -1e30
EPS_NORM = 1e-05
LANES = 128
PIECE = 512
HIGH = lax.Precision.HIGHEST
MIB = 1 << 20
bf16, f32 = jnp.bfloat16, jnp.float32
Shape = pltpu.HBM


def nn(left, right):
    return lax.dot_general(
        left, right, (((1,), (0,)), ((), ())), preferred_element_type=f32
    )


def nt(left, right, precision=None):
    return lax.dot_general(
        left, right, (((1,), (1,)), ((), ())), precision=precision, preferred_element_type=f32
    )


def tn(left, right):
    return lax.dot_general(
        left, right, (((0,), (0,)), ((), ())), preferred_element_type=f32
    )


def column_sums(values):
    return jnp.sum(values.astype(f32), axis=0, keepdims=True)


def norm_unit(values):
    average = jnp.mean(values, axis=-1, keepdims=True)
    centred = values - average
    spread = jnp.mean(centred * centred, axis=-1, keepdims=True)
    inverse = lax.rsqrt(spread + EPS_NORM)
    return centred * inverse, inverse


def norm_pull(upstream, unit, inverse, gain):
    scaled = upstream * gain
    centred = scaled - jnp.mean(scaled, axis=-1, keepdims=True)
    centred = centred - unit * jnp.mean(scaled * unit, axis=-1, keepdims=True)
    return centred * inverse


def gelu_pair(values):
    share = 0.5 * (1.0 + lax.erf(values * (2.0**-0.5)))
    slope = share + values * (jnp.exp(-0.5 * values * values) * 0.3989422804014327)
    return values * share, slope


def by_core(core, value, each, fine):
    count, width = value.shape
    split = value.reshape(count // (2 * each), 2, each, width)
    found = []
    for own in range(2):
        one = jnp.where((core == 0) == (own == 0), split[:, 1], split[:, 0])
        one = one.reshape(count // (2 * each), each // fine, fine, width)
        columns = [one[..., at : at + PIECE] for at in range(0, width, PIECE)]
        one = columns[0] if len(columns) == 1 else jnp.concatenate(columns, axis=1)
        found.append(one.astype(bf16))
    return found


def head_lanes(head):
    lane = lax.broadcasted_iota(jnp.int32, (1, PAIR), 1)
    return (lane >= head * HDIM) & (lane < (head + 1) * HDIM)


def only(value, head):
    return jnp.where(head_lanes(head), value, jnp.zeros_like(value))


TINY = pl.CostEstimate(flops=1, bytes_accessed=1, transcendentals=0)


def settings(limit=48):
    return pltpu.CompilerParams(
        dimension_semantics=("arbitrary",), vmem_limit_bytes=limit * MIB
    )


def in_hbm(*values):
    return [pltpu.with_memory_space_constraint(value, pltpu.HBM) for value in values]


def scores_of(key_rows, query, start, mask):
    score = nt(key_rows, query[start:])
    if isinstance(mask, str):
        rows = score.shape[0]
        row = lax.broadcasted_iota(jnp.int32, (rows, rows), 0)
        column = lax.broadcasted_iota(jnp.int32, (rows, rows), 1)
        corner = jnp.where(row <= column, score[:, :rows], NEG_FILL)
        if score.shape[1] == rows:
            return corner
        return jnp.concatenate([corner, score[:, rows:]], axis=1)
    return score if mask is None else score + mask


def from_start(whole, start, part, combine):
    if whole is None:
        return part
    if start == 0:
        return combine(whole, part)
    return jnp.concatenate([whole[:, :start], combine(whole[:, start:], part)], axis=1)


def forward_pair(q_ref, k_ref, v_ref, blocks, begun, out_ref, total_ref):
    values = v_ref[...].T
    outs = []
    for head in range(2):
        lanes = slice(head * HDIM, (head + 1) * HDIM)
        query = only(q_ref[...], head)
        earlier = None if begun is None else begun[1][0, head : head + 1, :]
        row_max, scores = earlier, []
        for first, rows, start, mask in blocks:
            score = scores_of(k_ref[pl.ds(first, rows), :], query, start, mask)
            row_max = from_start(row_max, start, score.max(0, keepdims=True), jnp.maximum)
            scores.append(score)
        total, out = None, None
        if begun is not None:
            total = jnp.exp(earlier - row_max)
            out = begun[0][lanes] * total
        for score, (first, rows, start, _) in zip(scores, blocks):
            exponent = jnp.exp(score - row_max[:, start:])
            total = from_start(total, start, exponent.sum(0, keepdims=True), jnp.add)
            part = nn(values[lanes, first : first + rows], exponent.astype(bf16))
            out = from_start(out, start, part, jnp.add)
        outs.append(out / total)
        total_ref[0, head : head + 1, :] = row_max + jnp.log(total)
    out_ref[...] = jnp.concatenate(outs, axis=0).T.astype(bf16)


def backward_pair(q_ref, k_ref, v_ref, out_ref, total_ref, g_ref, blocks, acc, fresh, dk_ref, dv_ref):
    queries, upstreams, keys = q_ref[...].T, g_ref[...].T, k_ref[...].T
    product = upstreams.astype(f32) * out_ref[...].T.astype(f32)
    for first, rows, start, mask in blocks:
        key_rows, value_rows = k_ref[pl.ds(first, rows), :], v_ref[pl.ds(first, rows), :]
        key_grads, value_grads = [], []
        for head in range(2):
            lanes = slice(head * HDIM, (head + 1) * HDIM)
            inner = product[lanes, start:].sum(0, keepdims=True)
            score = scores_of(key_rows, only(q_ref[...], head), start, mask)
            soft = jnp.exp(score - total_ref[0, head : head + 1, start:])
            grad_soft = nt(value_rows, only(g_ref[...], head)[start:])
            grad_score = (soft * (grad_soft - inner)).astype(bf16)
            value_grads.append(nt(upstreams[lanes, start:], soft.astype(bf16)))
            key_grads.append(nt(queries[lanes, start:], grad_score))
            part = nn(keys[lanes, first : first + rows], grad_score)
            if fresh and first == 0:
                acc[lanes, start:] = part
            else:
                acc[lanes, start:] += part
        dk_ref[pl.ds(first, rows), :] = jnp.concatenate(key_grads, axis=0).T.astype(bf16)
        dv_ref[pl.ds(first, rows), :] = jnp.concatenate(value_grads, axis=0).T.astype(bf16)


def causal_blocks(rows, size=256):
    return [(at, size, at, "causal") for at in range(0, rows, size)]


def totals_shape(rows, width):
    return (width // PAIR, 2, rows)


def own_forward(query, keys, values):
    rows, width = query.shape

    def body(q_ref, k_ref, v_ref, out_ref, total_ref):
        forward_pair(q_ref, k_ref, v_ref, causal_blocks(rows), None, out_ref, total_ref)

    block = pl.BlockSpec((rows, PAIR), lambda p: (0, p))
    total = pl.BlockSpec((1, 2, rows), lambda p: (p, 0, 0))
    return pl.pallas_call(
        body,
        out_shape=(Shape((rows, width), bf16), Shape(totals_shape(rows, width), f32)),
        grid=(width // PAIR,),
        in_specs=[block] * 3,
        out_specs=[block, total],
        cost_estimate=TINY,
        compiler_params=settings(),
        name="own_forward",
    )(*in_hbm(query, keys, values))


def lead_forward(query, keys, values, begun, begun_total, trailing):
    rows, width = query.shape

    def body(flag, q_ref, k_ref, v_ref, begun_ref, old_ref, out_ref, total_ref):
        @pl.when(flag[0] == 1)
        def _():
            begun = (begun_ref[...].T.astype(f32), old_ref)
            blocks = [(0, rows, 0, None)]
            forward_pair(q_ref, k_ref, v_ref, blocks, begun, out_ref, total_ref)

        @pl.when(flag[0] == 0)
        def _():
            out_ref[...] = begun_ref[...]
            total_ref[...] = old_ref[...]

    block = pl.BlockSpec((rows, PAIR), lambda p, flag: (0, p))
    total = pl.BlockSpec((1, 2, rows), lambda p, flag: (p, 0, 0))
    return pl.pallas_call(
        body,
        out_shape=(Shape((rows, width), bf16), Shape(totals_shape(rows, width), f32)),
        grid_spec=pltpu.PrefetchScalarGridSpec(
            num_scalar_prefetch=1,
            grid=(width // PAIR,),
            in_specs=[block] * 4 + [total],
            out_specs=[block, total],
        ),
        cost_estimate=TINY,
        compiler_params=settings(),
        name="lead_forward",
    )(trailing, *in_hbm(query, keys, values, begun, begun_total))


def slot_bias(filled_ref, slots):
    slot = lax.broadcasted_iota(jnp.int32, (slots, 1), 0)
    return jnp.where(slot < filled_ref[0], 0.0, NEG_FILL)


def cross_forward(query, keys, values, filled):
    rows, width = query.shape
    slots = keys.shape[0]

    def body(filled_ref, q_ref, k_ref, v_ref, out_ref, total_ref):
        blocks = [(0, slots, 0, slot_bias(filled_ref, slots))]
        forward_pair(q_ref, k_ref, v_ref, blocks, None, out_ref, total_ref)

    block = pl.BlockSpec((rows, PAIR), lambda p, f: (0, p))
    page = pl.BlockSpec((slots, PAIR), lambda p, f: (0, p))
    total = pl.BlockSpec((1, 2, rows), lambda p, f: (p, 0, 0))
    return pl.pallas_call(
        body,
        out_shape=(Shape((rows, width), bf16), Shape(totals_shape(rows, width), f32)),
        grid_spec=pltpu.PrefetchScalarGridSpec(
            num_scalar_prefetch=1,
            grid=(width // PAIR,),
            in_specs=[block, page, page],
            out_specs=[block, total],
        ),
        cost_estimate=TINY,
        compiler_params=settings(),
        name="cross_forward",
    )(filled, *in_hbm(query, keys, values))


def lead_backward(query, keys, values, out, total, grad, trailing, first, pairs, size=384):
    rows = query.shape[0]

    def body(flag, q_ref, k_ref, v_ref, out_ref, total_ref, g_ref, dq_ref, dk_ref, dv_ref):
        @pl.when(flag[0] == 1)
        def _():
            blocks = [(at, size, 0, None) for at in range(0, rows, size)]
            backward_pair(
                q_ref, k_ref, v_ref, out_ref, total_ref, g_ref, blocks, dq_ref, True, dk_ref, dv_ref
            )

        @pl.when(flag[0] == 0)
        def _():
            for ref in (dq_ref, dk_ref, dv_ref):
                ref[...] = jnp.zeros_like(ref)

    source = pl.BlockSpec((rows, PAIR), lambda p, flag: (0, p + first))
    target = pl.BlockSpec((rows, PAIR), lambda p, flag: (0, p))
    totals = pl.BlockSpec((1, 2, rows), lambda p, flag: (p + first, 0, 0))
    return pl.pallas_call(
        body,
        out_shape=[Shape((pairs * PAIR, rows), f32)] + [Shape((rows, pairs * PAIR), bf16)] * 2,
        grid_spec=pltpu.PrefetchScalarGridSpec(
            num_scalar_prefetch=1,
            grid=(pairs,),
            in_specs=[source] * 4 + [totals, source],
            out_specs=[pl.BlockSpec((PAIR, rows), lambda p, flag: (p, 0)), target, target],
        ),
        cost_estimate=TINY,
        compiler_params=settings(),
        name="lead_backward",
    )(trailing, *in_hbm(query, keys, values, out, total, grad))


def own_backward(query, keys, values, out, total, grad, begun, first, pairs):
    rows = query.shape[0]

    def body(q_ref, k_ref, v_ref, out_ref, total_ref, g_ref, begun_ref, dq_ref, dk_ref, dv_ref, acc):
        acc[...] = begun_ref[...]
        backward_pair(
            q_ref, k_ref, v_ref, out_ref, total_ref, g_ref, causal_blocks(rows), acc, False,
            dk_ref, dv_ref,
        )
        dq_ref[...] = (acc[...] * (HDIM**-0.5)).T.astype(bf16)

    source = pl.BlockSpec((rows, PAIR), lambda p: (0, p + first))
    target = pl.BlockSpec((rows, PAIR), lambda p: (0, p))
    totals = pl.BlockSpec((1, 2, rows), lambda p: (p + first, 0, 0))
    return pl.pallas_call(
        body,
        out_shape=[Shape((rows, pairs * PAIR), bf16)] * 3,
        grid=(pairs,),
        in_specs=[source] * 4 + [totals, source, pl.BlockSpec((PAIR, rows), lambda p: (p, 0))],
        out_specs=[target] * 3,
        scratch_shapes=[pltpu.VMEM((PAIR, rows), f32)],
        cost_estimate=TINY,
        compiler_params=settings(),
        name="own_backward",
    )(*in_hbm(query, keys, values, out, total, grad, begun))


def cross_backward(query, keys, values, out, total, grad, filled, first, pairs):
    rows, slots = query.shape[0], keys.shape[0]

    def body(
        filled_ref, q_ref, k_ref, v_ref, out_ref, total_ref, g_ref, dq_ref, dk_ref, dv_ref, acc
    ):
        blocks = [(0, slots, 0, slot_bias(filled_ref, slots))]
        backward_pair(
            q_ref, k_ref, v_ref, out_ref, total_ref, g_ref, blocks, acc, True, dk_ref, dv_ref
        )
        dq_ref[...] = (acc[...] * (HDIM**-0.5)).T.astype(bf16)

    source = pl.BlockSpec((rows, PAIR), lambda p, f: (0, p + first))
    page = pl.BlockSpec((slots, PAIR), lambda p, f: (0, p + first))
    target = pl.BlockSpec((rows, PAIR), lambda p, f: (0, p))
    page_target = pl.BlockSpec((slots, PAIR), lambda p, f: (0, p))
    totals = pl.BlockSpec((1, 2, rows), lambda p, f: (p + first, 0, 0))
    return pl.pallas_call(
        body,
        out_shape=[Shape((rows, pairs * PAIR), bf16)] + [Shape((slots, pairs * PAIR), bf16)] * 2,
        grid_spec=pltpu.PrefetchScalarGridSpec(
            num_scalar_prefetch=1,
            grid=(pairs,),
            in_specs=[source, page, page, source, totals, source],
            out_specs=[target, page_target, page_target],
            scratch_shapes=[pltpu.VMEM((PAIR, rows), f32)],
        ),
        cost_estimate=TINY,
        compiler_params=settings(),
        name="cross_backward",
    )(filled, *in_hbm(query, keys, values, out, total, grad))


def feed_forward(start_from, mixed, merge, cotangent, vectors, expand, bias, reduce, info, owners, begun):
    rows, width = start_from.shape
    hidden = expand.shape[1]
    block, tall = PIECE, 384
    steps, fine, others = hidden // block // 2, width // owners, owners // 2
    starts = range(0, rows, tall)
    final = begun is not None

    def body(info_ref, *refs):
        from_ref, mixed_ref, merge_ref, cot_ref, vec_ref, we_ref, be_ref, wr_ref = refs[:8]
        refs = refs[8:]
        if final:
            old_refs, refs = refs[:2], refs[2:]
            out_ref, two_ref, cross_ref, ms_ref, mo_ref = refs[:5]
            refs = refs[5:]
        else:
            new_refs, refs = refs[:3], refs[3:]
        rs_ref, ro_ref, es_ref, eo_ref, eb_ref, sums_ref = refs[:6]
        h, h_flip, g, branch, up, act, gp, sems = refs[6:14]
        after = from_ref if final else refs[14]
        step = pl.program_id(0)
        core, place, length = info_ref[0], info_ref[1], info_ref[2]

        def valid(start):
            row = lax.broadcasted_iota(jnp.int32, (tall, 1), 0) + (start + place)
            return (row < length).astype(f32)

        def copy(i):
            inside = (branch, up, after)[i]
            if final:
                return pltpu.make_async_copy(old_refs[i], inside, sems.at[i])
            return pltpu.make_async_copy(inside, new_refs[i], sems.at[i])

        @pl.when(step == 0)
        def _():
            if final:
                copy(0).start()
                copy(1).start()
            total = jnp.zeros((1, width), f32)
            for start in starts:
                at = pl.ds(start, tall)
                x = from_ref[at, :]
                if not final:
                    x = x + nn(mixed_ref[at, :], merge_ref[...]) + vec_ref[0:1, :]
                    after[at, :] = x
                    branch[at, :] = jnp.zeros((tall, width), f32)
                    up[at, :] = jnp.zeros((tall, width), f32)
                unit, _ = norm_unit(x)
                low = (unit * vec_ref[1:2, :] + vec_ref[2:3, :]).astype(bf16)
                h[at, :] = low
                h_flip[:, at] = low.T
                grad = (valid(start) * cot_ref[at, :].astype(f32)).astype(bf16)
                g[at, :] = grad
                total = total + column_sums(grad)
            sums_ref[...] = jnp.zeros_like(sums_ref)
            sums_ref[0:1, :] = total
            if final:
                copy(0).wait()
                copy(1).wait()
            else:
                copy(2).start()

        we, wr = we_ref[...], wr_ref[...]
        for start in starts:
            at = pl.ds(start, tall)
            low, slope = gelu_pair(nn(h[at, :], we) + be_ref[...])
            low = low.astype(bf16)
            act[at, :] = low
            branch[at, :] += nn(low, wr)
            grad = (nt(g[at, :], wr) * slope).astype(bf16)
            gp[at, :] = grad
            up[at, :] += nt(grad, we)
        if not final:
            @pl.when(step == steps - 1)
            def _():
                copy(0).start()
                copy(1).start()

        each = hidden // owners // fine
        for ref, one in zip(
            (rs_ref, ro_ref), by_core(core, tn(act[...], g[...]), hidden // owners, fine)
        ):
            ref[0], ref[1] = one[:, :each], one[:, each:]
        es_ref[...], eo_ref[...] = by_core(core, nn(h_flip[...], gp[...]), fine, fine)
        eb_ref[...] = nn(jnp.ones((8, rows), bf16), gp[...])

        @pl.when(step == steps - 1)
        def _():
            if not final:
                for i in range(3):
                    copy(i).wait()
                return
            gains = jnp.zeros((1, width), f32)
            shifts, merges = gains, gains
            for start in starts:
                at = pl.ds(start, tall)
                x, ok = after[at, :], valid(start)
                out_ref[at, :] = (ok * (x + branch[at, :] + vec_ref[3:4, :])).astype(bf16)
                unit, inverse = norm_unit(x)
                upstream = up[at, :]
                gains = gains + jnp.sum(upstream * unit, axis=0, keepdims=True)
                shifts = shifts + jnp.sum(upstream, axis=0, keepdims=True)
                pulled = norm_pull(upstream, unit, inverse, vec_ref[1:2, :])
                two = ok * cot_ref[at, :].astype(f32) + pulled
                two_ref[at, :] = two
                low = two.astype(bf16)
                g[at, :] = low
                merges = merges + column_sums(low)
                cross_ref[at, :] = nt(low, merge_ref[...]).astype(bf16)
            ms_ref[...], mo_ref[...] = by_core(core, tn(mixed_ref[...], g[...]), fine, fine)
            sums_ref[1:2, :], sums_ref[2:3, :], sums_ref[3:4, :] = gains, shifts, merges

    base = steps if final else 0

    def once(shape):
        return pl.BlockSpec(shape, lambda i, info: (0, 0), pipeline_mode=pl.Buffered(1))

    def fixed(shape):
        return pl.BlockSpec(shape, lambda i, info: (0,) * len(shape))

    each = hidden // owners // fine
    pairs = others // 2 // steps
    by_row = pl.BlockSpec((2, pairs, each, fine, PIECE), lambda i, info: (0, i, 0, 0, 0))
    by_column = pl.BlockSpec((others, 1, fine, PIECE), lambda i, info: (0, i, 0, 0))
    merged = (others, width // PIECE, fine, PIECE)
    hbm = pl.BlockSpec(memory_space=pltpu.HBM)
    full = (rows, width)
    shared_shapes = [
        *[Shape((2, others // 2, each, fine, PIECE), bf16)] * 2,
        *[Shape((others, steps, fine, PIECE), bf16)] * 2,
        Shape((8, hidden // 2), f32), Shape((8, width), f32),
    ]
    shared_specs = [
        by_row, by_row, by_column, by_column,
        pl.BlockSpec((8, block), lambda i, info: (0, i)), fixed((8, width)),
    ]
    if final:
        shapes = [Shape(full, bf16), Shape(full, f32), Shape(full, bf16), Shape(merged, bf16), Shape(merged, bf16)]
        specs = [fixed(full)] * 3 + [fixed(merged)] * 2
    else:
        shapes, specs = [Shape(full, f32)] * 3, [hbm] * 3
    return pl.pallas_call(
        body,
        out_shape=shapes + shared_shapes,
        grid_spec=pltpu.PrefetchScalarGridSpec(
            num_scalar_prefetch=1,
            grid=(steps,),
            in_specs=[
                once(full), once(full), once((width, width)), once(full), once((8, width)),
                pl.BlockSpec((width, block), lambda i, info: (0, base + i)),
                pl.BlockSpec((1, block), lambda i, info: (0, base + i)),
                pl.BlockSpec((block, width), lambda i, info: (base + i, 0)),
            ] + ([hbm] * 2 if final else []),
            out_specs=specs + shared_specs,
            scratch_shapes=[
                pltpu.VMEM(full, bf16), pltpu.VMEM((width, rows), bf16), pltpu.VMEM(full, bf16),
                pltpu.VMEM(full, f32), pltpu.VMEM(full, f32),
                pltpu.VMEM((rows, block), bf16), pltpu.VMEM((rows, block), bf16),
                pltpu.SemaphoreType.DMA((3,)),
            ] + ([] if final else [pltpu.VMEM(full, f32)]),
        ),
        cost_estimate=TINY,
        compiler_params=settings(60),
        name="feed_forward",
    )(
        info, *in_hbm(start_from, mixed, merge, cotangent), vectors,
        *in_hbm(expand), bias, *in_hbm(reduce), *(begun if final else ()),
    )


def streamed(name, body, info, inputs, outs, scratch=()):
    n, m = len(inputs), len(outs)

    def kernel(info_ref, *refs):
        ins, dests = refs[:n], refs[n : n + m]
        held, made = refs[n + m : 2 * n + m], refs[2 * n + m : 2 * n + 2 * m]
        in_sem, out_sem = refs[2 * n + 2 * m : 2 * n + 2 * m + 2]
        rest = refs[2 * n + 2 * m + 2 :]
        loads = [pltpu.make_async_copy(ins[i], held[i], in_sem.at[i]) for i in range(n)]
        for load in loads:
            load.start()
        waited, stores = set(), {}

        def need(i):
            if i not in waited:
                loads[i].wait()
                waited.add(i)
            return held[i]

        def give(i, send=False):
            if send:
                stores[i] = pltpu.make_async_copy(made[i], dests[i], out_sem.at[i])
                stores[i].start()
            return made[i]

        body(info_ref, need, give, *rest)
        for i in range(m):
            stores[i].wait()

    anywhere = pl.BlockSpec(memory_space=pltpu.HBM)
    return pl.pallas_call(
        kernel,
        out_shape=[Shape(shape, kind) for shape, kind in outs],
        grid_spec=pltpu.PrefetchScalarGridSpec(
            num_scalar_prefetch=1,
            grid=(1,),
            in_specs=[anywhere] * n,
            out_specs=[anywhere] * m,
            scratch_shapes=[pltpu.VMEM(value.shape, value.dtype) for value in inputs]
            + [pltpu.VMEM(shape, kind) for shape, kind in outs]
            + [pltpu.SemaphoreType.DMA((n,)), pltpu.SemaphoreType.DMA((m,))]
            + list(scratch),
        ),
        cost_estimate=TINY,
        compiler_params=settings(60),
        name=name,
    )(info, *inputs)


def probe_backward(info, probe_low, probe_high, probe_weight, after_one, two, output_weight, mixed, vectors, owners):
    rows, width = after_one.shape
    half, tall, fine = width // 2, 256, width // owners

    def body(info_ref, need, give, hidden, low_grad):
        core = info_ref[0]
        left, right = need(0), need(1)
        weight = need(2)
        vec = need(7)
        x_ref, two_ref = need(3), need(4)
        gains = jnp.zeros((1, width), f32)
        shifts, outs = gains, gains
        for start in range(0, rows, tall):
            at = pl.ds(start, tall)
            up = nt(left[at, :], weight[:, :half]) + nt(right[at, :], weight[:, half:])
            unit, inverse = norm_unit(x_ref[at, :])
            hidden[at, :] = (unit * vec[0:1, :] + vec[1:2, :]).astype(bf16)
            gains = gains + jnp.sum(up * unit, axis=0, keepdims=True)
            shifts = shifts + jnp.sum(up, axis=0, keepdims=True)
            one = two_ref[at, :] + norm_pull(up, unit, inverse, vec[0:1, :])
            give(0)[at, :] = one
            low = one.astype(bf16)
            low_grad[at, :] = low
            outs = outs + column_sums(low)
            if start == 0:
                need(5)
            give(1)[at, :] = nt(low, need(5)[...]).astype(bf16)
        give(0, True)
        give(1, True)
        sums = give(4)
        sums[...] = jnp.zeros_like(sums)
        sums[0:1, :], sums[1:2, :], sums[2:3, :] = gains, shifts, outs
        sums[3:4, :half] = column_sums(left[...])
        sums[3:4, half:] = column_sums(right[...])
        give(4, True)
        mixed_ref = need(6)
        columns = (
            (0, 1, hidden, left[...]),
            (1, 2, hidden, right[...]),
            (2, 4, mixed_ref, low_grad[...]),
        )
        for begin, end, source, grads in columns:
            pair = by_core(core, tn(source[...], grads), fine, fine)
            give(2)[:, begin:end], give(3)[:, begin:end] = pair
        give(2, True)
        give(3, True)

    return streamed(
        "probe_backward",
        body,
        info,
        [probe_low, probe_high, probe_weight, after_one, two, output_weight, mixed, vectors],
        [
            ((rows, width), f32), ((rows, width), bf16),
            ((owners // 2, 4, fine, PIECE), bf16), ((owners // 2, 4, fine, PIECE), bf16),
            ((8, width), f32),
        ],
        [pltpu.VMEM((rows, width), bf16), pltpu.VMEM((rows, width), bf16)],
    )


def page_backward(
    info, key_low, key_high, value_low, value_high, page_rows, key_weight, value_weight, owners,
    patch_total,
):
    slots, width = page_rows.shape
    half, fine = width // 2, width // owners
    pieces = patch_total // owners // fine * (width // PIECE)

    def body(info_ref, need, give):
        core, page = info_ref[0], info_ref[3]
        kl, kh, vl, vh = need(0)[...], need(1)[...], need(2)[...], need(3)[...]
        rows_ref = need(4)
        for i, grads in enumerate((kl, kh, vl, vh)):
            pair = by_core(core, tn(rows_ref[...], grads), fine, fine)
            give(0)[:, i : i + 1], give(1)[:, i : i + 1] = pair
        wk, wv = need(5), need(6)
        total = nt(kl, wk[:, :half]) + nt(kh, wk[:, half:])
        total = total + nt(vl, wv[:, :half]) + nt(vh, wv[:, half:])
        pair = by_core(core, total, patch_total // owners, fine)
        each = pair[0].shape[0]
        at = pl.ds(pl.multiple_of(page * each, each), each)
        for which in range(2):
            give(which)[:, 4:] = jnp.zeros((owners // 2, pieces, fine, PIECE), bf16)
            give(which)[at, 4:] = pair[which]
            give(which, True)
        sums = give(2)
        sums[...] = jnp.zeros_like(sums)
        sums[0:1, :half] = column_sums(vl)
        sums[0:1, half:] = column_sums(vh)
        give(2, True)

    return streamed(
        "page_backward",
        body,
        info,
        [key_low, key_high, value_low, value_high, page_rows, key_weight, value_weight],
        [
            *[((owners // 2, 4 + pieces, fine, PIECE), bf16)] * 2, ((8, width), f32),
        ],
    )


def lead_upstream(info, keys, values, key_weight, value_weight, lead_tokens, vectors):
    rows, width = lead_tokens.shape
    half, tall = width // 2, 256

    def body(info_ref, need, give, hidden):
        kl, kh, vl, vh = need(0), need(1), need(2), need(3)
        wk, wv = need(4), need(5)
        x_ref, vec = need(6), need(7)
        gains = jnp.zeros((1, width), f32)
        shifts = gains
        for start in range(0, rows, tall):
            at = pl.ds(start, tall)
            up = nt(kl[at, :], wk[:, :half]) + nt(kh[at, :], wk[:, half:])
            up = up + nt(vl[at, :], wv[:, :half]) + nt(vh[at, :], wv[:, half:])
            give(0)[at, :] = up.astype(bf16)
            unit, _ = norm_unit(x_ref[at, :].astype(f32))
            hidden[at, :] = (unit * vec[0:1, :] + vec[1:2, :]).astype(bf16)
            gains = gains + jnp.sum(up * unit, axis=0, keepdims=True)
            shifts = shifts + jnp.sum(up, axis=0, keepdims=True)
        give(0, True)
        sums = give(2)
        sums[...] = jnp.zeros_like(sums)
        sums[0:1, :], sums[1:2, :] = gains, shifts
        sums[2:3, :half], sums[2:3, half:] = column_sums(vl[...]), column_sums(vh[...])
        give(2, True)
        for i, ref in enumerate((kl, kh, vl, vh)):
            give(1)[:, i * half : (i + 1) * half] = tn(hidden[...], ref[...]).astype(bf16)
        give(1, True)

    return streamed(
        "lead_upstream",
        body,
        info,
        [*keys, *values, key_weight, value_weight, lead_tokens, vectors],
        [((rows, width), bf16), ((width, 2 * width), bf16), ((8, width), f32)],
        [pltpu.VMEM((rows, width), bf16)],
    )


def projection_grads(info, hidden, query_grad, key_grad, value_grad, lead_part, high, owners):
    rows, width = hidden.shape
    half, fine = width // 2, width // owners
    column = half if high else 0

    def body(info_ref, need, give):
        core = info_ref[0]
        h = need(0)
        for i in range(3):
            total = tn(h[...], need(1 + i)[...])
            if i:
                base = (i - 1) * width + column
                total = total + need(4)[:, base : base + half].astype(f32)
            pair = by_core(core, total, fine, fine)
            give(0)[:, i : i + 1], give(1)[:, i : i + 1] = pair
        give(0, True)
        give(1, True)

    return streamed(
        "projection_grads",
        body,
        info,
        [hidden, query_grad, key_grad, value_grad, lead_part],
        [((owners // 2, 3, fine, PIECE), bf16)] * 2,
    )


def first_norm_backward(info, queries, keys, values, weights, tokens, one, returned, vectors):
    rows, width = tokens.shape
    half, tall = width // 2, 384

    def body(info_ref, *refs):
        grads = refs[:6]
        wq, wk, wv, x_ref, vec, one_ref, back_ref = refs[6:13]
        out_ref, sums = refs[13:]
        gains = jnp.zeros((1, width), f32)
        shifts = gains
        for start in range(0, rows, tall):
            at = pl.ds(start, tall)
            up = 0.0
            for i, weight in enumerate((wq, wk, wv)):
                up = up + nt(grads[2 * i][at, :], weight[:, :half])
                up = up + nt(grads[2 * i + 1][at, :], weight[:, half:])
            unit, inverse = norm_unit(x_ref[at, :].astype(f32))
            gains = gains + jnp.sum(up * unit, axis=0, keepdims=True)
            shifts = shifts + jnp.sum(up, axis=0, keepdims=True)
            up = up + back_ref[at, :].astype(f32)
            out_ref[at, :] = one_ref[at, :] + norm_pull(up, unit, inverse, vec[0:1, :])
        sums[...] = jnp.zeros_like(sums)
        sums[0:1, :], sums[1:2, :] = gains, shifts
        sums[2:3, :half], sums[2:3, half:] = column_sums(grads[0][...]), column_sums(grads[1][...])
        sums[3:4, :half], sums[3:4, half:] = column_sums(grads[4][...]), column_sums(grads[5][...])

    narrow = pl.BlockSpec((rows, half), lambda i, info: (0, 0))
    wide = pl.BlockSpec((rows, width), lambda i, info: (0, 0))
    whole = pl.BlockSpec((width, width), lambda i, info: (0, 0))
    eight = pl.BlockSpec((8, width), lambda i, info: (0, 0))
    return pl.pallas_call(
        body,
        out_shape=[Shape((rows, width), f32), Shape((8, width), f32)],
        grid_spec=pltpu.PrefetchScalarGridSpec(
            num_scalar_prefetch=1,
            grid=(1,),
            in_specs=[narrow] * 6 + [whole] * 3 + [wide, eight, wide, wide],
            out_specs=[wide, eight],
        ),
        cost_estimate=TINY,
        compiler_params=settings(),
        name="first_norm_backward",
    )(info, *in_hbm(*queries, *keys, *values, *weights, tokens), vectors, *in_hbm(one, returned))


def digit_axes():
    patch_bits = lax.axis_size("patch").bit_length() - 1
    return [("tok", 0)] + [("patch", bit) for bit in reversed(range(patch_bits))]


def my_digit(axis, bit):
    return (lax.axis_index(axis) >> bit) & 1


def tied(*values):
    return lax.optimization_barrier(values)


FIRST_DIGIT = 4


class Part:
    def __init__(self, kept, tok_first, place, start=0, pieces=None):
        self.tok_first, self.place = tok_first, place
        self.pieces = pieces or kept.shape[1]
        self.terms = [(kept, owner_digits(), start)]


def owner_digits():
    return digit_axes()[:-1]


def stages_of(tok_first, direct):
    every = digit_axes()
    bits = every[-2:0:-1]
    loose, last = bits[: max(len(bits) - 2, 0)], bits[max(len(bits) - 2, 0) :]
    singles = [[one] for one in loose]
    ends = [last] if direct else [[one] for one in last]
    return ([every[:1]] + singles if tok_first else singles + [every[:1]]) + ends


class Sum:
    def __init__(self, direct, *sent):
        self.direct = direct
        self.parts = [part for _, parts in sent for part in parts]
        self.at = 0
        self.leaving = [array for array, _ in sent]
        self.hops = [[("patch", 0)]] * len(sent)
        self.groups = [parts for _, parts in sent]
        self.mine = self.came = None

    def send(self):
        self.arrived = [hop(value, steps) for value, steps in zip(self.leaving, self.hops)]

    def free(self, part, at):
        settled = [one for stage in stages_of(part.tok_first, self.direct)[:at] for one in stage]
        return [one for one in owner_digits() if one not in settled]

    def absorb(self, arrived):
        if self.mine is not None:
            self.came = arrived
            self.leaving = None
            return []
        for value, group in zip(arrived, self.groups):
            start = 0
            for part in group:
                part.terms = part.terms + [(value, self.free(part, self.at), start)]
                start += part.pieces
        stages = [stages_of(part.tok_first, self.direct) for part in self.parts]
        last = self.at == len(stages[0]) - 1
        ways = [stage[self.at] for stage in stages]
        self.at += 1
        jobs, self.hops, self.groups = [], [], []
        for digits in [way for i, way in enumerate(ways) if way not in ways[:i]]:
            group = [part for part, way in zip(self.parts, ways) if way == digits]
            free = self.free(group[0], self.at)
            for flips in range(0 if last else 1, 1 << len(digits)):
                flipped = [one for i, one in enumerate(digits) if flips >> i & 1]
                choices = []
                for chunk in range(1 << len(free)):
                    bits = {one: chunk >> (len(free) - 1 - i) & 1 for i, one in enumerate(free)}
                    choices.append((bits, flipped))
                terms = [(part.terms, part.pieces) for part in group]
                jobs.append((terms, choices, bf16 if flips else f32))
                if flips:
                    self.hops.append(flipped)
                    self.groups.append(group)
        return jobs

    def take(self, made):
        if self.at == len(stages_of(True, self.direct)):
            self.mine = made[0]
            made = made[1:]
        self.leaving = list(made)


def hop(value, steps):
    axis = steps[0][0]
    flip = sum(1 << bit for _, bit in steps)
    return lax.ppermute(value, axis, [(i, i ^ flip) for i in range(lax.axis_size(axis))])


def finished(shapes, *totals):
    arrays = [one for total in totals for one in [total.mine, *total.came]]

    def body(*refs):
        refs, outs = list(refs[: len(arrays)]), refs[len(arrays) :]
        for total in totals:
            mine_ref, *came = refs[: 1 + len(total.came)]
            refs = refs[1 + len(total.came) :]
            piece = 0
            for part in total.parts:
                out, at_column = part.place
                fine = mine_ref.shape[2]
                tall = shapes[out][0] // fine
                for p in range(part.pieces):
                    sum_here = mine_ref[0, piece]
                    for ref in came:
                        sum_here = sum_here + ref[0, piece].astype(f32)
                    row, column = p % tall * fine, at_column + p // tall * PIECE
                    outs[out][row : row + fine, column : column + PIECE] = sum_here
                    piece += 1

    return pl.pallas_call(
        body,
        out_shape=[Shape(shape, f32) for shape in shapes],
        cost_estimate=TINY,
        compiler_params=pltpu.CompilerParams(vmem_limit_bytes=40 * MIB),
        name="finished",
    )(*arrays)


def added_up(info, jobs):
    digits = digit_axes()
    arrays, known = [], {}
    for parts, _, _ in jobs:
        for terms, _ in parts:
            for value, _, _ in terms:
                if id(value) not in known:
                    known[id(value)] = len(arrays)
                    arrays.append(value)
    fine = arrays[0].shape[2]
    units = [(job, part) for job in range(len(jobs)) for part in range(len(jobs[job][0]))]
    loads = sum(len(jobs[job][0][part][0]) * len(jobs[job][1]) for job, part in units)

    def body(info_ref, *refs):
        n, m, k = len(arrays), len(jobs), len(units)
        ins, dests = refs[:n], refs[n : n + m]
        held, made = refs[n + m : n + m + k], refs[n + m + k : n + 2 * m + k]
        in_sem, out_sem = refs[n + 2 * m + k :]
        mine = {one: info_ref[FIRST_DIGIT + i] for i, one in enumerate(digits)}
        copies, count = [], 0
        for unit, (job, part) in enumerate(units):
            terms, pieces = jobs[job][0][part]
            copies.append([])
            for t, (value, free, start) in enumerate(terms):
                for c, (bits, flipped) in enumerate(jobs[job][1]):
                    index = 0
                    for one in free:
                        digit = bits[one] if one in bits else mine[one]
                        digit = 1 - digit if one in flipped else digit
                        index = 2 * index + digit
                    copy = pltpu.make_async_copy(
                        ins[known[id(value)]].at[index, pl.ds(start, pieces)],
                        held[unit].at[t, c],
                        in_sem.at[count],
                    )
                    copy.start()
                    copies[-1].append(copy)
                    count += 1
        offsets = [0] * m
        left = [len(jobs[job][0]) for job in range(m)]
        stores = []
        for unit, (job, part) in enumerate(units):
            terms, pieces = jobs[job][0][part]
            for copy in copies[unit]:
                copy.wait()
            offset = offsets[job]

            batch = max(one for one in range(1, 9) if pieces % one == 0)
            per = pieces // batch

            def step(i, _, unit=unit, job=job, count=len(terms), per=per, batch=batch, offset=offset):
                chunk = i // per
                for p in range(batch):
                    piece = i % per * batch + p
                    total = held[unit][0, chunk, piece].astype(f32)
                    for t in range(1, count):
                        total = total + held[unit][t, chunk, piece].astype(f32)
                    made[job][chunk, offset + piece] = total.astype(jobs[job][2])
                return 0

            lax.fori_loop(0, len(jobs[job][1]) * per, step, 0)
            offsets[job] += pieces
            left[job] -= 1
            if not left[job]:
                stores.append(pltpu.make_async_copy(made[job], dests[job], out_sem.at[job]))
                stores[-1].start()
        for store in stores:
            store.wait()

    anywhere = pl.BlockSpec(memory_space=pltpu.HBM)
    shapes = [
        ((len(choices), sum(pieces for _, pieces in parts), fine, PIECE), kind)
        for parts, choices, kind in jobs
    ]
    held = [
        pltpu.VMEM(
            (len(jobs[job][0][part][0]), len(jobs[job][1]), jobs[job][0][part][1], fine, PIECE), bf16
        )
        for job, part in units
    ]
    return pl.pallas_call(
        body,
        out_shape=[Shape(shape, kind) for shape, kind in shapes],
        grid_spec=pltpu.PrefetchScalarGridSpec(
            num_scalar_prefetch=1,
            grid=(1,),
            in_specs=[anywhere] * len(arrays),
            out_specs=[pl.BlockSpec(memory_space=pltpu.HBM)] * len(jobs),
            scratch_shapes=held
            + [pltpu.VMEM(shape, kind) for shape, kind in shapes]
            + [pltpu.SemaphoreType.DMA((loads,)), pltpu.SemaphoreType.DMA((len(jobs),))],
        ),
        cost_estimate=TINY,
        compiler_params=settings(60),
        name="added_up",
    )(info, *arrays)


def advance(info, chain, moving=(), fresh=()):
    moving = [one for one in moving if one.leaving is not None]
    chain, arrived = tied(chain, [one.arrived for one in moving])
    jobs, owners = [], []
    for one, values in zip(moving, arrived):
        new = one.absorb(values)
        owners.append((one, len(new)))
        jobs += new
    if jobs:
        made = added_up(info, jobs)
        for one, count in owners:
            if count:
                one.take(made[:count])
                made = made[count:]
    going = [one for one in moving + list(fresh) if one.leaving is not None]
    chain, leaving = tied(chain, [one.leaving for one in going])
    for one, values in zip(going, leaving):
        one.leaving = values
        one.send()
    return chain


def vector_table(feed, expand_bias, probe, page, lead, first):
    width = feed.shape[1]

    def body(feed_ref, bias_ref, probe_ref, page_ref, lead_ref, first_ref, out):
        rows = [
            first_ref[0:1, :] + lead_ref[0:1, :],
            first_ref[1:2, :] + lead_ref[1:2, :],
            first_ref[2:3, :],
            first_ref[3:4, :] + lead_ref[2:3, :],
            probe_ref[2:3, :],
            probe_ref[0:1, :],
            probe_ref[1:2, :],
            probe_ref[3:4, :],
            page_ref[0:1, :],
            feed_ref[3:4, :],
            feed_ref[1:2, :],
            feed_ref[2:3, :],
            feed_ref[0:1, :],
        ]
        out[...] = jnp.zeros_like(out)
        for i, row in enumerate(rows):
            out[i : i + 1, :] = row
        out[16 : 16 + bias_ref.shape[0], :] = bias_ref[...]

    return pl.pallas_call(
        body,
        out_shape=jax.ShapeDtypeStruct((24, width), f32),
        cost_estimate=TINY,
        name="vector_table",
    )(feed, expand_bias, probe, page, lead, first)


def scatter_rows(table, width, first, last):
    digits = digit_axes()
    fine = width >> len(digits)
    for axis, bit in digits[first:last]:
        half = table.shape[1] // 2
        if half % LANES:
            table = table + hop(table, [(axis, bit)])
        else:
            digit = my_digit(axis, bit)
            keep = lax.dynamic_slice_in_dim(table, digit * half, half, 1)
            give = lax.dynamic_slice_in_dim(table, (1 - digit) * half, half, 1)
            table = keep + hop(give, [(axis, bit)])
    if last < len(digits):
        return table
    inside = 0
    for axis, bit in digits[(table.shape[1] // fine).bit_length() * -1 + 1 :]:
        inside = 2 * inside + my_digit(axis, bit)
    return lax.dynamic_slice_in_dim(table, inside * fine, fine, 1)


def pick_entry(table, position):
    indices = jnp.arange(table.shape[0], dtype=jnp.int32)
    return jnp.sum(jnp.where(indices == position, table, 0))


def layer_norm(values, gain, shift):
    unit, _ = norm_unit(values)
    return (unit * gain + shift).astype(bf16)


def rows_of(*vectors):
    rows = jnp.stack(vectors, axis=0)
    return jnp.pad(rows, ((0, 8 - len(vectors)), (0, 0)))


def local(
    tokens,
    patches,
    cotangent,
    lengths,
    page_of,
    page_counts,
    self_gain,
    self_shift,
    query_weight,
    query_bias,
    key_weight,
    value_weight,
    value_bias,
    output_weight,
    output_bias,
    cross_gain,
    cross_shift,
    probe_weight,
    probe_bias,
    source_key,
    source_value,
    source_bias,
    merge_weight,
    merge_bias,
    feed_gain,
    feed_shift,
    expand_weight,
    expand_bias,
    reduce_weight,
    reduce_bias,
):
    head_scale = HDIM ** (-0.5)
    tok_index = lax.axis_index("tok").astype(jnp.int32)
    sequence = lax.axis_index("patch")
    core = my_digit("patch", 0).astype(jnp.int32)
    row_count, model_width = tokens.shape[1:]
    lead_tokens = lax.ppermute(tokens[0], "tok", [(0, 1)])
    gathered = lax.all_gather(patches, ("tok", "patch"), axis=0, tiled=True)
    inputs = tokens[0].astype(f32)
    page_index = pick_entry(page_of, sequence)
    filled = pick_entry(page_counts, page_index).reshape(1)
    trailing = tok_index.reshape(1)
    page_start = page_index * PAGE_SLOTS
    digits = [my_digit(*one).astype(jnp.int32) for one in digit_axes()]
    owners = 1 << len(digits)
    info = jnp.stack(
        [core, tok_index * row_count, pick_entry(lengths, sequence), page_index] + digits
    )
    self_vectors = rows_of(self_gain, self_shift)
    cross_vectors = rows_of(cross_gain, cross_shift)
    feed_vectors = rows_of(merge_bias, feed_gain, feed_shift, reduce_bias)

    hidden_one = layer_norm(inputs, self_gain, self_shift)
    query = ((nn(hidden_one, query_weight) + query_bias) * head_scale).astype(bf16)
    own_keys = nn(hidden_one, key_weight).astype(bf16)
    own_values = (nn(hidden_one, value_weight) + value_bias).astype(bf16)
    own_mixed, own_total = own_forward(query, own_keys, own_values)
    lead_tokens, own_mixed = tied(lead_tokens, own_mixed)
    hidden_lead = layer_norm(lead_tokens.astype(f32), self_gain, self_shift)
    lead_keys = nn(hidden_lead, key_weight).astype(bf16)
    lead_values = (nn(hidden_lead, value_weight) + value_bias).astype(bf16)
    self_mixed, self_total = lead_forward(
        query, lead_keys, lead_values, own_mixed, own_total, trailing
    )
    after_one = inputs + nn(self_mixed, output_weight) + output_bias
    hidden_two = layer_norm(after_one, cross_gain, cross_shift)
    probe = ((nn(hidden_two, probe_weight) + probe_bias) * head_scale).astype(bf16)
    page_rows = lax.dynamic_slice_in_dim(gathered, page_start, PAGE_SLOTS, 0)
    page_keys = nn(page_rows, source_key).astype(bf16)
    page_values = (nn(page_rows, source_value) + source_bias).astype(bf16)
    cross_mixed, cross_total = cross_forward(probe, page_keys, page_values, filled)

    feed_args = (
        cross_mixed, merge_weight, cotangent[0], feed_vectors, expand_weight, expand_bias[None],
        reduce_weight, info, owners,
    )
    branch, upstream, after_two, *fed = feed_forward(after_one, *feed_args, None)
    fine = model_width // owners
    deep = expand_weight.shape[1] // 2

    def by_owner(value):
        return value.reshape((-1,) + value.shape[2:])

    first = Sum(
        False,
        (fed[2], [Part(fed[3], True, (0, 0))]),
        (by_owner(fed[0]), [Part(by_owner(fed[1]), False, (1, 0))]),
    )
    low_bias, low_sums = fed[4:]
    after_two, branch, upstream = advance(info, (after_two, branch, upstream), [], [first])
    block_output, grad_two, grad_cross_out, *fed = feed_forward(
        after_two, *feed_args, (branch, upstream)
    )
    second = Sum(
        False,
        (fed[4], [Part(fed[5], True, (0, deep))]),
        (by_owner(fed[2]), [Part(by_owner(fed[3]), False, (2, 0))]),
        (fed[0], [Part(fed[1], False, (3, 0))]),
    )
    expand_bias_sums = jnp.concatenate([low_bias[0], fed[6][0]])
    feed_sums = fed[7]

    half_pairs = model_width // PAIR // 2
    cross_args = (probe, page_keys, page_values, cross_mixed, cross_total)
    grad_cross_out = advance(info, grad_cross_out, [first], [second])
    low = cross_backward(*cross_args, grad_cross_out, filled, 0, half_pairs)
    low, grad_cross_out = advance(info, (low, grad_cross_out), [first, second])
    high = cross_backward(*cross_args, grad_cross_out, filled, half_pairs, half_pairs)
    patch_total = patches.shape[0] * lax.axis_size(("tok", "patch"))
    paged = page_backward(
        info, low[1], high[1], low[2], high[2], page_rows, source_key, source_value, owners,
        patch_total,
    )
    probed = probe_backward(
        info, low[0], high[0], probe_weight, after_one, grad_two, output_weight, self_mixed,
        cross_vectors, owners,
    )
    grad_one, grad_self_out, probe_sums = probed[0], probed[1], probed[4]
    third = Sum(
        False,
        (
            paged[0],
            [Part(paged[1], True, (0, 0), 0, 4), Part(paged[1], False, (1, 0), 4, paged[1].shape[1] - 4)],
        ),
        (probed[2], [Part(probed[3], False, (2, 0))]),
    )
    self_args = (query, lead_keys, lead_values, self_mixed, self_total)
    own_args = (query, own_keys, own_values, self_mixed, self_total)
    grad_self_out = advance(info, grad_self_out, [first, second], [third])
    lead_low = lead_backward(*self_args, grad_self_out, trailing, 0, half_pairs)
    lead_low, grad_self_out = advance(info, (lead_low, grad_self_out), [first, second, third])
    lead_high = lead_backward(*self_args, grad_self_out, trailing, half_pairs, half_pairs)
    led_grad, led_part, lead_sums = lead_upstream(
        info, (lead_low[1], lead_high[1]), (lead_low[2], lead_high[2]), key_weight,
        value_weight, lead_tokens, self_vectors,
    )
    led_grad, led_part, grad_self_out = advance(
        info, (led_grad, led_part, grad_self_out), [first, second, third]
    )
    returned = lax.ppermute(led_grad, "tok", [(1, 0)])
    own_low = own_backward(*own_args, grad_self_out, lead_low[0], 0, half_pairs)
    own_low, grad_self_out = advance(info, (own_low, grad_self_out), [second, third])
    parts = projection_grads(info, hidden_one, *own_low, led_part, False, owners)
    half = model_width // 2
    fourth = Sum(True, (parts[0], [Part(parts[1], i == 1, (i, 0), i, 1) for i in range(3)]))
    own_low, grad_self_out = advance(info, (own_low, grad_self_out), [], [fourth])
    own_high = own_backward(*own_args, grad_self_out, lead_high[0], half_pairs, half_pairs)
    own_low, own_high, returned = advance(
        info, (own_low, own_high, returned), [third, fourth]
    )
    tokens_grad, first_sums = first_norm_backward(
        info, (own_low[0], own_high[0]), (own_low[1], own_high[1]), (own_low[2], own_high[2]),
        (query_weight, key_weight, value_weight), tokens[0], grad_one, returned, self_vectors,
    )
    first_sums, own_high, led_part = advance(
        info, (first_sums, own_high, led_part), [third, fourth]
    )
    parts = projection_grads(info, hidden_one, *own_high, led_part, True, owners)
    bias_rows = expand_bias_sums.reshape(owners, -1, fine)
    bias_rows = jnp.transpose(bias_rows, (1, 0, 2)).reshape(-1, model_width)
    table = vector_table(feed_sums, bias_rows, probe_sums, paged[2], lead_sums, first_sums)
    table = scatter_rows(table, model_width, 0, 1)
    fifth = Sum(True, (parts[0], [Part(parts[1], i != 1, (i, half), i, 1) for i in range(3)]))
    table = advance(info, table, [fourth], [fifth])
    table = scatter_rows(table, model_width, 1, 3)
    table = advance(info, table, [fourth, fifth])
    sums = scatter_rows(table, model_width, 3, len(digits))
    totals = [first, second, third, fourth, fifth]
    while any(one.leaving is not None for one in totals):
        sums = advance(info, sums, totals)
    tall = expand_weight.shape[1] // owners
    model, half_reduce = (fine, model_width), (tall, half)
    expand_grad, reduce_low, reduce_high, merge_grad = finished(
        [(fine, expand_weight.shape[1]), half_reduce, half_reduce, model], first, second
    )
    is_first = tok_index == 0
    given = jnp.where(is_first, reduce_high, reduce_low).astype(bf16)
    taken = hop(given, [("tok", 0)]).astype(f32)
    reduce_grad = jnp.concatenate(
        [jnp.where(is_first, reduce_low, taken), jnp.where(is_first, taken, reduce_high)], axis=1
    )
    source_grads, patches_grad, middle_grads = finished(
        [(fine, 2 * model_width), (patches.shape[0], model_width), (fine, 2 * model_width)], third
    )
    projections = finished([model] * 3, fourth, fifth)
    return (
        block_output[None],
        tokens_grad[None],
        patches_grad,
        sums[0],
        sums[1],
        projections[0],
        sums[2],
        projections[1],
        projections[2],
        sums[3],
        middle_grads[:, model_width:],
        sums[4],
        sums[5],
        sums[6],
        middle_grads[:, :model_width],
        sums[7],
        source_grads[:, :model_width],
        source_grads[:, model_width:],
        sums[8],
        merge_grad,
        sums[9],
        sums[10],
        sums[11],
        expand_grad,
        sums[16 : 16 + expand_bias.shape[0] // model_width].reshape(-1),
        reduce_grad,
        sums[12],
    )


def solution(mesh):
    placed = (
        P("patch", "tok", None),
        P(("tok", "patch"), None),
        P("patch", "tok", None),
        P(),
        P(),
        P(),
        P(),
        P(),
        P(),
        P(),
        P(),
        P(),
        P(),
        P(),
        P(),
        P(),
        P(),
        P(),
        P(),
        P(),
        P(),
        P(),
        P(),
        P(),
        P(),
        P(),
        P(),
        P(),
        P(),
        P(),
    )
    return jax.shard_map(
        local,
        mesh=mesh,
        in_specs=placed,
        out_specs=(
            P("patch", "tok", None),
            P("patch", "tok", None),
            P(("tok", "patch"), None),
            P(("tok", "patch")),
            P(("tok", "patch")),
            P(("tok", "patch"), None),
            P(("tok", "patch")),
            P(("tok", "patch"), None),
            P(("tok", "patch"), None),
            P(("tok", "patch")),
            P(("tok", "patch"), None),
            P(("tok", "patch")),
            P(("tok", "patch")),
            P(("tok", "patch")),
            P(("tok", "patch"), None),
            P(("tok", "patch")),
            P(("tok", "patch"), None),
            P(("tok", "patch"), None),
            P(("tok", "patch")),
            P(("tok", "patch"), None),
            P(("tok", "patch")),
            P(("tok", "patch")),
            P(("tok", "patch")),
            P(("tok", "patch"), None),
            P(("tok", "patch")),
            P(("tok", "patch"), None),
            P(("tok", "patch")),
        ),
        check_vma=False,
    )
```

```python
import jax
import jax.numpy as jnp
from jax import lax
from jax.experimental import pallas as pl
from jax.experimental.pallas import tpu as pltpu
from jax.sharding import PartitionSpec as P

HDIM = 64
PAIR = 2 * HDIM
PAGE_SLOTS = 512
NEG_FILL = -1e30
EPS_NORM = 1e-05
LANES = 128
PIECE = 512
HIGH = lax.Precision.HIGHEST
MIB = 1 << 20
bf16, f32 = jnp.bfloat16, jnp.float32
Shape = pltpu.HBM


def nn(left, right):
    return lax.dot_general(
        left, right, (((1,), (0,)), ((), ())), preferred_element_type=f32
    )


def nt(left, right, precision=None):
    return lax.dot_general(
        left, right, (((1,), (1,)), ((), ())), precision=precision, preferred_element_type=f32
    )


def tn(left, right):
    return lax.dot_general(
        left, right, (((0,), (0,)), ((), ())), preferred_element_type=f32
    )


def column_sums(values):
    return jnp.sum(values.astype(f32), axis=0, keepdims=True)


def norm_unit(values):
    average = jnp.mean(values, axis=-1, keepdims=True)
    centred = values - average
    spread = jnp.mean(centred * centred, axis=-1, keepdims=True)
    inverse = lax.rsqrt(spread + EPS_NORM)
    return centred * inverse, inverse


def norm_pull(upstream, unit, inverse, gain):
    scaled = upstream * gain
    centred = scaled - jnp.mean(scaled, axis=-1, keepdims=True)
    centred = centred - unit * jnp.mean(scaled * unit, axis=-1, keepdims=True)
    return centred * inverse


def gelu_pair(values):
    share = 0.5 * (1.0 + lax.erf(values * (2.0**-0.5)))
    slope = share + values * (jnp.exp(-0.5 * values * values) * 0.3989422804014327)
    return values * share, slope


def by_core(core, value, each, fine):
    count, width = value.shape
    split = value.reshape(count // (2 * each), 2, each, width)
    found = []
    for own in range(2):
        one = jnp.where((core == 0) == (own == 0), split[:, 1], split[:, 0])
        one = one.reshape(count // (2 * each), each // fine, fine, width)
        columns = [one[..., at : at + PIECE] for at in range(0, width, PIECE)]
        one = columns[0] if len(columns) == 1 else jnp.concatenate(columns, axis=1)
        found.append(one.astype(bf16))
    return found


def head_lanes(head):
    lane = lax.broadcasted_iota(jnp.int32, (1, PAIR), 1)
    return (lane >= head * HDIM) & (lane < (head + 1) * HDIM)


def only(value, head):
    return jnp.where(head_lanes(head), value, jnp.zeros_like(value))


TINY = pl.CostEstimate(flops=1, bytes_accessed=1, transcendentals=0)


def settings(limit=48):
    return pltpu.CompilerParams(
        dimension_semantics=("arbitrary",), vmem_limit_bytes=limit * MIB
    )


def in_hbm(*values):
    return [pltpu.with_memory_space_constraint(value, pltpu.HBM) for value in values]


def scores_of(key_rows, query, start, mask):
    score = nt(key_rows, query[start:])
    if isinstance(mask, str):
        rows = score.shape[0]
        row = lax.broadcasted_iota(jnp.int32, (rows, rows), 0)
        column = lax.broadcasted_iota(jnp.int32, (rows, rows), 1)
        corner = jnp.where(row <= column, score[:, :rows], NEG_FILL)
        if score.shape[1] == rows:
            return corner
        return jnp.concatenate([corner, score[:, rows:]], axis=1)
    return score if mask is None else score + mask


def from_start(whole, start, part, combine):
    if whole is None:
        return part
    if start == 0:
        return combine(whole, part)
    return jnp.concatenate([whole[:, :start], combine(whole[:, start:], part)], axis=1)


def forward_pair(q_ref, k_ref, v_ref, blocks, begun, out_ref, total_ref):
    values = v_ref[...].T
    outs = []
    for head in range(2):
        lanes = slice(head * HDIM, (head + 1) * HDIM)
        query = only(q_ref[...], head)
        earlier = None if begun is None else begun[1][0, head : head + 1, :]
        row_max, scores = None, []
        for first, rows, start, mask in blocks:
            score = scores_of(k_ref[pl.ds(first, rows), :], query, start, mask)
            row_max = from_start(row_max, start, score.max(0, keepdims=True), jnp.maximum)
            scores.append(score)
        if begun is not None:
            row_max = jnp.maximum(row_max, earlier)
        total, out = None, None
        for score, (first, rows, start, _) in zip(scores, blocks):
            exponent = jnp.exp(score - row_max[:, start:])
            total = from_start(total, start, exponent.sum(0, keepdims=True), jnp.add)
            part = nn(values[lanes, first : first + rows], exponent.astype(bf16))
            out = from_start(out, start, part, jnp.add)
        if begun is not None:
            share = jnp.exp(earlier - row_max)
            total = total + share
            out = out + begun[0][lanes] * share
        outs.append(out / total)
        total_ref[0, head : head + 1, :] = row_max + jnp.log(total)
    out_ref[...] = jnp.concatenate(outs, axis=0).T.astype(bf16)


def backward_pair(q_ref, k_ref, v_ref, out_ref, total_ref, g_ref, blocks, acc, fresh, dk_ref, dv_ref):
    queries, upstreams, keys = q_ref[...].T, g_ref[...].T, k_ref[...].T
    product = upstreams.astype(f32) * out_ref[...].T.astype(f32)
    for first, rows, start, mask in blocks:
        key_rows, value_rows = k_ref[pl.ds(first, rows), :], v_ref[pl.ds(first, rows), :]
        key_grads, value_grads = [], []
        for head in range(2):
            lanes = slice(head * HDIM, (head + 1) * HDIM)
            inner = product[lanes, start:].sum(0, keepdims=True)
            score = scores_of(key_rows, only(q_ref[...], head), start, mask)
            soft = jnp.exp(score - total_ref[0, head : head + 1, start:])
            grad_soft = nt(value_rows, only(g_ref[...], head)[start:])
            grad_score = (soft * (grad_soft - inner)).astype(bf16)
            value_grads.append(nt(upstreams[lanes, start:], soft.astype(bf16)))
            key_grads.append(nt(queries[lanes, start:], grad_score))
            part = nn(keys[lanes, first : first + rows], grad_score)
            if fresh and first == 0:
                acc[lanes, start:] = part
            else:
                acc[lanes, start:] += part
        dk_ref[pl.ds(first, rows), :] = jnp.concatenate(key_grads, axis=0).T.astype(bf16)
        dv_ref[pl.ds(first, rows), :] = jnp.concatenate(value_grads, axis=0).T.astype(bf16)


def causal_blocks(rows, size=256):
    return [(at, size, at, "causal") for at in range(0, rows, size)]


def totals_shape(rows, width):
    return (width // PAIR, 2, rows)


def own_forward(query, keys, values):
    rows, width = query.shape

    def body(q_ref, k_ref, v_ref, out_ref, total_ref):
        forward_pair(q_ref, k_ref, v_ref, causal_blocks(rows), None, out_ref, total_ref)

    block = pl.BlockSpec((rows, PAIR), lambda p: (0, p))
    total = pl.BlockSpec((1, 2, rows), lambda p: (p, 0, 0))
    return pl.pallas_call(
        body,
        out_shape=(Shape((rows, width), bf16), Shape(totals_shape(rows, width), f32)),
        grid=(width // PAIR,),
        in_specs=[block] * 3,
        out_specs=[block, total],
        cost_estimate=TINY,
        compiler_params=settings(),
        name="own_forward",
    )(*in_hbm(query, keys, values))


def lead_forward(query, keys, values, begun, begun_total, trailing):
    rows, width = query.shape

    def body(flag, q_ref, k_ref, v_ref, begun_ref, old_ref, out_ref, total_ref):
        @pl.when(flag[0] == 1)
        def _():
            begun = (begun_ref[...].T.astype(f32), old_ref)
            blocks = [(0, rows, 0, None)]
            forward_pair(q_ref, k_ref, v_ref, blocks, begun, out_ref, total_ref)

        @pl.when(flag[0] == 0)
        def _():
            out_ref[...] = begun_ref[...]
            total_ref[...] = old_ref[...]

    block = pl.BlockSpec((rows, PAIR), lambda p, flag: (0, p))
    total = pl.BlockSpec((1, 2, rows), lambda p, flag: (p, 0, 0))
    return pl.pallas_call(
        body,
        out_shape=(Shape((rows, width), bf16), Shape(totals_shape(rows, width), f32)),
        grid_spec=pltpu.PrefetchScalarGridSpec(
            num_scalar_prefetch=1,
            grid=(width // PAIR,),
            in_specs=[block] * 4 + [total],
            out_specs=[block, total],
        ),
        cost_estimate=TINY,
        compiler_params=settings(),
        name="lead_forward",
    )(trailing, *in_hbm(query, keys, values, begun, begun_total))


def slot_bias(filled_ref, slots):
    slot = lax.broadcasted_iota(jnp.int32, (slots, 1), 0)
    return jnp.where(slot < filled_ref[0], 0.0, NEG_FILL)


def cross_forward(query, keys, values, filled):
    rows, width = query.shape
    slots = keys.shape[0]

    def body(filled_ref, q_ref, k_ref, v_ref, out_ref, total_ref):
        blocks = [(0, slots, 0, slot_bias(filled_ref, slots))]
        forward_pair(q_ref, k_ref, v_ref, blocks, None, out_ref, total_ref)

    block = pl.BlockSpec((rows, PAIR), lambda p, f: (0, p))
    page = pl.BlockSpec((slots, PAIR), lambda p, f: (0, p))
    total = pl.BlockSpec((1, 2, rows), lambda p, f: (p, 0, 0))
    return pl.pallas_call(
        body,
        out_shape=(Shape((rows, width), bf16), Shape(totals_shape(rows, width), f32)),
        grid_spec=pltpu.PrefetchScalarGridSpec(
            num_scalar_prefetch=1,
            grid=(width // PAIR,),
            in_specs=[block, page, page],
            out_specs=[block, total],
        ),
        cost_estimate=TINY,
        compiler_params=settings(),
        name="cross_forward",
    )(filled, *in_hbm(query, keys, values))


def lead_backward(query, keys, values, out, total, grad, trailing, first, pairs, size=384):
    rows = query.shape[0]

    def body(flag, q_ref, k_ref, v_ref, out_ref, total_ref, g_ref, dq_ref, dk_ref, dv_ref):
        @pl.when(flag[0] == 1)
        def _():
            blocks = [(at, size, 0, None) for at in range(0, rows, size)]
            backward_pair(
                q_ref, k_ref, v_ref, out_ref, total_ref, g_ref, blocks, dq_ref, True, dk_ref, dv_ref
            )

        @pl.when(flag[0] == 0)
        def _():
            for ref in (dq_ref, dk_ref, dv_ref):
                ref[...] = jnp.zeros_like(ref)

    source = pl.BlockSpec((rows, PAIR), lambda p, flag: (0, p + first))
    target = pl.BlockSpec((rows, PAIR), lambda p, flag: (0, p))
    totals = pl.BlockSpec((1, 2, rows), lambda p, flag: (p + first, 0, 0))
    return pl.pallas_call(
        body,
        out_shape=[Shape((pairs * PAIR, rows), f32)] + [Shape((rows, pairs * PAIR), bf16)] * 2,
        grid_spec=pltpu.PrefetchScalarGridSpec(
            num_scalar_prefetch=1,
            grid=(pairs,),
            in_specs=[source] * 4 + [totals, source],
            out_specs=[pl.BlockSpec((PAIR, rows), lambda p, flag: (p, 0)), target, target],
        ),
        cost_estimate=TINY,
        compiler_params=settings(),
        name="lead_backward",
    )(trailing, *in_hbm(query, keys, values, out, total, grad))


def own_backward(query, keys, values, out, total, grad, begun, first, pairs):
    rows = query.shape[0]

    def body(q_ref, k_ref, v_ref, out_ref, total_ref, g_ref, begun_ref, dq_ref, dk_ref, dv_ref, acc):
        acc[...] = begun_ref[...]
        backward_pair(
            q_ref, k_ref, v_ref, out_ref, total_ref, g_ref, causal_blocks(rows), acc, False,
            dk_ref, dv_ref,
        )
        dq_ref[...] = (acc[...] * (HDIM**-0.5)).T.astype(bf16)

    source = pl.BlockSpec((rows, PAIR), lambda p: (0, p + first))
    target = pl.BlockSpec((rows, PAIR), lambda p: (0, p))
    totals = pl.BlockSpec((1, 2, rows), lambda p: (p + first, 0, 0))
    return pl.pallas_call(
        body,
        out_shape=[Shape((rows, pairs * PAIR), bf16)] * 3,
        grid=(pairs,),
        in_specs=[source] * 4 + [totals, source, pl.BlockSpec((PAIR, rows), lambda p: (p, 0))],
        out_specs=[target] * 3,
        scratch_shapes=[pltpu.VMEM((PAIR, rows), f32)],
        cost_estimate=TINY,
        compiler_params=settings(),
        name="own_backward",
    )(*in_hbm(query, keys, values, out, total, grad, begun))


def cross_backward(query, keys, values, out, total, grad, filled, first, pairs):
    rows, slots = query.shape[0], keys.shape[0]

    def body(
        filled_ref, q_ref, k_ref, v_ref, out_ref, total_ref, g_ref, dq_ref, dk_ref, dv_ref, acc
    ):
        blocks = [(0, slots, 0, slot_bias(filled_ref, slots))]
        backward_pair(
            q_ref, k_ref, v_ref, out_ref, total_ref, g_ref, blocks, acc, True, dk_ref, dv_ref
        )
        dq_ref[...] = (acc[...] * (HDIM**-0.5)).T.astype(bf16)

    source = pl.BlockSpec((rows, PAIR), lambda p, f: (0, p + first))
    page = pl.BlockSpec((slots, PAIR), lambda p, f: (0, p + first))
    target = pl.BlockSpec((rows, PAIR), lambda p, f: (0, p))
    page_target = pl.BlockSpec((slots, PAIR), lambda p, f: (0, p))
    totals = pl.BlockSpec((1, 2, rows), lambda p, f: (p + first, 0, 0))
    return pl.pallas_call(
        body,
        out_shape=[Shape((rows, pairs * PAIR), bf16)] + [Shape((slots, pairs * PAIR), bf16)] * 2,
        grid_spec=pltpu.PrefetchScalarGridSpec(
            num_scalar_prefetch=1,
            grid=(pairs,),
            in_specs=[source, page, page, source, totals, source],
            out_specs=[target, page_target, page_target],
            scratch_shapes=[pltpu.VMEM((PAIR, rows), f32)],
        ),
        cost_estimate=TINY,
        compiler_params=settings(),
        name="cross_backward",
    )(filled, *in_hbm(query, keys, values, out, total, grad))


def feed_forward(start_from, mixed, merge, cotangent, vectors, expand, bias, reduce, info, owners, begun):
    rows, width = start_from.shape
    hidden = expand.shape[1]
    block, tall = PIECE, 384
    steps, fine, others = hidden // block // 2, width // owners, owners // 2
    starts = range(0, rows, tall)
    final = begun is not None

    def body(info_ref, *refs):
        from_ref, mixed_ref, merge_ref, cot_ref, vec_ref, we_ref, be_ref, wr_ref = refs[:8]
        refs = refs[8:]
        if final:
            old_refs, refs = refs[:2], refs[2:]
            out_ref, two_ref, cross_ref, ms_ref, mo_ref = refs[:5]
            refs = refs[5:]
        else:
            new_refs, refs = refs[:3], refs[3:]
        rs_ref, ro_ref, es_ref, eo_ref, eb_ref, sums_ref = refs[:6]
        h, h_flip, g, branch, up, act, gp, sems = refs[6:14]
        after = from_ref if final else refs[14]
        step = pl.program_id(0)
        core, place, length = info_ref[0], info_ref[1], info_ref[2]

        def valid(start):
            row = lax.broadcasted_iota(jnp.int32, (tall, 1), 0) + (start + place)
            return (row < length).astype(f32)

        def copy(i):
            inside = (branch, up, after)[i]
            if final:
                return pltpu.make_async_copy(old_refs[i], inside, sems.at[i])
            return pltpu.make_async_copy(inside, new_refs[i], sems.at[i])

        @pl.when(step == 0)
        def _():
            if final:
                copy(0).start()
                copy(1).start()
            total = jnp.zeros((1, width), f32)
            for start in starts:
                at = pl.ds(start, tall)
                x = from_ref[at, :]
                if not final:
                    x = x + nn(mixed_ref[at, :], merge_ref[...]) + vec_ref[0:1, :]
                    after[at, :] = x
                    branch[at, :] = jnp.zeros((tall, width), f32)
                    up[at, :] = jnp.zeros((tall, width), f32)
                unit, _ = norm_unit(x)
                low = (unit * vec_ref[1:2, :] + vec_ref[2:3, :]).astype(bf16)
                h[at, :] = low
                h_flip[:, at] = low.T
                grad = (valid(start) * cot_ref[at, :].astype(f32)).astype(bf16)
                g[at, :] = grad
                total = total + column_sums(grad)
            sums_ref[...] = jnp.zeros_like(sums_ref)
            sums_ref[0:1, :] = total
            if final:
                copy(0).wait()
                copy(1).wait()
            else:
                copy(2).start()

        we, wr = we_ref[...], wr_ref[...]
        for start in starts:
            at = pl.ds(start, tall)
            low, slope = gelu_pair(nn(h[at, :], we) + be_ref[...])
            low = low.astype(bf16)
            act[at, :] = low
            branch[at, :] += nn(low, wr)
            grad = (nt(g[at, :], wr) * slope).astype(bf16)
            gp[at, :] = grad
            up[at, :] += nt(grad, we)
        if not final:
            @pl.when(step == steps - 1)
            def _():
                copy(0).start()
                copy(1).start()

        each = hidden // owners // fine
        for ref, one in zip(
            (rs_ref, ro_ref), by_core(core, tn(act[...], g[...]), hidden // owners, fine)
        ):
            ref[0], ref[1] = one[:, :each], one[:, each:]
        es_ref[...], eo_ref[...] = by_core(core, nn(h_flip[...], gp[...]), fine, fine)
        eb_ref[...] = nn(jnp.ones((8, rows), bf16), gp[...])

        @pl.when(step == steps - 1)
        def _():
            if not final:
                for i in range(3):
                    copy(i).wait()
                return
            gains = jnp.zeros((1, width), f32)
            shifts, merges = gains, gains
            for start in starts:
                at = pl.ds(start, tall)
                x, ok = after[at, :], valid(start)
                out_ref[at, :] = (ok * (x + branch[at, :] + vec_ref[3:4, :])).astype(bf16)
                unit, inverse = norm_unit(x)
                upstream = up[at, :]
                gains = gains + jnp.sum(upstream * unit, axis=0, keepdims=True)
                shifts = shifts + jnp.sum(upstream, axis=0, keepdims=True)
                pulled = norm_pull(upstream, unit, inverse, vec_ref[1:2, :])
                two = ok * cot_ref[at, :].astype(f32) + pulled
                two_ref[at, :] = two
                low = two.astype(bf16)
                g[at, :] = low
                merges = merges + column_sums(low)
                cross_ref[at, :] = nt(low, merge_ref[...]).astype(bf16)
            ms_ref[...], mo_ref[...] = by_core(core, tn(mixed_ref[...], g[...]), fine, fine)
            sums_ref[1:2, :], sums_ref[2:3, :], sums_ref[3:4, :] = gains, shifts, merges

    base = steps if final else 0

    def once(shape):
        return pl.BlockSpec(shape, lambda i, info: (0, 0), pipeline_mode=pl.Buffered(1))

    def fixed(shape):
        return pl.BlockSpec(shape, lambda i, info: (0,) * len(shape))

    each = hidden // owners // fine
    pairs = others // 2 // steps
    by_row = pl.BlockSpec((2, pairs, each, fine, PIECE), lambda i, info: (0, i, 0, 0, 0))
    by_column = pl.BlockSpec((others, 1, fine, PIECE), lambda i, info: (0, i, 0, 0))
    merged = (others, width // PIECE, fine, PIECE)
    hbm = pl.BlockSpec(memory_space=pltpu.HBM)
    full = (rows, width)
    shared_shapes = [
        *[Shape((2, others // 2, each, fine, PIECE), bf16)] * 2,
        *[Shape((others, steps, fine, PIECE), bf16)] * 2,
        Shape((8, hidden // 2), f32), Shape((8, width), f32),
    ]
    shared_specs = [
        by_row, by_row, by_column, by_column,
        pl.BlockSpec((8, block), lambda i, info: (0, i)), fixed((8, width)),
    ]
    if final:
        shapes = [Shape(full, bf16), Shape(full, f32), Shape(full, bf16), Shape(merged, bf16), Shape(merged, bf16)]
        specs = [fixed(full)] * 3 + [fixed(merged)] * 2
    else:
        shapes, specs = [Shape(full, f32)] * 3, [hbm] * 3
    return pl.pallas_call(
        body,
        out_shape=shapes + shared_shapes,
        grid_spec=pltpu.PrefetchScalarGridSpec(
            num_scalar_prefetch=1,
            grid=(steps,),
            in_specs=[
                once(full), once(full), once((width, width)), once(full), once((8, width)),
                pl.BlockSpec((width, block), lambda i, info: (0, base + i)),
                pl.BlockSpec((1, block), lambda i, info: (0, base + i)),
                pl.BlockSpec((block, width), lambda i, info: (base + i, 0)),
            ] + ([hbm] * 2 if final else []),
            out_specs=specs + shared_specs,
            scratch_shapes=[
                pltpu.VMEM(full, bf16), pltpu.VMEM((width, rows), bf16), pltpu.VMEM(full, bf16),
                pltpu.VMEM(full, f32), pltpu.VMEM(full, f32),
                pltpu.VMEM((rows, block), bf16), pltpu.VMEM((rows, block), bf16),
                pltpu.SemaphoreType.DMA((3,)),
            ] + ([] if final else [pltpu.VMEM(full, f32)]),
        ),
        cost_estimate=TINY,
        compiler_params=settings(60),
        name="feed_forward",
    )(
        info, *in_hbm(start_from, mixed, merge, cotangent), vectors,
        *in_hbm(expand), bias, *in_hbm(reduce), *(begun if final else ()),
    )


def streamed(name, body, info, inputs, outs, scratch=()):
    n, m = len(inputs), len(outs)

    def kernel(info_ref, *refs):
        ins, dests = refs[:n], refs[n : n + m]
        held, made = refs[n + m : 2 * n + m], refs[2 * n + m : 2 * n + 2 * m]
        in_sem, out_sem = refs[2 * n + 2 * m : 2 * n + 2 * m + 2]
        rest = refs[2 * n + 2 * m + 2 :]
        loads = [pltpu.make_async_copy(ins[i], held[i], in_sem.at[i]) for i in range(n)]
        for load in loads:
            load.start()
        waited, stores = set(), {}

        def need(i):
            if i not in waited:
                loads[i].wait()
                waited.add(i)
            return held[i]

        def give(i, send=False):
            if send:
                stores[i] = pltpu.make_async_copy(made[i], dests[i], out_sem.at[i])
                stores[i].start()
            return made[i]

        body(info_ref, need, give, *rest)
        for i in range(m):
            stores[i].wait()

    anywhere = pl.BlockSpec(memory_space=pltpu.HBM)
    return pl.pallas_call(
        kernel,
        out_shape=[Shape(shape, kind) for shape, kind in outs],
        grid_spec=pltpu.PrefetchScalarGridSpec(
            num_scalar_prefetch=1,
            grid=(1,),
            in_specs=[anywhere] * n,
            out_specs=[anywhere] * m,
            scratch_shapes=[pltpu.VMEM(value.shape, value.dtype) for value in inputs]
            + [pltpu.VMEM(shape, kind) for shape, kind in outs]
            + [pltpu.SemaphoreType.DMA((n,)), pltpu.SemaphoreType.DMA((m,))]
            + list(scratch),
        ),
        cost_estimate=TINY,
        compiler_params=settings(60),
        name=name,
    )(info, *inputs)


def probe_backward(info, probe_low, probe_high, probe_weight, after_one, two, output_weight, mixed, vectors, owners):
    rows, width = after_one.shape
    half, tall, fine = width // 2, 256, width // owners

    def body(info_ref, need, give, hidden, low_grad):
        core = info_ref[0]
        left, right = need(0), need(1)
        weight = need(2)
        vec = need(7)
        x_ref, two_ref = need(3), need(4)
        gains = jnp.zeros((1, width), f32)
        shifts, outs = gains, gains
        for start in range(0, rows, tall):
            at = pl.ds(start, tall)
            up = nt(left[at, :], weight[:, :half]) + nt(right[at, :], weight[:, half:])
            unit, inverse = norm_unit(x_ref[at, :])
            hidden[at, :] = (unit * vec[0:1, :] + vec[1:2, :]).astype(bf16)
            gains = gains + jnp.sum(up * unit, axis=0, keepdims=True)
            shifts = shifts + jnp.sum(up, axis=0, keepdims=True)
            one = two_ref[at, :] + norm_pull(up, unit, inverse, vec[0:1, :])
            give(0)[at, :] = one
            low = one.astype(bf16)
            low_grad[at, :] = low
            outs = outs + column_sums(low)
            if start == 0:
                need(5)
            give(1)[at, :] = nt(low, need(5)[...]).astype(bf16)
        give(0, True)
        give(1, True)
        sums = give(4)
        sums[...] = jnp.zeros_like(sums)
        sums[0:1, :], sums[1:2, :], sums[2:3, :] = gains, shifts, outs
        sums[3:4, :half] = column_sums(left[...])
        sums[3:4, half:] = column_sums(right[...])
        give(4, True)
        mixed_ref = need(6)
        columns = (
            (0, 1, hidden, left[...]),
            (1, 2, hidden, right[...]),
            (2, 4, mixed_ref, low_grad[...]),
        )
        for begin, end, source, grads in columns:
            pair = by_core(core, tn(source[...], grads), fine, fine)
            give(2)[:, begin:end], give(3)[:, begin:end] = pair
        give(2, True)
        give(3, True)

    return streamed(
        "probe_backward",
        body,
        info,
        [probe_low, probe_high, probe_weight, after_one, two, output_weight, mixed, vectors],
        [
            ((rows, width), f32), ((rows, width), bf16),
            ((owners // 2, 4, fine, PIECE), bf16), ((owners // 2, 4, fine, PIECE), bf16),
            ((8, width), f32),
        ],
        [pltpu.VMEM((rows, width), bf16), pltpu.VMEM((rows, width), bf16)],
    )


def page_backward(
    info, key_low, key_high, value_low, value_high, page_rows, key_weight, value_weight, owners,
    patch_total,
):
    slots, width = page_rows.shape
    half, fine = width // 2, width // owners
    pieces = patch_total // owners // fine * (width // PIECE)

    def body(info_ref, need, give):
        core, page = info_ref[0], info_ref[3]
        kl, kh, vl, vh = need(0)[...], need(1)[...], need(2)[...], need(3)[...]
        rows_ref = need(4)
        for i, grads in enumerate((kl, kh, vl, vh)):
            pair = by_core(core, tn(rows_ref[...], grads), fine, fine)
            give(0)[:, i : i + 1], give(1)[:, i : i + 1] = pair
        wk, wv = need(5), need(6)
        total = nt(kl, wk[:, :half]) + nt(kh, wk[:, half:])
        total = total + nt(vl, wv[:, :half]) + nt(vh, wv[:, half:])
        pair = by_core(core, total, patch_total // owners, fine)
        each = pair[0].shape[0]
        at = pl.ds(pl.multiple_of(page * each, each), each)
        for which in range(2):
            give(which)[:, 4:] = jnp.zeros((owners // 2, pieces, fine, PIECE), bf16)
            give(which)[at, 4:] = pair[which]
            give(which, True)
        sums = give(2)
        sums[...] = jnp.zeros_like(sums)
        sums[0:1, :half] = column_sums(vl)
        sums[0:1, half:] = column_sums(vh)
        give(2, True)

    return streamed(
        "page_backward",
        body,
        info,
        [key_low, key_high, value_low, value_high, page_rows, key_weight, value_weight],
        [
            *[((owners // 2, 4 + pieces, fine, PIECE), bf16)] * 2, ((8, width), f32),
        ],
    )


def lead_upstream(info, keys, values, key_weight, value_weight, lead_tokens, vectors):
    rows, width = lead_tokens.shape
    half, tall = width // 2, 256

    def body(info_ref, need, give, hidden):
        kl, kh, vl, vh = need(0), need(1), need(2), need(3)
        wk, wv = need(4), need(5)
        x_ref, vec = need(6), need(7)
        gains = jnp.zeros((1, width), f32)
        shifts = gains
        for start in range(0, rows, tall):
            at = pl.ds(start, tall)
            up = nt(kl[at, :], wk[:, :half]) + nt(kh[at, :], wk[:, half:])
            up = up + nt(vl[at, :], wv[:, :half]) + nt(vh[at, :], wv[:, half:])
            give(0)[at, :] = up.astype(bf16)
            unit, _ = norm_unit(x_ref[at, :].astype(f32))
            hidden[at, :] = (unit * vec[0:1, :] + vec[1:2, :]).astype(bf16)
            gains = gains + jnp.sum(up * unit, axis=0, keepdims=True)
            shifts = shifts + jnp.sum(up, axis=0, keepdims=True)
        give(0, True)
        sums = give(2)
        sums[...] = jnp.zeros_like(sums)
        sums[0:1, :], sums[1:2, :] = gains, shifts
        sums[2:3, :half], sums[2:3, half:] = column_sums(vl[...]), column_sums(vh[...])
        give(2, True)
        for i, ref in enumerate((kl, kh, vl, vh)):
            give(1)[:, i * half : (i + 1) * half] = tn(hidden[...], ref[...]).astype(bf16)
        give(1, True)

    return streamed(
        "lead_upstream",
        body,
        info,
        [*keys, *values, key_weight, value_weight, lead_tokens, vectors],
        [((rows, width), bf16), ((width, 2 * width), bf16), ((8, width), f32)],
        [pltpu.VMEM((rows, width), bf16)],
    )


def projection_grads(info, hidden, query_grad, key_grad, value_grad, lead_part, high, owners):
    rows, width = hidden.shape
    half, fine = width // 2, width // owners
    column = half if high else 0

    def body(info_ref, need, give):
        core = info_ref[0]
        h = need(0)
        for i in range(3):
            total = tn(h[...], need(1 + i)[...])
            if i:
                base = (i - 1) * width + column
                total = total + need(4)[:, base : base + half].astype(f32)
            pair = by_core(core, total, fine, fine)
            give(0)[:, i : i + 1], give(1)[:, i : i + 1] = pair
        give(0, True)
        give(1, True)

    return streamed(
        "projection_grads",
        body,
        info,
        [hidden, query_grad, key_grad, value_grad, lead_part],
        [((owners // 2, 3, fine, PIECE), bf16)] * 2,
    )


def first_norm_backward(info, queries, keys, values, weights, tokens, one, returned, vectors):
    rows, width = tokens.shape
    half, tall = width // 2, 384

    def body(info_ref, *refs):
        grads = refs[:6]
        wq, wk, wv, x_ref, vec, one_ref, back_ref = refs[6:13]
        out_ref, sums = refs[13:]
        gains = jnp.zeros((1, width), f32)
        shifts = gains
        for start in range(0, rows, tall):
            at = pl.ds(start, tall)
            up = 0.0
            for i, weight in enumerate((wq, wk, wv)):
                up = up + nt(grads[2 * i][at, :], weight[:, :half])
                up = up + nt(grads[2 * i + 1][at, :], weight[:, half:])
            unit, inverse = norm_unit(x_ref[at, :].astype(f32))
            gains = gains + jnp.sum(up * unit, axis=0, keepdims=True)
            shifts = shifts + jnp.sum(up, axis=0, keepdims=True)
            up = up + back_ref[at, :].astype(f32)
            out_ref[at, :] = one_ref[at, :] + norm_pull(up, unit, inverse, vec[0:1, :])
        sums[...] = jnp.zeros_like(sums)
        sums[0:1, :], sums[1:2, :] = gains, shifts
        sums[2:3, :half], sums[2:3, half:] = column_sums(grads[0][...]), column_sums(grads[1][...])
        sums[3:4, :half], sums[3:4, half:] = column_sums(grads[4][...]), column_sums(grads[5][...])

    narrow = pl.BlockSpec((rows, half), lambda i, info: (0, 0))
    wide = pl.BlockSpec((rows, width), lambda i, info: (0, 0))
    whole = pl.BlockSpec((width, width), lambda i, info: (0, 0))
    eight = pl.BlockSpec((8, width), lambda i, info: (0, 0))
    return pl.pallas_call(
        body,
        out_shape=[Shape((rows, width), f32), Shape((8, width), f32)],
        grid_spec=pltpu.PrefetchScalarGridSpec(
            num_scalar_prefetch=1,
            grid=(1,),
            in_specs=[narrow] * 6 + [whole] * 3 + [wide, eight, wide, wide],
            out_specs=[wide, eight],
        ),
        cost_estimate=TINY,
        compiler_params=settings(),
        name="first_norm_backward",
    )(info, *in_hbm(*queries, *keys, *values, *weights, tokens), vectors, *in_hbm(one, returned))


def digit_axes():
    patch_bits = lax.axis_size("patch").bit_length() - 1
    return [("tok", 0)] + [("patch", bit) for bit in reversed(range(patch_bits))]


def my_digit(axis, bit):
    return (lax.axis_index(axis) >> bit) & 1


def tied(*values):
    return lax.optimization_barrier(values)


FIRST_DIGIT = 4


class Gather:
    def __init__(self, block):
        every = digit_axes()
        self.order = every[-2:0:-1] + every[:1] + every[-1:]
        self.held, self.at = block[None], 0
        self.arrived = hop(self.held, self.order[:1])

    def step(self, chain):
        chain, arrived = tied(chain, self.arrived)
        self.held = jnp.concatenate([self.held, arrived], axis=0)
        self.at += 1
        if self.at < len(self.order):
            chain, self.held = tied(chain, self.held)
            self.arrived = hop(self.held, self.order[self.at : self.at + 1])
        return chain

    def rest(self, chain):
        while self.at < len(self.order):
            chain = self.step(chain)
        return chain

    def places(self, first, count):
        digits = digit_axes()
        device = first + jnp.arange(count, dtype=jnp.int32)
        place = jnp.zeros((count,), jnp.int32)
        for i, one in enumerate(self.order):
            theirs = (device >> (len(digits) - 1 - digits.index(one))) & 1
            place = place | ((theirs ^ my_digit(*one)) << i)
        return place.astype(jnp.int32)


def page_forward(places, blocks, key_weight, value_weight, value_bias):
    count, (each, width) = places.shape[0], blocks.shape[1:]
    slots = count * each

    def body(place_ref, blocks_ref, wk_ref, wv_ref, bias_ref, rows_out, k_out, v_out, rows, wk, wv, k, v, sems):
        copies = [
            pltpu.make_async_copy(
                blocks_ref.at[place_ref[i]], rows.at[pl.ds(i * each, each)], sems.at[i]
            )
            for i in range(count)
        ]
        copies.append(pltpu.make_async_copy(wk_ref, wk, sems.at[count]))
        copies.append(pltpu.make_async_copy(wv_ref, wv, sems.at[count + 1]))
        for copy in copies:
            copy.start()
        for copy in copies[:-1]:
            copy.wait()
        stores = [pltpu.make_async_copy(rows, rows_out, sems.at[count + 2])]
        stores[0].start()
        k[...] = nn(rows[...], wk[...]).astype(bf16)
        stores.append(pltpu.make_async_copy(k, k_out, sems.at[count + 3]))
        stores[1].start()
        copies[-1].wait()
        v[...] = (nn(rows[...], wv[...]) + bias_ref[...]).astype(bf16)
        stores.append(pltpu.make_async_copy(v, v_out, sems.at[count + 4]))
        stores[2].start()
        for store in stores:
            store.wait()

    hbm = pl.BlockSpec(memory_space=pltpu.HBM)
    return pl.pallas_call(
        body,
        out_shape=[Shape((slots, width), bf16)] * 3,
        grid_spec=pltpu.PrefetchScalarGridSpec(
            num_scalar_prefetch=1,
            grid=(1,),
            in_specs=[hbm] * 3 + [pl.BlockSpec((1, width), lambda i, places: (0, 0))],
            out_specs=[hbm] * 3,
            scratch_shapes=[
                pltpu.VMEM((slots, width), bf16), pltpu.VMEM((width, width), bf16),
                pltpu.VMEM((width, width), bf16), pltpu.VMEM((slots, width), bf16),
                pltpu.VMEM((slots, width), bf16), pltpu.SemaphoreType.DMA((count + 5,)),
            ],
        ),
        cost_estimate=TINY,
        compiler_params=settings(),
        name="page_forward",
    )(places, blocks, key_weight, value_weight, value_bias)


class Part:
    def __init__(self, kept, tok_first, place, start=0, pieces=None):
        self.tok_first, self.place = tok_first, place
        self.pieces = pieces or kept.shape[1]
        self.terms = [(kept, owner_digits(), start)]


def owner_digits():
    return digit_axes()[:-1]


def stages_of(tok_first, direct):
    every = digit_axes()
    bits = every[-2:0:-1]
    loose, last = bits[: max(len(bits) - 2, 0)], bits[max(len(bits) - 2, 0) :]
    singles = [[one] for one in loose]
    ends = [last] if direct else [[one] for one in last]
    return ([every[:1]] + singles if tok_first else singles + [every[:1]]) + ends


class Sum:
    def __init__(self, direct, *sent):
        self.direct = direct
        self.parts = [part for _, parts in sent for part in parts]
        self.at = 0
        self.leaving = [array for array, _ in sent]
        self.hops = [[("patch", 0)]] * len(sent)
        self.groups = [parts for _, parts in sent]
        self.mine = self.came = None

    def send(self):
        self.arrived = [hop(value, steps) for value, steps in zip(self.leaving, self.hops)]

    def free(self, part, at):
        settled = [one for stage in stages_of(part.tok_first, self.direct)[:at] for one in stage]
        return [one for one in owner_digits() if one not in settled]

    def absorb(self, arrived):
        if self.mine is not None:
            self.came = arrived
            self.leaving = None
            return []
        for value, group in zip(arrived, self.groups):
            start = 0
            for part in group:
                part.terms = part.terms + [(value, self.free(part, self.at), start)]
                start += part.pieces
        stages = [stages_of(part.tok_first, self.direct) for part in self.parts]
        last = self.at == len(stages[0]) - 1
        ways = [stage[self.at] for stage in stages]
        self.at += 1
        jobs, self.hops, self.groups = [], [], []
        for digits in [way for i, way in enumerate(ways) if way not in ways[:i]]:
            group = [part for part, way in zip(self.parts, ways) if way == digits]
            free = self.free(group[0], self.at)
            for flips in range(0 if last else 1, 1 << len(digits)):
                flipped = [one for i, one in enumerate(digits) if flips >> i & 1]
                choices = []
                for chunk in range(1 << len(free)):
                    bits = {one: chunk >> (len(free) - 1 - i) & 1 for i, one in enumerate(free)}
                    choices.append((bits, flipped))
                terms = [(part.terms, part.pieces) for part in group]
                jobs.append((terms, choices, bf16 if flips else f32))
                if flips:
                    self.hops.append(flipped)
                    self.groups.append(group)
        return jobs

    def take(self, made):
        if self.at == len(stages_of(True, self.direct)):
            self.mine = made[0]
            made = made[1:]
        self.leaving = list(made)


def hop(value, steps):
    axis = steps[0][0]
    flip = sum(1 << bit for _, bit in steps)
    return lax.ppermute(value, axis, [(i, i ^ flip) for i in range(lax.axis_size(axis))])


def finished(shapes, *totals):
    arrays = [one for total in totals for one in [total.mine, *total.came]]

    def body(*refs):
        refs, outs = list(refs[: len(arrays)]), refs[len(arrays) :]
        for total in totals:
            mine_ref, *came = refs[: 1 + len(total.came)]
            refs = refs[1 + len(total.came) :]
            piece = 0
            for part in total.parts:
                out, at_column = part.place
                fine = mine_ref.shape[2]
                tall = shapes[out][0] // fine
                for p in range(part.pieces):
                    sum_here = mine_ref[0, piece]
                    for ref in came:
                        sum_here = sum_here + ref[0, piece].astype(f32)
                    row, column = p % tall * fine, at_column + p // tall * PIECE
                    outs[out][row : row + fine, column : column + PIECE] = sum_here
                    piece += 1

    return pl.pallas_call(
        body,
        out_shape=[Shape(shape, f32) for shape in shapes],
        cost_estimate=TINY,
        compiler_params=pltpu.CompilerParams(vmem_limit_bytes=40 * MIB),
        name="finished",
    )(*arrays)


def added_up(info, jobs):
    digits = digit_axes()
    arrays, known = [], {}
    for parts, _, _ in jobs:
        for terms, _ in parts:
            for value, _, _ in terms:
                if id(value) not in known:
                    known[id(value)] = len(arrays)
                    arrays.append(value)
    fine = arrays[0].shape[2]
    units = [(job, part) for job in range(len(jobs)) for part in range(len(jobs[job][0]))]
    loads = sum(len(jobs[job][0][part][0]) * len(jobs[job][1]) for job, part in units)

    def body(info_ref, *refs):
        n, m, k = len(arrays), len(jobs), len(units)
        ins, dests = refs[:n], refs[n : n + m]
        held, made = refs[n + m : n + m + k], refs[n + m + k : n + 2 * m + k]
        in_sem, out_sem = refs[n + 2 * m + k :]
        mine = {one: info_ref[FIRST_DIGIT + i] for i, one in enumerate(digits)}
        copies, count = [], 0
        for unit, (job, part) in enumerate(units):
            terms, pieces = jobs[job][0][part]
            copies.append([])
            for t, (value, free, start) in enumerate(terms):
                for c, (bits, flipped) in enumerate(jobs[job][1]):
                    index = 0
                    for one in free:
                        digit = bits[one] if one in bits else mine[one]
                        digit = 1 - digit if one in flipped else digit
                        index = 2 * index + digit
                    copy = pltpu.make_async_copy(
                        ins[known[id(value)]].at[index, pl.ds(start, pieces)],
                        held[unit].at[t, c],
                        in_sem.at[count],
                    )
                    copy.start()
                    copies[-1].append(copy)
                    count += 1
        offsets = [0] * m
        left = [len(jobs[job][0]) for job in range(m)]
        stores = []
        for unit, (job, part) in enumerate(units):
            terms, pieces = jobs[job][0][part]
            for copy in copies[unit]:
                copy.wait()
            offset = offsets[job]

            batch = max(one for one in range(1, 9) if pieces % one == 0)
            per = pieces // batch

            def step(i, _, unit=unit, job=job, count=len(terms), per=per, batch=batch, offset=offset):
                chunk = i // per
                for p in range(batch):
                    piece = i % per * batch + p
                    total = held[unit][0, chunk, piece].astype(f32)
                    for t in range(1, count):
                        total = total + held[unit][t, chunk, piece].astype(f32)
                    made[job][chunk, offset + piece] = total.astype(jobs[job][2])
                return 0

            lax.fori_loop(0, len(jobs[job][1]) * per, step, 0)
            offsets[job] += pieces
            left[job] -= 1
            if not left[job]:
                stores.append(pltpu.make_async_copy(made[job], dests[job], out_sem.at[job]))
                stores[-1].start()
        for store in stores:
            store.wait()

    anywhere = pl.BlockSpec(memory_space=pltpu.HBM)
    shapes = [
        ((len(choices), sum(pieces for _, pieces in parts), fine, PIECE), kind)
        for parts, choices, kind in jobs
    ]
    held = [
        pltpu.VMEM(
            (len(jobs[job][0][part][0]), len(jobs[job][1]), jobs[job][0][part][1], fine, PIECE), bf16
        )
        for job, part in units
    ]
    return pl.pallas_call(
        body,
        out_shape=[Shape(shape, kind) for shape, kind in shapes],
        grid_spec=pltpu.PrefetchScalarGridSpec(
            num_scalar_prefetch=1,
            grid=(1,),
            in_specs=[anywhere] * len(arrays),
            out_specs=[pl.BlockSpec(memory_space=pltpu.HBM)] * len(jobs),
            scratch_shapes=held
            + [pltpu.VMEM(shape, kind) for shape, kind in shapes]
            + [pltpu.SemaphoreType.DMA((loads,)), pltpu.SemaphoreType.DMA((len(jobs),))],
        ),
        cost_estimate=TINY,
        compiler_params=settings(60),
        name="added_up",
    )(info, *arrays)


def advance(info, chain, moving=(), fresh=()):
    moving = [one for one in moving if one.leaving is not None]
    chain, arrived = tied(chain, [one.arrived for one in moving])
    jobs, owners = [], []
    for one, values in zip(moving, arrived):
        new = one.absorb(values)
        owners.append((one, len(new)))
        jobs += new
    if jobs:
        made = added_up(info, jobs)
        for one, count in owners:
            if count:
                one.take(made[:count])
                made = made[count:]
    going = [one for one in moving + list(fresh) if one.leaving is not None]
    chain, leaving = tied(chain, [one.leaving for one in going])
    for one, values in zip(going, leaving):
        one.leaving = values
        one.send()
    return chain


def vector_table(feed, expand_bias, probe, page, lead, first):
    width = feed.shape[1]

    def body(feed_ref, bias_ref, probe_ref, page_ref, lead_ref, first_ref, out):
        rows = [
            first_ref[0:1, :] + lead_ref[0:1, :],
            first_ref[1:2, :] + lead_ref[1:2, :],
            first_ref[2:3, :],
            first_ref[3:4, :] + lead_ref[2:3, :],
            probe_ref[2:3, :],
            probe_ref[0:1, :],
            probe_ref[1:2, :],
            probe_ref[3:4, :],
            page_ref[0:1, :],
            feed_ref[3:4, :],
            feed_ref[1:2, :],
            feed_ref[2:3, :],
            feed_ref[0:1, :],
        ]
        out[...] = jnp.zeros_like(out)
        for i, row in enumerate(rows):
            out[i : i + 1, :] = row
        out[16 : 16 + bias_ref.shape[0], :] = bias_ref[...]

    return pl.pallas_call(
        body,
        out_shape=jax.ShapeDtypeStruct((24, width), f32),
        cost_estimate=TINY,
        name="vector_table",
    )(feed, expand_bias, probe, page, lead, first)


def scatter_rows(table, width, first, last):
    digits = digit_axes()
    fine = width >> len(digits)
    for axis, bit in digits[first:last]:
        half = table.shape[1] // 2
        if half % LANES:
            table = table + hop(table, [(axis, bit)])
        else:
            digit = my_digit(axis, bit)
            keep = lax.dynamic_slice_in_dim(table, digit * half, half, 1)
            give = lax.dynamic_slice_in_dim(table, (1 - digit) * half, half, 1)
            table = keep + hop(give, [(axis, bit)])
    if last < len(digits):
        return table
    inside = 0
    for axis, bit in digits[(table.shape[1] // fine).bit_length() * -1 + 1 :]:
        inside = 2 * inside + my_digit(axis, bit)
    return lax.dynamic_slice_in_dim(table, inside * fine, fine, 1)


def pick_entry(table, position):
    indices = jnp.arange(table.shape[0], dtype=jnp.int32)
    return jnp.sum(jnp.where(indices == position, table, 0))


def layer_norm(values, gain, shift):
    unit, _ = norm_unit(values)
    return (unit * gain + shift).astype(bf16)


def rows_of(*vectors):
    rows = jnp.stack(vectors, axis=0)
    return jnp.pad(rows, ((0, 8 - len(vectors)), (0, 0)))


def local(
    tokens,
    patches,
    cotangent,
    lengths,
    page_of,
    page_counts,
    self_gain,
    self_shift,
    query_weight,
    query_bias,
    key_weight,
    value_weight,
    value_bias,
    output_weight,
    output_bias,
    cross_gain,
    cross_shift,
    probe_weight,
    probe_bias,
    source_key,
    source_value,
    source_bias,
    merge_weight,
    merge_bias,
    feed_gain,
    feed_shift,
    expand_weight,
    expand_bias,
    reduce_weight,
    reduce_bias,
):
    head_scale = HDIM ** (-0.5)
    tok_index = lax.axis_index("tok").astype(jnp.int32)
    sequence = lax.axis_index("patch")
    core = my_digit("patch", 0).astype(jnp.int32)
    row_count, model_width = tokens.shape[1:]
    lead_tokens = lax.ppermute(tokens[0], "tok", [(0, 1)])
    inputs = tokens[0].astype(f32)
    page_index = pick_entry(page_of, sequence)
    filled = pick_entry(page_counts, page_index).reshape(1)
    trailing = tok_index.reshape(1)
    page_start = page_index * PAGE_SLOTS
    digits = [my_digit(*one).astype(jnp.int32) for one in digit_axes()]
    owners = 1 << len(digits)
    info = jnp.stack(
        [core, tok_index * row_count, pick_entry(lengths, sequence), page_index] + digits
    )
    self_vectors = rows_of(self_gain, self_shift)
    cross_vectors = rows_of(cross_gain, cross_shift)
    feed_vectors = rows_of(merge_bias, feed_gain, feed_shift, reduce_bias)

    hidden_one = layer_norm(inputs, self_gain, self_shift)
    query = ((nn(hidden_one, query_weight) + query_bias) * head_scale).astype(bf16)
    own_keys = nn(hidden_one, key_weight).astype(bf16)
    own_values = (nn(hidden_one, value_weight) + value_bias).astype(bf16)
    gather = Gather(patches)
    query = gather.step(query)
    own_values = gather.step(own_values)
    own_mixed, own_total = own_forward(query, own_keys, own_values)
    lead_tokens, own_mixed = gather.step((lead_tokens, own_mixed))
    hidden_lead = layer_norm(lead_tokens.astype(f32), self_gain, self_shift)
    lead_keys = nn(hidden_lead, key_weight).astype(bf16)
    lead_values = (nn(hidden_lead, value_weight) + value_bias).astype(bf16)
    self_mixed, self_total = lead_forward(
        query, lead_keys, lead_values, own_mixed, own_total, trailing
    )
    self_mixed = gather.step(self_mixed)
    after_one = inputs + nn(self_mixed, output_weight) + output_bias
    hidden_two = layer_norm(after_one, cross_gain, cross_shift)
    probe = ((nn(hidden_two, probe_weight) + probe_bias) * head_scale).astype(bf16)
    probe = gather.rest(probe)
    page_rows, page_keys, page_values = page_forward(
        gather.places(page_start // patches.shape[0], PAGE_SLOTS // patches.shape[0]),
        gather.held, source_key, source_value, source_bias[None],
    )
    cross_mixed, cross_total = cross_forward(probe, page_keys, page_values, filled)

    feed_args = (
        cross_mixed, merge_weight, cotangent[0], feed_vectors, expand_weight, expand_bias[None],
        reduce_weight, info, owners,
    )
    branch, upstream, after_two, *fed = feed_forward(after_one, *feed_args, None)
    fine = model_width // owners
    deep = expand_weight.shape[1] // 2

    def by_owner(value):
        return value.reshape((-1,) + value.shape[2:])

    first = Sum(
        False,
        (fed[2], [Part(fed[3], True, (0, 0))]),
        (by_owner(fed[0]), [Part(by_owner(fed[1]), False, (1, 0))]),
    )
    low_bias, low_sums = fed[4:]
    after_two, branch, upstream = advance(info, (after_two, branch, upstream), [], [first])
    block_output, grad_two, grad_cross_out, *fed = feed_forward(
        after_two, *feed_args, (branch, upstream)
    )
    second = Sum(
        False,
        (fed[4], [Part(fed[5], True, (0, deep))]),
        (by_owner(fed[2]), [Part(by_owner(fed[3]), False, (2, 0))]),
        (fed[0], [Part(fed[1], False, (3, 0))]),
    )
    expand_bias_sums = jnp.concatenate([low_bias[0], fed[6][0]])
    feed_sums = fed[7]

    half_pairs = model_width // PAIR // 2
    cross_args = (probe, page_keys, page_values, cross_mixed, cross_total)
    grad_cross_out = advance(info, grad_cross_out, [first], [second])
    low = cross_backward(*cross_args, grad_cross_out, filled, 0, half_pairs)
    low, grad_cross_out = tied(low, grad_cross_out)
    high = cross_backward(*cross_args, grad_cross_out, filled, half_pairs, half_pairs)
    low, high = advance(info, (low, high), [first, second])
    patch_total = patches.shape[0] * lax.axis_size(("tok", "patch"))
    paged = page_backward(
        info, low[1], high[1], low[2], high[2], page_rows, source_key, source_value, owners,
        patch_total,
    )
    probed = probe_backward(
        info, low[0], high[0], probe_weight, after_one, grad_two, output_weight, self_mixed,
        cross_vectors, owners,
    )
    grad_one, grad_self_out, probe_sums = probed[0], probed[1], probed[4]
    third = Sum(
        False,
        (
            paged[0],
            [Part(paged[1], True, (0, 0), 0, 4), Part(paged[1], False, (1, 0), 4, paged[1].shape[1] - 4)],
        ),
        (probed[2], [Part(probed[3], False, (2, 0))]),
    )
    self_args = (query, lead_keys, lead_values, self_mixed, self_total)
    own_args = (query, own_keys, own_values, self_mixed, self_total)
    grad_self_out = advance(info, grad_self_out, [first, second], [third])
    lead_low = lead_backward(*self_args, grad_self_out, trailing, 0, half_pairs)
    lead_low, grad_self_out = advance(info, (lead_low, grad_self_out), [first, second, third])
    lead_high = lead_backward(*self_args, grad_self_out, trailing, half_pairs, half_pairs)
    led_grad, led_part, lead_sums = lead_upstream(
        info, (lead_low[1], lead_high[1]), (lead_low[2], lead_high[2]), key_weight,
        value_weight, lead_tokens, self_vectors,
    )
    led_grad, led_part, grad_self_out = advance(
        info, (led_grad, led_part, grad_self_out), [first, second, third]
    )
    returned = lax.ppermute(led_grad, "tok", [(1, 0)])
    own_low = own_backward(*own_args, grad_self_out, lead_low[0], 0, half_pairs)
    own_low, grad_self_out = advance(info, (own_low, grad_self_out), [second, third])
    parts = projection_grads(info, hidden_one, *own_low, led_part, False, owners)
    half = model_width // 2
    fourth = Sum(False, (parts[0], [Part(parts[1], i == 1, (i, 0), i, 1) for i in range(3)]))
    own_low, grad_self_out = advance(info, (own_low, grad_self_out), [], [fourth])
    own_high = own_backward(*own_args, grad_self_out, lead_high[0], half_pairs, half_pairs)
    own_low, own_high, returned = advance(
        info, (own_low, own_high, returned), [third, fourth]
    )
    tokens_grad, first_sums = first_norm_backward(
        info, (own_low[0], own_high[0]), (own_low[1], own_high[1]), (own_low[2], own_high[2]),
        (query_weight, key_weight, value_weight), tokens[0], grad_one, returned, self_vectors,
    )
    first_sums, own_high, led_part = advance(
        info, (first_sums, own_high, led_part), [third, fourth]
    )
    parts = projection_grads(info, hidden_one, *own_high, led_part, True, owners)
    bias_rows = expand_bias_sums.reshape(owners, -1, fine)
    bias_rows = jnp.transpose(bias_rows, (1, 0, 2)).reshape(-1, model_width)
    table = vector_table(feed_sums, bias_rows, probe_sums, paged[2], lead_sums, first_sums)
    table = scatter_rows(table, model_width, 0, 1)
    fifth = Sum(True, (parts[0], [Part(parts[1], i != 1, (i, half), i, 1) for i in range(3)]))
    table = advance(info, table, [], [fifth])
    table = scatter_rows(table, model_width, 1, 2)
    table = advance(info, table, [fourth, fifth])
    table = scatter_rows(table, model_width, 2, 3)
    table = advance(info, table, [fourth, fifth])
    table = scatter_rows(table, model_width, 3, len(digits) - 1)
    table = advance(info, table, [fourth, fifth])
    sums = scatter_rows(table, model_width, len(digits) - 1, len(digits))
    totals = [first, second, third, fourth, fifth]
    while any(one.leaving is not None for one in totals):
        sums = advance(info, sums, totals)
    tall = expand_weight.shape[1] // owners
    model, half_reduce = (fine, model_width), (tall, half)
    expand_grad, reduce_low, reduce_high, merge_grad = finished(
        [(fine, expand_weight.shape[1]), half_reduce, half_reduce, model], first, second
    )
    is_first = tok_index == 0
    given = jnp.where(is_first, reduce_high, reduce_low).astype(bf16)
    taken = hop(given, [("tok", 0)]).astype(f32)
    reduce_grad = jnp.concatenate(
        [jnp.where(is_first, reduce_low, taken), jnp.where(is_first, taken, reduce_high)], axis=1
    )
    source_grads, patches_grad, middle_grads = finished(
        [(fine, 2 * model_width), (patches.shape[0], model_width), (fine, 2 * model_width)], third
    )
    projections = finished([model] * 3, fourth, fifth)
    return (
        block_output[None],
        tokens_grad[None],
        patches_grad,
        sums[0],
        sums[1],
        projections[0],
        sums[2],
        projections[1],
        projections[2],
        sums[3],
        middle_grads[:, model_width:],
        sums[4],
        sums[5],
        sums[6],
        middle_grads[:, :model_width],
        sums[7],
        source_grads[:, :model_width],
        source_grads[:, model_width:],
        sums[8],
        merge_grad,
        sums[9],
        sums[10],
        sums[11],
        expand_grad,
        sums[16 : 16 + expand_bias.shape[0] // model_width].reshape(-1),
        reduce_grad,
        sums[12],
    )


def solution(mesh):
    placed = (
        P("patch", "tok", None),
        P(("tok", "patch"), None),
        P("patch", "tok", None),
        P(),
        P(),
        P(),
        P(),
        P(),
        P(),
        P(),
        P(),
        P(),
        P(),
        P(),
        P(),
        P(),
        P(),
        P(),
        P(),
        P(),
        P(),
        P(),
        P(),
        P(),
        P(),
        P(),
        P(),
        P(),
        P(),
        P(),
    )
    return jax.shard_map(
        local,
        mesh=mesh,
        in_specs=placed,
        out_specs=(
            P("patch", "tok", None),
            P("patch", "tok", None),
            P(("tok", "patch"), None),
            P(("tok", "patch")),
            P(("tok", "patch")),
            P(("tok", "patch"), None),
            P(("tok", "patch")),
            P(("tok", "patch"), None),
            P(("tok", "patch"), None),
            P(("tok", "patch")),
            P(("tok", "patch"), None),
            P(("tok", "patch")),
            P(("tok", "patch")),
            P(("tok", "patch")),
            P(("tok", "patch"), None),
            P(("tok", "patch")),
            P(("tok", "patch"), None),
            P(("tok", "patch"), None),
            P(("tok", "patch")),
            P(("tok", "patch"), None),
            P(("tok", "patch")),
            P(("tok", "patch")),
            P(("tok", "patch")),
            P(("tok", "patch"), None),
            P(("tok", "patch")),
            P(("tok", "patch"), None),
            P(("tok", "patch")),
        ),
        check_vma=False,
    )
```

```python
import jax
import jax.numpy as jnp
from jax import lax
from jax.experimental import pallas as pl
from jax.experimental.pallas import tpu as pltpu
from jax.sharding import PartitionSpec as P

HDIM = 64
PAIR = 2 * HDIM
PAGE_SLOTS = 512
NEG_FILL = -1e30
EPS_NORM = 1e-05
LANES = 128
PIECE = 512
HIGH = lax.Precision.HIGHEST
MIB = 1 << 20
bf16, f32 = jnp.bfloat16, jnp.float32
Shape = pltpu.HBM


def nn(left, right):
    return lax.dot_general(
        left, right, (((1,), (0,)), ((), ())), preferred_element_type=f32
    )


def nt(left, right, precision=None):
    return lax.dot_general(
        left, right, (((1,), (1,)), ((), ())), precision=precision, preferred_element_type=f32
    )


def tn(left, right):
    return lax.dot_general(
        left, right, (((0,), (0,)), ((), ())), preferred_element_type=f32
    )


def column_sums(values):
    return jnp.sum(values.astype(f32), axis=0, keepdims=True)


def norm_unit(values):
    average = jnp.mean(values, axis=-1, keepdims=True)
    centred = values - average
    spread = jnp.mean(centred * centred, axis=-1, keepdims=True)
    inverse = lax.rsqrt(spread + EPS_NORM)
    return centred * inverse, inverse


def norm_pull(upstream, unit, inverse, gain):
    scaled = upstream * gain
    centred = scaled - jnp.mean(scaled, axis=-1, keepdims=True)
    centred = centred - unit * jnp.mean(scaled * unit, axis=-1, keepdims=True)
    return centred * inverse


def gelu_pair(values):
    share = 0.5 * (1.0 + lax.erf(values * (2.0**-0.5)))
    slope = share + values * (jnp.exp(-0.5 * values * values) * 0.3989422804014327)
    return values * share, slope


def by_core(core, value, each, fine):
    count, width = value.shape
    split = value.reshape(count // (2 * each), 2, each, width)
    found = []
    for own in range(2):
        one = jnp.where((core == 0) == (own == 0), split[:, 1], split[:, 0])
        one = one.reshape(count // (2 * each), each // fine, fine, width)
        columns = [one[..., at : at + PIECE] for at in range(0, width, PIECE)]
        one = columns[0] if len(columns) == 1 else jnp.concatenate(columns, axis=1)
        found.append(one.astype(bf16))
    return found


def head_lanes(head):
    lane = lax.broadcasted_iota(jnp.int32, (1, PAIR), 1)
    return (lane >= head * HDIM) & (lane < (head + 1) * HDIM)


def only(value, head):
    return jnp.where(head_lanes(head), value, jnp.zeros_like(value))


TINY = pl.CostEstimate(flops=1, bytes_accessed=1, transcendentals=0)


def settings(limit=48):
    return pltpu.CompilerParams(
        dimension_semantics=("arbitrary",), vmem_limit_bytes=limit * MIB
    )


def in_hbm(*values):
    return [pltpu.with_memory_space_constraint(value, pltpu.HBM) for value in values]


def scores_of(key_rows, query, start, mask):
    score = nt(key_rows, query[start:])
    if isinstance(mask, str):
        rows = score.shape[0]
        row = lax.broadcasted_iota(jnp.int32, (rows, rows), 0)
        column = lax.broadcasted_iota(jnp.int32, (rows, rows), 1)
        corner = jnp.where(row <= column, score[:, :rows], NEG_FILL)
        if score.shape[1] == rows:
            return corner
        return jnp.concatenate([corner, score[:, rows:]], axis=1)
    return score if mask is None else score + mask


def from_start(whole, start, part, combine):
    if whole is None:
        return part
    if start == 0:
        return combine(whole, part)
    return jnp.concatenate([whole[:, :start], combine(whole[:, start:], part)], axis=1)


def forward_pair(q_ref, k_ref, v_ref, blocks, begun, out_ref, total_ref):
    values = v_ref[...].T
    outs = []
    for head in range(2):
        lanes = slice(head * HDIM, (head + 1) * HDIM)
        query = only(q_ref[...], head)
        earlier = None if begun is None else begun[1][0, head : head + 1, :]
        row_max, scores = None, []
        for first, rows, start, mask in blocks:
            score = scores_of(k_ref[pl.ds(first, rows), :], query, start, mask)
            row_max = from_start(row_max, start, score.max(0, keepdims=True), jnp.maximum)
            scores.append(score)
        if begun is not None:
            row_max = jnp.maximum(row_max, earlier)
        total, out = None, None
        for score, (first, rows, start, _) in zip(scores, blocks):
            exponent = jnp.exp(score - row_max[:, start:])
            total = from_start(total, start, exponent.sum(0, keepdims=True), jnp.add)
            part = nn(values[lanes, first : first + rows], exponent.astype(bf16))
            out = from_start(out, start, part, jnp.add)
        if begun is not None:
            share = jnp.exp(earlier - row_max)
            total = total + share
            out = out + begun[0][lanes] * share
        outs.append(out / total)
        total_ref[0, head : head + 1, :] = row_max + jnp.log(total)
    out_ref[...] = jnp.concatenate(outs, axis=0).T.astype(bf16)


def backward_pair(q_ref, k_ref, v_ref, out_ref, total_ref, g_ref, blocks, acc, fresh, dk_ref, dv_ref):
    queries, upstreams, keys = q_ref[...].T, g_ref[...].T, k_ref[...].T
    product = upstreams.astype(f32) * out_ref[...].T.astype(f32)
    for first, rows, start, mask in blocks:
        key_rows, value_rows = k_ref[pl.ds(first, rows), :], v_ref[pl.ds(first, rows), :]
        key_grads, value_grads = [], []
        for head in range(2):
            lanes = slice(head * HDIM, (head + 1) * HDIM)
            inner = product[lanes, start:].sum(0, keepdims=True)
            score = scores_of(key_rows, only(q_ref[...], head), start, mask)
            soft = jnp.exp(score - total_ref[0, head : head + 1, start:])
            grad_soft = nt(value_rows, only(g_ref[...], head)[start:])
            grad_score = (soft * (grad_soft - inner)).astype(bf16)
            value_grads.append(nt(upstreams[lanes, start:], soft.astype(bf16)))
            key_grads.append(nt(queries[lanes, start:], grad_score))
            part = nn(keys[lanes, first : first + rows], grad_score)
            if fresh and first == 0:
                acc[lanes, start:] = part
            else:
                acc[lanes, start:] += part
        dk_ref[pl.ds(first, rows), :] = jnp.concatenate(key_grads, axis=0).T.astype(bf16)
        dv_ref[pl.ds(first, rows), :] = jnp.concatenate(value_grads, axis=0).T.astype(bf16)


def causal_blocks(rows, size=256):
    return [(at, size, at, "causal") for at in range(0, rows, size)]


def totals_shape(rows, width):
    return (width // PAIR, 2, rows)


def own_forward(query, keys, values):
    rows, width = query.shape

    def body(q_ref, k_ref, v_ref, out_ref, total_ref):
        forward_pair(q_ref, k_ref, v_ref, causal_blocks(rows), None, out_ref, total_ref)

    block = pl.BlockSpec((rows, PAIR), lambda p: (0, p))
    total = pl.BlockSpec((1, 2, rows), lambda p: (p, 0, 0))
    return pl.pallas_call(
        body,
        out_shape=(Shape((rows, width), bf16), Shape(totals_shape(rows, width), f32)),
        grid=(width // PAIR,),
        in_specs=[block] * 3,
        out_specs=[block, total],
        cost_estimate=TINY,
        compiler_params=settings(),
        name="own_forward",
    )(*in_hbm(query, keys, values))


def lead_forward(query, keys, values, begun, begun_total, trailing):
    rows, width = query.shape

    def body(flag, q_ref, k_ref, v_ref, begun_ref, old_ref, out_ref, total_ref):
        @pl.when(flag[0] == 1)
        def _():
            begun = (begun_ref[...].T.astype(f32), old_ref)
            blocks = [(0, rows, 0, None)]
            forward_pair(q_ref, k_ref, v_ref, blocks, begun, out_ref, total_ref)

        @pl.when(flag[0] == 0)
        def _():
            out_ref[...] = begun_ref[...]
            total_ref[...] = old_ref[...]

    block = pl.BlockSpec((rows, PAIR), lambda p, flag: (0, p))
    total = pl.BlockSpec((1, 2, rows), lambda p, flag: (p, 0, 0))
    return pl.pallas_call(
        body,
        out_shape=(Shape((rows, width), bf16), Shape(totals_shape(rows, width), f32)),
        grid_spec=pltpu.PrefetchScalarGridSpec(
            num_scalar_prefetch=1,
            grid=(width // PAIR,),
            in_specs=[block] * 4 + [total],
            out_specs=[block, total],
        ),
        cost_estimate=TINY,
        compiler_params=settings(),
        name="lead_forward",
    )(trailing, *in_hbm(query, keys, values, begun, begun_total))


def slot_bias(filled_ref, slots):
    slot = lax.broadcasted_iota(jnp.int32, (slots, 1), 0)
    return jnp.where(slot < filled_ref[0], 0.0, NEG_FILL)


def cross_forward(query, keys, values, filled):
    rows, width = query.shape
    slots = keys.shape[0]

    def body(filled_ref, q_ref, k_ref, v_ref, out_ref, total_ref):
        blocks = [(0, slots, 0, slot_bias(filled_ref, slots))]
        forward_pair(q_ref, k_ref, v_ref, blocks, None, out_ref, total_ref)

    block = pl.BlockSpec((rows, PAIR), lambda p, f: (0, p))
    page = pl.BlockSpec((slots, PAIR), lambda p, f: (0, p))
    total = pl.BlockSpec((1, 2, rows), lambda p, f: (p, 0, 0))
    return pl.pallas_call(
        body,
        out_shape=(Shape((rows, width), bf16), Shape(totals_shape(rows, width), f32)),
        grid_spec=pltpu.PrefetchScalarGridSpec(
            num_scalar_prefetch=1,
            grid=(width // PAIR,),
            in_specs=[block, page, page],
            out_specs=[block, total],
        ),
        cost_estimate=TINY,
        compiler_params=settings(),
        name="cross_forward",
    )(filled, *in_hbm(query, keys, values))


def lead_backward(query, keys, values, out, total, grad, trailing, first, pairs, size=384):
    rows = query.shape[0]

    def body(flag, q_ref, k_ref, v_ref, out_ref, total_ref, g_ref, dq_ref, dk_ref, dv_ref):
        @pl.when(flag[0] == 1)
        def _():
            blocks = [(at, size, 0, None) for at in range(0, rows, size)]
            backward_pair(
                q_ref, k_ref, v_ref, out_ref, total_ref, g_ref, blocks, dq_ref, True, dk_ref, dv_ref
            )

        @pl.when(flag[0] == 0)
        def _():
            for ref in (dq_ref, dk_ref, dv_ref):
                ref[...] = jnp.zeros_like(ref)

    source = pl.BlockSpec((rows, PAIR), lambda p, flag: (0, p + first))
    target = pl.BlockSpec((rows, PAIR), lambda p, flag: (0, p))
    totals = pl.BlockSpec((1, 2, rows), lambda p, flag: (p + first, 0, 0))
    return pl.pallas_call(
        body,
        out_shape=[Shape((pairs * PAIR, rows), f32)] + [Shape((rows, pairs * PAIR), bf16)] * 2,
        grid_spec=pltpu.PrefetchScalarGridSpec(
            num_scalar_prefetch=1,
            grid=(pairs,),
            in_specs=[source] * 4 + [totals, source],
            out_specs=[pl.BlockSpec((PAIR, rows), lambda p, flag: (p, 0)), target, target],
        ),
        cost_estimate=TINY,
        compiler_params=settings(),
        name="lead_backward",
    )(trailing, *in_hbm(query, keys, values, out, total, grad))


def own_backward(query, keys, values, out, total, grad, begun, first, pairs):
    rows = query.shape[0]

    def body(q_ref, k_ref, v_ref, out_ref, total_ref, g_ref, begun_ref, dq_ref, dk_ref, dv_ref, acc):
        acc[...] = begun_ref[...]
        backward_pair(
            q_ref, k_ref, v_ref, out_ref, total_ref, g_ref, causal_blocks(rows), acc, False,
            dk_ref, dv_ref,
        )
        dq_ref[...] = (acc[...] * (HDIM**-0.5)).T.astype(bf16)

    source = pl.BlockSpec((rows, PAIR), lambda p: (0, p + first))
    target = pl.BlockSpec((rows, PAIR), lambda p: (0, p))
    totals = pl.BlockSpec((1, 2, rows), lambda p: (p + first, 0, 0))
    return pl.pallas_call(
        body,
        out_shape=[Shape((rows, pairs * PAIR), bf16)] * 3,
        grid=(pairs,),
        in_specs=[source] * 4 + [totals, source, pl.BlockSpec((PAIR, rows), lambda p: (p, 0))],
        out_specs=[target] * 3,
        scratch_shapes=[pltpu.VMEM((PAIR, rows), f32)],
        cost_estimate=TINY,
        compiler_params=settings(),
        name="own_backward",
    )(*in_hbm(query, keys, values, out, total, grad, begun))


def cross_backward(query, keys, values, out, total, grad, filled, first, pairs):
    rows, slots = query.shape[0], keys.shape[0]

    def body(
        filled_ref, q_ref, k_ref, v_ref, out_ref, total_ref, g_ref, dq_ref, dk_ref, dv_ref, acc
    ):
        blocks = [(0, slots, 0, slot_bias(filled_ref, slots))]
        backward_pair(
            q_ref, k_ref, v_ref, out_ref, total_ref, g_ref, blocks, acc, True, dk_ref, dv_ref
        )
        dq_ref[...] = (acc[...] * (HDIM**-0.5)).T.astype(bf16)

    source = pl.BlockSpec((rows, PAIR), lambda p, f: (0, p + first))
    page = pl.BlockSpec((slots, PAIR), lambda p, f: (0, p + first))
    target = pl.BlockSpec((rows, PAIR), lambda p, f: (0, p))
    page_target = pl.BlockSpec((slots, PAIR), lambda p, f: (0, p))
    totals = pl.BlockSpec((1, 2, rows), lambda p, f: (p + first, 0, 0))
    return pl.pallas_call(
        body,
        out_shape=[Shape((rows, pairs * PAIR), bf16)] + [Shape((slots, pairs * PAIR), bf16)] * 2,
        grid_spec=pltpu.PrefetchScalarGridSpec(
            num_scalar_prefetch=1,
            grid=(pairs,),
            in_specs=[source, page, page, source, totals, source],
            out_specs=[target, page_target, page_target],
            scratch_shapes=[pltpu.VMEM((PAIR, rows), f32)],
        ),
        cost_estimate=TINY,
        compiler_params=settings(),
        name="cross_backward",
    )(filled, *in_hbm(query, keys, values, out, total, grad))


def feed_forward(start_from, mixed, merge, cotangent, vectors, expand, bias, reduce, info, owners, begun):
    rows, width = start_from.shape
    hidden = expand.shape[1]
    block, tall = PIECE, 384
    steps, fine, others = hidden // block // 2, width // owners, owners // 2
    starts = range(0, rows, tall)
    final = begun is not None

    def body(info_ref, *refs):
        from_ref, mixed_ref, merge_ref, cot_ref, vec_ref, we_ref, be_ref, wr_ref = refs[:8]
        refs = refs[8:]
        if final:
            old_refs, refs = refs[:2], refs[2:]
            out_ref, two_ref, cross_ref, ms_ref, mo_ref = refs[:5]
            refs = refs[5:]
        else:
            new_refs, refs = refs[:3], refs[3:]
        rs_ref, ro_ref, es_ref, eo_ref, eb_ref, sums_ref = refs[:6]
        h, h_flip, g, branch, up, act, gp, sems = refs[6:14]
        after = from_ref if final else refs[14]
        step = pl.program_id(0)
        core, place, length = info_ref[0], info_ref[1], info_ref[2]

        def valid(start):
            row = lax.broadcasted_iota(jnp.int32, (tall, 1), 0) + (start + place)
            return (row < length).astype(f32)

        def copy(i):
            inside = (branch, up, after)[i]
            if final:
                return pltpu.make_async_copy(old_refs[i], inside, sems.at[i])
            return pltpu.make_async_copy(inside, new_refs[i], sems.at[i])

        @pl.when(step == 0)
        def _():
            if final:
                copy(0).start()
                copy(1).start()
            total = jnp.zeros((1, width), f32)
            for start in starts:
                at = pl.ds(start, tall)
                x = from_ref[at, :]
                if not final:
                    x = x + nn(mixed_ref[at, :], merge_ref[...]) + vec_ref[0:1, :]
                    after[at, :] = x
                    branch[at, :] = jnp.zeros((tall, width), f32)
                    up[at, :] = jnp.zeros((tall, width), f32)
                unit, _ = norm_unit(x)
                low = (unit * vec_ref[1:2, :] + vec_ref[2:3, :]).astype(bf16)
                h[at, :] = low
                h_flip[:, at] = low.T
                grad = (valid(start) * cot_ref[at, :].astype(f32)).astype(bf16)
                g[at, :] = grad
                total = total + column_sums(grad)
            sums_ref[...] = jnp.zeros_like(sums_ref)
            sums_ref[0:1, :] = total
            if final:
                copy(0).wait()
                copy(1).wait()
            else:
                copy(2).start()

        we, wr = we_ref[...], wr_ref[...]
        for start in starts:
            at = pl.ds(start, tall)
            low, slope = gelu_pair(nn(h[at, :], we) + be_ref[...])
            low = low.astype(bf16)
            act[at, :] = low
            branch[at, :] += nn(low, wr)
            grad = (nt(g[at, :], wr) * slope).astype(bf16)
            gp[at, :] = grad
            up[at, :] += nt(grad, we)
        if not final:
            @pl.when(step == steps - 1)
            def _():
                copy(0).start()
                copy(1).start()

        each = hidden // owners // fine
        for ref, one in zip(
            (rs_ref, ro_ref), by_core(core, tn(act[...], g[...]), hidden // owners, fine)
        ):
            ref[0], ref[1] = one[:, :each], one[:, each:]
        es_ref[...], eo_ref[...] = by_core(core, nn(h_flip[...], gp[...]), fine, fine)
        eb_ref[...] = nn(jnp.ones((8, rows), bf16), gp[...])

        @pl.when(step == steps - 1)
        def _():
            if not final:
                for i in range(3):
                    copy(i).wait()
                return
            gains = jnp.zeros((1, width), f32)
            shifts, merges = gains, gains
            for start in starts:
                at = pl.ds(start, tall)
                x, ok = after[at, :], valid(start)
                out_ref[at, :] = (ok * (x + branch[at, :] + vec_ref[3:4, :])).astype(bf16)
                unit, inverse = norm_unit(x)
                upstream = up[at, :]
                gains = gains + jnp.sum(upstream * unit, axis=0, keepdims=True)
                shifts = shifts + jnp.sum(upstream, axis=0, keepdims=True)
                pulled = norm_pull(upstream, unit, inverse, vec_ref[1:2, :])
                two = ok * cot_ref[at, :].astype(f32) + pulled
                two_ref[at, :] = two
                low = two.astype(bf16)
                g[at, :] = low
                merges = merges + column_sums(low)
                cross_ref[at, :] = nt(low, merge_ref[...]).astype(bf16)
            ms_ref[...], mo_ref[...] = by_core(core, tn(mixed_ref[...], g[...]), fine, fine)
            sums_ref[1:2, :], sums_ref[2:3, :], sums_ref[3:4, :] = gains, shifts, merges

    base = steps if final else 0

    def once(shape):
        return pl.BlockSpec(shape, lambda i, info: (0, 0), pipeline_mode=pl.Buffered(1))

    def fixed(shape):
        return pl.BlockSpec(shape, lambda i, info: (0,) * len(shape))

    each = hidden // owners // fine
    pairs = others // 2 // steps
    by_row = pl.BlockSpec((2, pairs, each, fine, PIECE), lambda i, info: (0, i, 0, 0, 0))
    by_column = pl.BlockSpec((others, 1, fine, PIECE), lambda i, info: (0, i, 0, 0))
    merged = (others, width // PIECE, fine, PIECE)
    hbm = pl.BlockSpec(memory_space=pltpu.HBM)
    full = (rows, width)
    shared_shapes = [
        *[Shape((2, others // 2, each, fine, PIECE), bf16)] * 2,
        *[Shape((others, steps, fine, PIECE), bf16)] * 2,
        Shape((8, hidden // 2), f32), Shape((8, width), f32),
    ]
    shared_specs = [
        by_row, by_row, by_column, by_column,
        pl.BlockSpec((8, block), lambda i, info: (0, i)), fixed((8, width)),
    ]
    if final:
        shapes = [Shape(full, bf16), Shape(full, f32), Shape(full, bf16), Shape(merged, bf16), Shape(merged, bf16)]
        specs = [fixed(full)] * 3 + [fixed(merged)] * 2
    else:
        shapes, specs = [Shape(full, f32)] * 3, [hbm] * 3
    return pl.pallas_call(
        body,
        out_shape=shapes + shared_shapes,
        grid_spec=pltpu.PrefetchScalarGridSpec(
            num_scalar_prefetch=1,
            grid=(steps,),
            in_specs=[
                once(full), once(full), once((width, width)), once(full), once((8, width)),
                pl.BlockSpec((width, block), lambda i, info: (0, base + i)),
                pl.BlockSpec((1, block), lambda i, info: (0, base + i)),
                pl.BlockSpec((block, width), lambda i, info: (base + i, 0)),
            ] + ([hbm] * 2 if final else []),
            out_specs=specs + shared_specs,
            scratch_shapes=[
                pltpu.VMEM(full, bf16), pltpu.VMEM((width, rows), bf16), pltpu.VMEM(full, bf16),
                pltpu.VMEM(full, f32), pltpu.VMEM(full, f32),
                pltpu.VMEM((rows, block), bf16), pltpu.VMEM((rows, block), bf16),
                pltpu.SemaphoreType.DMA((3,)),
            ] + ([] if final else [pltpu.VMEM(full, f32)]),
        ),
        cost_estimate=TINY,
        compiler_params=settings(60),
        name="feed_forward",
    )(
        info, *in_hbm(start_from, mixed, merge, cotangent), vectors,
        *in_hbm(expand), bias, *in_hbm(reduce), *(begun if final else ()),
    )


def streamed(name, body, info, inputs, outs, scratch=()):
    n, m = len(inputs), len(outs)

    def kernel(info_ref, *refs):
        ins, dests = refs[:n], refs[n : n + m]
        refs = refs[n + m :]
        held, made, refs = refs[:n], refs[n : n + m], refs[n + m :]
        in_sem, out_sem, *rest = refs
        loads = [pltpu.make_async_copy(ins[i], held[i], in_sem.at[i]) for i in range(n)]
        for load in loads:
            load.start()
        waited, stores = set(), {}

        def need(i):
            if i not in waited:
                loads[i].wait()
                waited.add(i)
            return held[i]

        def give(i, send=False):
            if send:
                stores[i] = pltpu.make_async_copy(made[i], dests[i], out_sem.at[i])
                stores[i].start()
            return made[i]

        body(info_ref, need, give, *rest)
        for i in range(m):
            stores[i].wait()

    anywhere = pl.BlockSpec(memory_space=pltpu.HBM)
    return pl.pallas_call(
        kernel,
        out_shape=[Shape(shape, kind) for shape, kind in outs],
        grid_spec=pltpu.PrefetchScalarGridSpec(
            num_scalar_prefetch=1,
            grid=(1,),
            in_specs=[anywhere] * n,
            out_specs=[anywhere] * m,
            scratch_shapes=[pltpu.VMEM(value.shape, value.dtype) for value in inputs]
            + [pltpu.VMEM(shape, kind) for shape, kind in outs]
            + [pltpu.SemaphoreType.DMA((n,)), pltpu.SemaphoreType.DMA((m,))]
            + list(scratch),
        ),
        cost_estimate=TINY,
        compiler_params=settings(60),
        name=name,
    )(info, *inputs)


def norm_project(name, info, tokens, weights, ways, vectors, keep):
    rows, width = tokens.shape
    n = len(weights)

    def body(info_ref, need, give):
        vec = need(1)
        for start in range(0, rows, 256):
            at = pl.ds(start, 256)
            unit, _ = norm_unit(need(0)[at, :].astype(f32))
            low = (unit * vec[0:1, :] + vec[1:2, :]).astype(bf16)
            if keep:
                give(n)[at, :] = low
            for i, (row, factor) in enumerate(ways):
                made = nn(low, need(2 + i)[...])
                if row is not None:
                    made = made + vec[row : row + 1, :]
                give(i)[at, :] = (made * factor).astype(bf16)
        for i in range(n + keep):
            give(i, True)

    return streamed(
        name, body, info, [tokens, vectors, *weights], [((rows, width), bf16)] * (n + keep),
    )


def output_project(info, mixed, tokens, output_weight, probe_weight, vectors):
    rows, width = tokens.shape

    def body(info_ref, need, give):
        vec = need(2)
        for start in range(0, rows, 256):
            at = pl.ds(start, 256)
            x = need(1)[at, :].astype(f32) + nn(need(0)[at, :], need(3)[...]) + vec[0:1, :]
            give(0)[at, :] = x
            unit, _ = norm_unit(x)
            low = (unit * vec[1:2, :] + vec[2:3, :]).astype(bf16)
            made = nn(low, need(4)[...]) + vec[3:4, :]
            give(1)[at, :] = (made * (HDIM**-0.5)).astype(bf16)
        give(0, True)
        give(1, True)

    return streamed(
        "output_project", body, info, [mixed, tokens, vectors, output_weight, probe_weight],
        [((rows, width), f32), ((rows, width), bf16)],
    )


def probe_backward(info, probe_low, probe_high, probe_weight, after_one, two, output_weight, mixed, vectors, owners):
    rows, width = after_one.shape
    half, tall, fine = width // 2, 256, width // owners

    def body(info_ref, need, give, hidden, low_grad):
        core = info_ref[0]
        left, right = need(0), need(1)
        weight = need(2)
        vec = need(7)
        x_ref, two_ref = need(3), need(4)
        gains = jnp.zeros((1, width), f32)
        shifts, outs = gains, gains
        for start in range(0, rows, tall):
            at = pl.ds(start, tall)
            up = nt(left[at, :], weight[:, :half]) + nt(right[at, :], weight[:, half:])
            unit, inverse = norm_unit(x_ref[at, :])
            hidden[at, :] = (unit * vec[0:1, :] + vec[1:2, :]).astype(bf16)
            gains = gains + jnp.sum(up * unit, axis=0, keepdims=True)
            shifts = shifts + jnp.sum(up, axis=0, keepdims=True)
            one = two_ref[at, :] + norm_pull(up, unit, inverse, vec[0:1, :])
            give(0)[at, :] = one
            low = one.astype(bf16)
            low_grad[at, :] = low
            outs = outs + column_sums(low)
            if start == 0:
                need(5)
            give(1)[at, :] = nt(low, need(5)[...]).astype(bf16)
        give(0, True)
        give(1, True)
        sums = give(4)
        sums[...] = jnp.zeros_like(sums)
        sums[0:1, :], sums[1:2, :], sums[2:3, :] = gains, shifts, outs
        sums[3:4, :half] = column_sums(left[...])
        sums[3:4, half:] = column_sums(right[...])
        give(4, True)
        mixed_ref = need(6)
        columns = (
            (0, 1, hidden, left[...]),
            (1, 2, hidden, right[...]),
            (2, 4, mixed_ref, low_grad[...]),
        )
        for begin, end, source, grads in columns:
            pair = by_core(core, tn(source[...], grads), fine, fine)
            give(2)[:, begin:end], give(3)[:, begin:end] = pair
        give(2, True)
        give(3, True)

    return streamed(
        "probe_backward",
        body,
        info,
        [probe_low, probe_high, probe_weight, after_one, two, output_weight, mixed, vectors],
        [
            ((rows, width), f32), ((rows, width), bf16),
            ((owners // 2, 4, fine, PIECE), bf16), ((owners // 2, 4, fine, PIECE), bf16),
            ((8, width), f32),
        ],
        [pltpu.VMEM((rows, width), bf16), pltpu.VMEM((rows, width), bf16)],
    )


def page_backward(
    info, key_low, key_high, value_low, value_high, page_rows, key_weight, value_weight, owners,
    patch_total,
):
    slots, width = page_rows.shape
    half, fine = width // 2, width // owners
    pieces = patch_total // owners // fine * (width // PIECE)

    def body(info_ref, need, give):
        core, page = info_ref[0], info_ref[3]
        kl, kh, vl, vh = need(0)[...], need(1)[...], need(2)[...], need(3)[...]
        rows_ref = need(4)
        for i, grads in enumerate((kl, kh, vl, vh)):
            pair = by_core(core, tn(rows_ref[...], grads), fine, fine)
            give(0)[:, i : i + 1], give(1)[:, i : i + 1] = pair
        wk, wv = need(5), need(6)
        total = nt(kl, wk[:, :half]) + nt(kh, wk[:, half:])
        total = total + nt(vl, wv[:, :half]) + nt(vh, wv[:, half:])
        pair = by_core(core, total, patch_total // owners, fine)
        each = pair[0].shape[0]
        at = pl.ds(pl.multiple_of(page * each, each), each)
        for which in range(2):
            give(which)[:, 4:] = jnp.zeros((owners // 2, pieces, fine, PIECE), bf16)
            give(which)[at, 4:] = pair[which]
            give(which, True)
        sums = give(2)
        sums[...] = jnp.zeros_like(sums)
        sums[0:1, :half] = column_sums(vl)
        sums[0:1, half:] = column_sums(vh)
        give(2, True)

    return streamed(
        "page_backward",
        body,
        info,
        [key_low, key_high, value_low, value_high, page_rows, key_weight, value_weight],
        [
            *[((owners // 2, 4 + pieces, fine, PIECE), bf16)] * 2, ((8, width), f32),
        ],
    )


def lead_upstream(info, keys, values, key_weight, value_weight, lead_tokens, vectors):
    rows, width = lead_tokens.shape
    half, tall = width // 2, 256

    def body(info_ref, need, give, hidden):
        kl, kh, vl, vh = need(0), need(1), need(2), need(3)
        wk, wv = need(4), need(5)
        x_ref, vec = need(6), need(7)
        gains = jnp.zeros((1, width), f32)
        shifts = gains
        for start in range(0, rows, tall):
            at = pl.ds(start, tall)
            up = nt(kl[at, :], wk[:, :half]) + nt(kh[at, :], wk[:, half:])
            up = up + nt(vl[at, :], wv[:, :half]) + nt(vh[at, :], wv[:, half:])
            give(0)[at, :] = up.astype(bf16)
            unit, _ = norm_unit(x_ref[at, :].astype(f32))
            hidden[at, :] = (unit * vec[0:1, :] + vec[1:2, :]).astype(bf16)
            gains = gains + jnp.sum(up * unit, axis=0, keepdims=True)
            shifts = shifts + jnp.sum(up, axis=0, keepdims=True)
        give(0, True)
        sums = give(2)
        sums[...] = jnp.zeros_like(sums)
        sums[0:1, :], sums[1:2, :] = gains, shifts
        sums[2:3, :half], sums[2:3, half:] = column_sums(vl[...]), column_sums(vh[...])
        give(2, True)
        for i, ref in enumerate((kl, kh, vl, vh)):
            give(1)[:, i * half : (i + 1) * half] = tn(hidden[...], ref[...]).astype(bf16)
        give(1, True)

    return streamed(
        "lead_upstream",
        body,
        info,
        [*keys, *values, key_weight, value_weight, lead_tokens, vectors],
        [((rows, width), bf16), ((width, 2 * width), bf16), ((8, width), f32)],
        [pltpu.VMEM((rows, width), bf16)],
    )


def projection_grads(info, hidden, query_grad, key_grad, value_grad, lead_part, high, owners):
    rows, width = hidden.shape
    half, fine = width // 2, width // owners
    column = half if high else 0

    def body(info_ref, need, give):
        core = info_ref[0]
        h = need(0)
        for i in range(3):
            total = tn(h[...], need(1 + i)[...])
            if i:
                base = (i - 1) * width + column
                total = total + need(4)[:, base : base + half].astype(f32)
            pair = by_core(core, total, fine, fine)
            give(0)[:, i : i + 1], give(1)[:, i : i + 1] = pair
        give(0, True)
        give(1, True)

    return streamed(
        "projection_grads",
        body,
        info,
        [hidden, query_grad, key_grad, value_grad, lead_part],
        [((owners // 2, 3, fine, PIECE), bf16)] * 2,
    )


def first_norm_backward(info, queries, keys, values, weights, tokens, one, returned, vectors):
    rows, width = tokens.shape
    half, tall = width // 2, 256

    def body(info_ref, need, give):
        grads = [need(i) for i in range(6)]
        vec = need(10)
        gains = jnp.zeros((1, width), f32)
        shifts = gains
        for start in range(0, rows, tall):
            at = pl.ds(start, tall)
            up = 0.0
            for i in range(3):
                up = up + nt(grads[2 * i][at, :], need(6 + i)[:, :half])
                up = up + nt(grads[2 * i + 1][at, :], need(6 + i)[:, half:])
            unit, inverse = norm_unit(need(9)[at, :].astype(f32))
            gains = gains + jnp.sum(up * unit, axis=0, keepdims=True)
            shifts = shifts + jnp.sum(up, axis=0, keepdims=True)
            up = up + need(12)[at, :].astype(f32)
            give(0)[at, :] = need(11)[at, :] + norm_pull(up, unit, inverse, vec[0:1, :])
        give(0, True)
        sums = give(1)
        sums[...] = jnp.zeros_like(sums)
        sums[0:1, :], sums[1:2, :] = gains, shifts
        sums[2:3, :half], sums[2:3, half:] = column_sums(grads[0][...]), column_sums(grads[1][...])
        sums[3:4, :half], sums[3:4, half:] = column_sums(grads[4][...]), column_sums(grads[5][...])
        give(1, True)

    return streamed(
        "first_norm_backward", body, info,
        [*queries, *keys, *values, *weights, tokens, vectors, one, returned],
        [((rows, width), f32), ((8, width), f32)],
    )


def digit_axes():
    patch_bits = lax.axis_size("patch").bit_length() - 1
    return [("tok", 0)] + [("patch", bit) for bit in reversed(range(patch_bits))]


def my_digit(axis, bit):
    return (lax.axis_index(axis) >> bit) & 1


def tied(*values):
    return lax.optimization_barrier(values)


FIRST_DIGIT = 4


class Gather:
    def __init__(self, block):
        every = digit_axes()
        self.order = every[-2:0:-1] + every[:1] + every[-1:]
        self.held, self.at = block[None], 2
        one, two = self.order[:2]
        self.arrived = [hop(self.held, steps) for steps in ([one], [two], [one, two])]

    def step(self, chain):
        chain, arrived = tied(chain, self.arrived)
        self.held = jnp.concatenate([self.held, *arrived], axis=0)
        if self.at < len(self.order):
            chain, self.held = tied(chain, self.held)
            self.arrived = [hop(self.held, self.order[self.at : self.at + 1])]
        self.at += 1
        return chain

    def rest(self, chain):
        while self.at <= len(self.order):
            chain = self.step(chain)
        return chain

    def places(self, first, count):
        digits = digit_axes()
        device = first + jnp.arange(count, dtype=jnp.int32)
        place = jnp.zeros((count,), jnp.int32)
        for i, one in enumerate(self.order):
            theirs = (device >> (len(digits) - 1 - digits.index(one))) & 1
            place = place | ((theirs ^ my_digit(*one)) << i)
        return place.astype(jnp.int32)


def page_forward(places, blocks, key_weight, value_weight, value_bias):
    count, (each, width) = places.shape[0], blocks.shape[1:]
    slots = count * each

    def body(place_ref, blocks_ref, wk_ref, wv_ref, bias_ref, rows_out, k_out, v_out, rows, wk, wv, k, v, sems):
        copies = [
            pltpu.make_async_copy(
                blocks_ref.at[place_ref[i]], rows.at[pl.ds(i * each, each)], sems.at[i]
            )
            for i in range(count)
        ]
        copies.append(pltpu.make_async_copy(wk_ref, wk, sems.at[count]))
        copies.append(pltpu.make_async_copy(wv_ref, wv, sems.at[count + 1]))
        for copy in copies:
            copy.start()
        for copy in copies[:-1]:
            copy.wait()
        stores = [pltpu.make_async_copy(rows, rows_out, sems.at[count + 2])]
        stores[0].start()
        k[...] = nn(rows[...], wk[...]).astype(bf16)
        stores.append(pltpu.make_async_copy(k, k_out, sems.at[count + 3]))
        stores[1].start()
        copies[-1].wait()
        v[...] = (nn(rows[...], wv[...]) + bias_ref[...]).astype(bf16)
        stores.append(pltpu.make_async_copy(v, v_out, sems.at[count + 4]))
        stores[2].start()
        for store in stores:
            store.wait()

    hbm = pl.BlockSpec(memory_space=pltpu.HBM)
    return pl.pallas_call(
        body,
        out_shape=[Shape((slots, width), bf16)] * 3,
        grid_spec=pltpu.PrefetchScalarGridSpec(
            num_scalar_prefetch=1,
            grid=(1,),
            in_specs=[hbm] * 3 + [pl.BlockSpec((1, width), lambda i, places: (0, 0))],
            out_specs=[hbm] * 3,
            scratch_shapes=[
                pltpu.VMEM((slots, width), bf16), pltpu.VMEM((width, width), bf16),
                pltpu.VMEM((width, width), bf16), pltpu.VMEM((slots, width), bf16),
                pltpu.VMEM((slots, width), bf16), pltpu.SemaphoreType.DMA((count + 5,)),
            ],
        ),
        cost_estimate=TINY,
        compiler_params=settings(),
        name="page_forward",
    )(places, blocks, key_weight, value_weight, value_bias)


class Part:
    def __init__(self, kept, tok_first, place, start=0, pieces=None):
        self.tok_first, self.place = tok_first, place
        self.pieces = pieces or kept.shape[1]
        self.terms = [(kept, owner_digits(), start)]


def owner_digits():
    return digit_axes()[:-1]


def stages_of(tok_first, direct):
    every = digit_axes()
    bits = every[-2:0:-1]
    loose, last = bits[: max(len(bits) - 2, 0)], bits[max(len(bits) - 2, 0) :]
    singles = [[one] for one in loose]
    ends = [last] if direct else [[one] for one in last]
    return ([every[:1]] + singles if tok_first else singles + [every[:1]]) + ends


class Sum:
    def __init__(self, direct, *sent):
        self.direct = direct
        self.parts = [part for _, parts in sent for part in parts]
        self.at = 0
        self.leaving = [array for array, _ in sent]
        self.hops = [[("patch", 0)]] * len(sent)
        self.groups = [parts for _, parts in sent]
        self.mine = self.came = None

    def send(self):
        self.arrived = [hop(value, steps) for value, steps in zip(self.leaving, self.hops)]

    def free(self, part, at):
        settled = [one for stage in stages_of(part.tok_first, self.direct)[:at] for one in stage]
        return [one for one in owner_digits() if one not in settled]

    def absorb(self, arrived):
        if self.mine is not None:
            self.came = arrived
            self.leaving = None
            return []
        for value, group in zip(arrived, self.groups):
            start = 0
            for part in group:
                part.terms = part.terms + [(value, self.free(part, self.at), start)]
                start += part.pieces
        stages = [stages_of(part.tok_first, self.direct) for part in self.parts]
        last = self.at == len(stages[0]) - 1
        ways = [stage[self.at] for stage in stages]
        self.at += 1
        jobs, self.hops, self.groups = [], [], []
        for digits in [way for i, way in enumerate(ways) if way not in ways[:i]]:
            group = [part for part, way in zip(self.parts, ways) if way == digits]
            free = self.free(group[0], self.at)
            for flips in range(0 if last else 1, 1 << len(digits)):
                flipped = [one for i, one in enumerate(digits) if flips >> i & 1]
                choices = []
                for chunk in range(1 << len(free)):
                    bits = {one: chunk >> (len(free) - 1 - i) & 1 for i, one in enumerate(free)}
                    choices.append((bits, flipped))
                terms = [(part.terms, part.pieces) for part in group]
                jobs.append((terms, choices, bf16 if flips else f32))
                if flips:
                    self.hops.append(flipped)
                    self.groups.append(group)
        return jobs

    def take(self, made):
        if self.at == len(stages_of(True, self.direct)):
            self.mine = made[0]
            made = made[1:]
        self.leaving = list(made)


def hop(value, steps):
    axis = steps[0][0]
    flip = sum(1 << bit for _, bit in steps)
    return lax.ppermute(value, axis, [(i, i ^ flip) for i in range(lax.axis_size(axis))])


def finished(shapes, *totals):
    arrays = [one for total in totals for one in [total.mine, *total.came]]

    def body(*refs):
        refs, outs = list(refs[: len(arrays)]), refs[len(arrays) :]
        for total in totals:
            mine_ref, *came = refs[: 1 + len(total.came)]
            refs = refs[1 + len(total.came) :]
            piece = 0
            for part in total.parts:
                out, at_column = part.place
                fine = mine_ref.shape[2]
                tall = shapes[out][0] // fine
                for p in range(part.pieces):
                    sum_here = mine_ref[0, piece]
                    for ref in came:
                        sum_here = sum_here + ref[0, piece].astype(f32)
                    row, column = p % tall * fine, at_column + p // tall * PIECE
                    outs[out][row : row + fine, column : column + PIECE] = sum_here
                    piece += 1

    return pl.pallas_call(
        body,
        out_shape=[Shape(shape, f32) for shape in shapes],
        cost_estimate=TINY,
        compiler_params=pltpu.CompilerParams(vmem_limit_bytes=40 * MIB),
        name="finished",
    )(*arrays)


def added_up(info, jobs):
    digits = digit_axes()
    arrays, known = [], {}
    for parts, _, _ in jobs:
        for terms, _ in parts:
            for value, _, _ in terms:
                if id(value) not in known:
                    known[id(value)] = len(arrays)
                    arrays.append(value)
    fine = arrays[0].shape[2]
    units = [(job, part) for job in range(len(jobs)) for part in range(len(jobs[job][0]))]
    loads = sum(len(jobs[job][0][part][0]) * len(jobs[job][1]) for job, part in units)

    def body(info_ref, *refs):
        n, m, k = len(arrays), len(jobs), len(units)
        ins, dests = refs[:n], refs[n : n + m]
        held, made = refs[n + m : n + m + k], refs[n + m + k : n + 2 * m + k]
        in_sem, out_sem = refs[n + 2 * m + k :]
        mine = {one: info_ref[FIRST_DIGIT + i] for i, one in enumerate(digits)}
        copies, count = [], 0
        for unit, (job, part) in enumerate(units):
            terms, pieces = jobs[job][0][part]
            copies.append([])
            for t, (value, free, start) in enumerate(terms):
                for c, (bits, flipped) in enumerate(jobs[job][1]):
                    index = 0
                    for one in free:
                        digit = bits[one] if one in bits else mine[one]
                        digit = 1 - digit if one in flipped else digit
                        index = 2 * index + digit
                    copy = pltpu.make_async_copy(
                        ins[known[id(value)]].at[index, pl.ds(start, pieces)],
                        held[unit].at[t, c],
                        in_sem.at[count],
                    )
                    copy.start()
                    copies[-1].append(copy)
                    count += 1
        offsets = [0] * m
        left = [len(jobs[job][0]) for job in range(m)]
        stores = []
        for unit, (job, part) in enumerate(units):
            terms, pieces = jobs[job][0][part]
            for copy in copies[unit]:
                copy.wait()
            offset = offsets[job]

            batch = max(one for one in range(1, 9) if pieces % one == 0)
            per = pieces // batch

            def step(i, _, unit=unit, job=job, count=len(terms), per=per, batch=batch, offset=offset):
                chunk = i // per
                for p in range(batch):
                    piece = i % per * batch + p
                    total = held[unit][0, chunk, piece].astype(f32)
                    for t in range(1, count):
                        total = total + held[unit][t, chunk, piece].astype(f32)
                    made[job][chunk, offset + piece] = total.astype(jobs[job][2])
                return 0

            lax.fori_loop(0, len(jobs[job][1]) * per, step, 0)
            offsets[job] += pieces
            left[job] -= 1
            if not left[job]:
                stores.append(pltpu.make_async_copy(made[job], dests[job], out_sem.at[job]))
                stores[-1].start()
        for store in stores:
            store.wait()

    anywhere = pl.BlockSpec(memory_space=pltpu.HBM)
    shapes = [
        ((len(choices), sum(pieces for _, pieces in parts), fine, PIECE), kind)
        for parts, choices, kind in jobs
    ]
    held = [
        pltpu.VMEM(
            (len(jobs[job][0][part][0]), len(jobs[job][1]), jobs[job][0][part][1], fine, PIECE), bf16
        )
        for job, part in units
    ]
    return pl.pallas_call(
        body,
        out_shape=[Shape(shape, kind) for shape, kind in shapes],
        grid_spec=pltpu.PrefetchScalarGridSpec(
            num_scalar_prefetch=1,
            grid=(1,),
            in_specs=[anywhere] * len(arrays),
            out_specs=[pl.BlockSpec(memory_space=pltpu.HBM)] * len(jobs),
            scratch_shapes=held
            + [pltpu.VMEM(shape, kind) for shape, kind in shapes]
            + [pltpu.SemaphoreType.DMA((loads,)), pltpu.SemaphoreType.DMA((len(jobs),))],
        ),
        cost_estimate=TINY,
        compiler_params=settings(60),
        name="added_up",
    )(info, *arrays)


def advance(info, chain, moving=(), fresh=()):
    moving = [one for one in moving if one.leaving is not None]
    chain, arrived = tied(chain, [one.arrived for one in moving])
    jobs, owners = [], []
    for one, values in zip(moving, arrived):
        new = one.absorb(values)
        owners.append((one, len(new)))
        jobs += new
    if jobs:
        made = added_up(info, jobs)
        for one, count in owners:
            if count:
                one.take(made[:count])
                made = made[count:]
    going = [one for one in moving + list(fresh) if one.leaving is not None]
    chain, leaving = tied(chain, [one.leaving for one in going])
    for one, values in zip(going, leaving):
        one.leaving = values
        one.send()
    return chain


def vector_table(feed, expand_bias, probe, page, lead, first):
    width = feed.shape[1]

    def body(feed_ref, bias_ref, probe_ref, page_ref, lead_ref, first_ref, out):
        rows = [
            first_ref[0:1, :] + lead_ref[0:1, :],
            first_ref[1:2, :] + lead_ref[1:2, :],
            first_ref[2:3, :],
            first_ref[3:4, :] + lead_ref[2:3, :],
            probe_ref[2:3, :],
            probe_ref[0:1, :],
            probe_ref[1:2, :],
            probe_ref[3:4, :],
            page_ref[0:1, :],
            feed_ref[3:4, :],
            feed_ref[1:2, :],
            feed_ref[2:3, :],
            feed_ref[0:1, :],
        ]
        out[...] = jnp.zeros_like(out)
        for i, row in enumerate(rows):
            out[i : i + 1, :] = row
        out[16 : 16 + bias_ref.shape[0], :] = bias_ref[...]

    return pl.pallas_call(
        body,
        out_shape=jax.ShapeDtypeStruct((24, width), f32),
        cost_estimate=TINY,
        name="vector_table",
    )(feed, expand_bias, probe, page, lead, first)


def scatter_rows(table, width, first, last):
    digits = digit_axes()
    fine = width >> len(digits)
    for axis, bit in digits[first:last]:
        half = table.shape[1] // 2
        if half % LANES:
            table = table + hop(table, [(axis, bit)])
        else:
            digit = my_digit(axis, bit)
            keep = lax.dynamic_slice_in_dim(table, digit * half, half, 1)
            give = lax.dynamic_slice_in_dim(table, (1 - digit) * half, half, 1)
            table = keep + hop(give, [(axis, bit)])
    if last < len(digits):
        return table
    inside = 0
    for axis, bit in digits[(table.shape[1] // fine).bit_length() * -1 + 1 :]:
        inside = 2 * inside + my_digit(axis, bit)
    return lax.dynamic_slice_in_dim(table, inside * fine, fine, 1)


def pick_entry(table, position):
    indices = jnp.arange(table.shape[0], dtype=jnp.int32)
    return jnp.sum(jnp.where(indices == position, table, 0))


def rows_of(*vectors):
    rows = jnp.stack(vectors, axis=0)
    return jnp.pad(rows, ((0, 8 - len(vectors)), (0, 0)))


def local(
    tokens,
    patches,
    cotangent,
    lengths,
    page_of,
    page_counts,
    self_gain,
    self_shift,
    query_weight,
    query_bias,
    key_weight,
    value_weight,
    value_bias,
    output_weight,
    output_bias,
    cross_gain,
    cross_shift,
    probe_weight,
    probe_bias,
    source_key,
    source_value,
    source_bias,
    merge_weight,
    merge_bias,
    feed_gain,
    feed_shift,
    expand_weight,
    expand_bias,
    reduce_weight,
    reduce_bias,
):
    head_scale = HDIM ** (-0.5)
    tok_index = lax.axis_index("tok").astype(jnp.int32)
    sequence = lax.axis_index("patch")
    core = my_digit("patch", 0).astype(jnp.int32)
    row_count, model_width = tokens.shape[1:]
    lead_tokens = lax.ppermute(tokens[0], "tok", [(0, 1)])
    page_index = pick_entry(page_of, sequence)
    filled = pick_entry(page_counts, page_index).reshape(1)
    trailing = tok_index.reshape(1)
    page_start = page_index * PAGE_SLOTS
    digits = [my_digit(*one).astype(jnp.int32) for one in digit_axes()]
    owners = 1 << len(digits)
    info = jnp.stack(
        [core, tok_index * row_count, pick_entry(lengths, sequence), page_index] + digits
    )
    self_vectors = rows_of(self_gain, self_shift, query_bias, value_bias)
    cross_vectors = rows_of(cross_gain, cross_shift)
    output_vectors = rows_of(output_bias, cross_gain, cross_shift, probe_bias)
    feed_vectors = rows_of(merge_bias, feed_gain, feed_shift, reduce_bias)

    gather = Gather(patches)
    nothing = jnp.zeros((1,), jnp.int32)
    query, own_keys, own_values, hidden_one = norm_project(
        "own_project", nothing, tokens[0], [query_weight, key_weight, value_weight],
        [(2, head_scale), (None, 1.0), (3, 1.0)], self_vectors, True,
    )
    query = gather.step(query)
    own_mixed, own_total = own_forward(query, own_keys, own_values)
    lead_tokens, own_mixed = gather.step((lead_tokens, own_mixed))
    lead_keys, lead_values = norm_project(
        "lead_project", nothing, lead_tokens, [key_weight, value_weight],
        [(None, 1.0), (3, 1.0)], self_vectors, False,
    )
    self_mixed, self_total = lead_forward(
        query, lead_keys, lead_values, own_mixed, own_total, trailing
    )
    self_mixed = gather.step(self_mixed)
    after_one, probe = output_project(
        nothing, self_mixed, tokens[0], output_weight, probe_weight, output_vectors
    )
    probe = gather.rest(probe)
    page_rows, page_keys, page_values = page_forward(
        gather.places(page_start // patches.shape[0], PAGE_SLOTS // patches.shape[0]),
        gather.held, source_key, source_value, source_bias[None],
    )
    cross_mixed, cross_total = cross_forward(probe, page_keys, page_values, filled)

    feed_args = (
        cross_mixed, merge_weight, cotangent[0], feed_vectors, expand_weight, expand_bias[None],
        reduce_weight, info, owners,
    )
    branch, upstream, after_two, *fed = feed_forward(after_one, *feed_args, None)
    fine = model_width // owners
    deep = expand_weight.shape[1] // 2

    def by_owner(value):
        return value.reshape((-1,) + value.shape[2:])

    first = Sum(
        False,
        (fed[2], [Part(fed[3], True, (0, 0))]),
        (by_owner(fed[0]), [Part(by_owner(fed[1]), False, (1, 0))]),
    )
    low_bias, low_sums = fed[4:]
    after_two, branch, upstream = advance(info, (after_two, branch, upstream), [], [first])
    block_output, grad_two, grad_cross_out, *fed = feed_forward(
        after_two, *feed_args, (branch, upstream)
    )
    second = Sum(
        False,
        (fed[4], [Part(fed[5], True, (0, deep))]),
        (by_owner(fed[2]), [Part(by_owner(fed[3]), False, (2, 0))]),
        (fed[0], [Part(fed[1], False, (3, 0))]),
    )
    expand_bias_sums = jnp.concatenate([low_bias[0], fed[6][0]])
    feed_sums = fed[7]

    half_pairs = model_width // PAIR // 2
    cross_args = (probe, page_keys, page_values, cross_mixed, cross_total)
    grad_cross_out = advance(info, grad_cross_out, [first], [second])
    low = cross_backward(*cross_args, grad_cross_out, filled, 0, half_pairs)
    low, grad_cross_out = advance(info, (low, grad_cross_out), [second])
    high = cross_backward(*cross_args, grad_cross_out, filled, half_pairs, half_pairs)
    low, high = advance(info, (low, high), [first])
    patch_total = patches.shape[0] * lax.axis_size(("tok", "patch"))
    paged = page_backward(
        info, low[1], high[1], low[2], high[2], page_rows, source_key, source_value, owners,
        patch_total,
    )
    probed = probe_backward(
        info, low[0], high[0], probe_weight, after_one, grad_two, output_weight, self_mixed,
        cross_vectors, owners,
    )
    grad_one, grad_self_out, probe_sums = probed[0], probed[1], probed[4]
    third = Sum(
        False,
        (
            paged[0],
            [Part(paged[1], True, (0, 0), 0, 4), Part(paged[1], False, (1, 0), 4, paged[1].shape[1] - 4)],
        ),
        (probed[2], [Part(probed[3], False, (2, 0))]),
    )
    self_args = (query, lead_keys, lead_values, self_mixed, self_total)
    own_args = (query, own_keys, own_values, self_mixed, self_total)
    grad_self_out = advance(info, grad_self_out, [first, second], [third])
    lead_low = lead_backward(*self_args, grad_self_out, trailing, 0, half_pairs)
    lead_low, grad_self_out = advance(info, (lead_low, grad_self_out), [first, second, third])
    lead_high = lead_backward(*self_args, grad_self_out, trailing, half_pairs, half_pairs)
    led_grad, led_part, lead_sums = lead_upstream(
        info, (lead_low[1], lead_high[1]), (lead_low[2], lead_high[2]), key_weight,
        value_weight, lead_tokens, self_vectors,
    )
    led_grad, led_part, grad_self_out = advance(
        info, (led_grad, led_part, grad_self_out), [first, second, third]
    )
    returned = lax.ppermute(led_grad, "tok", [(1, 0)])
    own_low = own_backward(*own_args, grad_self_out, lead_low[0], 0, half_pairs)
    own_low, grad_self_out = advance(info, (own_low, grad_self_out), [second, third])
    parts = projection_grads(info, hidden_one, *own_low, led_part, False, owners)
    half = model_width // 2
    fourth = Sum(False, (parts[0], [Part(parts[1], i == 1, (i, 0), i, 1) for i in range(3)]))
    own_low, grad_self_out = advance(info, (own_low, grad_self_out), [], [fourth])
    own_high = own_backward(*own_args, grad_self_out, lead_high[0], half_pairs, half_pairs)
    own_low, own_high, returned = advance(
        info, (own_low, own_high, returned), [third, fourth]
    )
    tokens_grad, first_sums = first_norm_backward(
        info, (own_low[0], own_high[0]), (own_low[1], own_high[1]), (own_low[2], own_high[2]),
        (query_weight, key_weight, value_weight), tokens[0], grad_one, returned, self_vectors,
    )
    first_sums, own_high, led_part = advance(
        info, (first_sums, own_high, led_part), [third, fourth]
    )
    parts = projection_grads(info, hidden_one, *own_high, led_part, True, owners)
    bias_rows = expand_bias_sums.reshape(owners, -1, fine)
    bias_rows = jnp.transpose(bias_rows, (1, 0, 2)).reshape(-1, model_width)
    table = vector_table(feed_sums, bias_rows, probe_sums, paged[2], lead_sums, first_sums)
    table = scatter_rows(table, model_width, 0, 1)
    fifth = Sum(True, (parts[0], [Part(parts[1], i != 1, (i, half), i, 1) for i in range(3)]))
    table = advance(info, table, [fourth], [fifth])
    table = scatter_rows(table, model_width, 1, 2)
    table = advance(info, table, [fourth, fifth])
    table = scatter_rows(table, model_width, 2, 3)
    table = advance(info, table, [fourth, fifth])
    table = scatter_rows(table, model_width, 3, len(digits) - 1)
    table = advance(info, table, [fourth, fifth])
    sums = scatter_rows(table, model_width, len(digits) - 1, len(digits))
    totals = [first, second, third, fourth, fifth]
    while any(one.leaving is not None for one in totals):
        sums = advance(info, sums, totals)
    tall = expand_weight.shape[1] // owners
    model, half_reduce = (fine, model_width), (tall, half)
    expand_grad, reduce_low, reduce_high, merge_grad = finished(
        [(fine, expand_weight.shape[1]), half_reduce, half_reduce, model], first, second
    )
    is_first = tok_index == 0
    given = jnp.where(is_first, reduce_high, reduce_low).astype(bf16)
    taken = hop(given, [("tok", 0)]).astype(f32)
    reduce_grad = jnp.concatenate(
        [jnp.where(is_first, reduce_low, taken), jnp.where(is_first, taken, reduce_high)], axis=1
    )
    source_grads, patches_grad, middle_grads = finished(
        [(fine, 2 * model_width), (patches.shape[0], model_width), (fine, 2 * model_width)], third
    )
    projections = finished([model] * 3, fourth, fifth)
    return (
        block_output[None],
        tokens_grad[None],
        patches_grad,
        sums[0],
        sums[1],
        projections[0],
        sums[2],
        projections[1],
        projections[2],
        sums[3],
        middle_grads[:, model_width:],
        sums[4],
        sums[5],
        sums[6],
        middle_grads[:, :model_width],
        sums[7],
        source_grads[:, :model_width],
        source_grads[:, model_width:],
        sums[8],
        merge_grad,
        sums[9],
        sums[10],
        sums[11],
        expand_grad,
        sums[16 : 16 + expand_bias.shape[0] // model_width].reshape(-1),
        reduce_grad,
        sums[12],
    )


def solution(mesh):
    placed = (
        P("patch", "tok", None),
        P(("tok", "patch"), None),
        P("patch", "tok", None),
        P(),
        P(),
        P(),
        P(),
        P(),
        P(),
        P(),
        P(),
        P(),
        P(),
        P(),
        P(),
        P(),
        P(),
        P(),
        P(),
        P(),
        P(),
        P(),
        P(),
        P(),
        P(),
        P(),
        P(),
        P(),
        P(),
        P(),
    )
    return jax.shard_map(
        local,
        mesh=mesh,
        in_specs=placed,
        out_specs=(
            P("patch", "tok", None),
            P("patch", "tok", None),
            P(("tok", "patch"), None),
            P(("tok", "patch")),
            P(("tok", "patch")),
            P(("tok", "patch"), None),
            P(("tok", "patch")),
            P(("tok", "patch"), None),
            P(("tok", "patch"), None),
            P(("tok", "patch")),
            P(("tok", "patch"), None),
            P(("tok", "patch")),
            P(("tok", "patch")),
            P(("tok", "patch")),
            P(("tok", "patch"), None),
            P(("tok", "patch")),
            P(("tok", "patch"), None),
            P(("tok", "patch"), None),
            P(("tok", "patch")),
            P(("tok", "patch"), None),
            P(("tok", "patch")),
            P(("tok", "patch")),
            P(("tok", "patch")),
            P(("tok", "patch"), None),
            P(("tok", "patch")),
            P(("tok", "patch"), None),
            P(("tok", "patch")),
        ),
        check_vma=False,
    )
```

```python
import jax
import jax.numpy as jnp
from jax import lax
from jax.experimental import pallas as pl
from jax.experimental.pallas import tpu as pltpu
from jax.sharding import PartitionSpec as P

HDIM = 64
PAIR = 2 * HDIM
PAGE_SLOTS = 512
NEG_FILL = -1e30
EPS_NORM = 1e-05
LANES = 128
PIECE = 512
HIGH = lax.Precision.HIGHEST
MIB = 1 << 20
bf16, f32 = jnp.bfloat16, jnp.float32
Shape = pltpu.HBM


def nn(left, right):
    return lax.dot_general(
        left, right, (((1,), (0,)), ((), ())), preferred_element_type=f32
    )


def nt(left, right, precision=None):
    return lax.dot_general(
        left, right, (((1,), (1,)), ((), ())), precision=precision, preferred_element_type=f32
    )


def tn(left, right):
    return lax.dot_general(
        left, right, (((0,), (0,)), ((), ())), preferred_element_type=f32
    )


def column_sums(values):
    return jnp.sum(values.astype(f32), axis=0, keepdims=True)


def norm_unit(values):
    average = jnp.mean(values, axis=-1, keepdims=True)
    centred = values - average
    spread = jnp.mean(centred * centred, axis=-1, keepdims=True)
    inverse = lax.rsqrt(spread + EPS_NORM)
    return centred * inverse, inverse


def norm_pull(upstream, unit, inverse, gain):
    scaled = upstream * gain
    centred = scaled - jnp.mean(scaled, axis=-1, keepdims=True)
    centred = centred - unit * jnp.mean(scaled * unit, axis=-1, keepdims=True)
    return centred * inverse


def gelu_pair(values):
    share = 0.5 * (1.0 + lax.erf(values * (2.0**-0.5)))
    slope = share + values * (jnp.exp(-0.5 * values * values) * 0.3989422804014327)
    return values * share, slope


def by_core(core, value, each, fine):
    count, width = value.shape
    split = value.reshape(count // (2 * each), 2, each, width)
    found = []
    for own in range(2):
        one = jnp.where((core == 0) == (own == 0), split[:, 1], split[:, 0])
        one = one.reshape(count // (2 * each), each // fine, fine, width)
        columns = [one[..., at : at + PIECE] for at in range(0, width, PIECE)]
        one = columns[0] if len(columns) == 1 else jnp.concatenate(columns, axis=1)
        found.append(one.astype(bf16))
    return found


def head_lanes(head):
    lane = lax.broadcasted_iota(jnp.int32, (1, PAIR), 1)
    return (lane >= head * HDIM) & (lane < (head + 1) * HDIM)


def only(value, head):
    return jnp.where(head_lanes(head), value, jnp.zeros_like(value))


TINY = pl.CostEstimate(flops=1, bytes_accessed=1, transcendentals=0)


def settings(limit=48):
    return pltpu.CompilerParams(
        dimension_semantics=("arbitrary",), vmem_limit_bytes=limit * MIB
    )


def in_hbm(*values):
    return [pltpu.with_memory_space_constraint(value, pltpu.HBM) for value in values]


def scores_of(key_rows, query, start, mask):
    score = nt(key_rows, query[start:])
    if isinstance(mask, str):
        rows = score.shape[0]
        row = lax.broadcasted_iota(jnp.int32, (rows, rows), 0)
        column = lax.broadcasted_iota(jnp.int32, (rows, rows), 1)
        corner = jnp.where(row <= column, score[:, :rows], NEG_FILL)
        if score.shape[1] == rows:
            return corner
        return jnp.concatenate([corner, score[:, rows:]], axis=1)
    return score if mask is None else score + mask


def from_start(whole, start, part, combine):
    if whole is None:
        return part
    if start == 0:
        return combine(whole, part)
    return jnp.concatenate([whole[:, :start], combine(whole[:, start:], part)], axis=1)


def forward_pair(q_ref, k_ref, v_ref, blocks, begun, out_ref, total_ref):
    values = v_ref[...].T
    outs = []
    for head in range(2):
        lanes = slice(head * HDIM, (head + 1) * HDIM)
        query = only(q_ref[...], head)
        earlier = None if begun is None else begun[1][0, head : head + 1, :]
        row_max, scores = None, []
        for first, rows, start, mask in blocks:
            score = scores_of(k_ref[pl.ds(first, rows), :], query, start, mask)
            row_max = from_start(row_max, start, score.max(0, keepdims=True), jnp.maximum)
            scores.append(score)
        if begun is not None:
            row_max = jnp.maximum(row_max, earlier)
        total, out = None, None
        for score, (first, rows, start, _) in zip(scores, blocks):
            exponent = jnp.exp(score - row_max[:, start:])
            total = from_start(total, start, exponent.sum(0, keepdims=True), jnp.add)
            part = nn(values[lanes, first : first + rows], exponent.astype(bf16))
            out = from_start(out, start, part, jnp.add)
        if begun is not None:
            share = jnp.exp(earlier - row_max)
            total = total + share
            out = out + begun[0][lanes] * share
        outs.append(out / total)
        total_ref[0, head : head + 1, :] = row_max + jnp.log(total)
    out_ref[...] = jnp.concatenate(outs, axis=0).T.astype(bf16)


def backward_pair(q_ref, k_ref, v_ref, out_ref, total_ref, g_ref, blocks, acc, fresh, dk_ref, dv_ref):
    queries, upstreams, keys = q_ref[...].T, g_ref[...].T, k_ref[...].T
    product = upstreams.astype(f32) * out_ref[...].T.astype(f32)
    for first, rows, start, mask in blocks:
        key_rows, value_rows = k_ref[pl.ds(first, rows), :], v_ref[pl.ds(first, rows), :]
        key_grads, value_grads = [], []
        for head in range(2):
            lanes = slice(head * HDIM, (head + 1) * HDIM)
            inner = product[lanes, start:].sum(0, keepdims=True)
            score = scores_of(key_rows, only(q_ref[...], head), start, mask)
            soft = jnp.exp(score - total_ref[0, head : head + 1, start:])
            grad_soft = nt(value_rows, only(g_ref[...], head)[start:])
            grad_score = (soft * (grad_soft - inner)).astype(bf16)
            value_grads.append(nt(upstreams[lanes, start:], soft.astype(bf16)))
            key_grads.append(nt(queries[lanes, start:], grad_score))
            part = nn(keys[lanes, first : first + rows], grad_score)
            if fresh and first == 0:
                acc[lanes, start:] = part
            else:
                acc[lanes, start:] += part
        dk_ref[pl.ds(first, rows), :] = jnp.concatenate(key_grads, axis=0).T.astype(bf16)
        dv_ref[pl.ds(first, rows), :] = jnp.concatenate(value_grads, axis=0).T.astype(bf16)


def causal_blocks(rows, size=256):
    return [(at, size, at, "causal") for at in range(0, rows, size)]


def totals_shape(rows, width):
    return (width // PAIR, 2, rows)


def own_forward(query, keys, values):
    rows, width = query.shape

    def body(q_ref, k_ref, v_ref, out_ref, total_ref):
        forward_pair(q_ref, k_ref, v_ref, causal_blocks(rows), None, out_ref, total_ref)

    block = pl.BlockSpec((rows, PAIR), lambda p: (0, p))
    total = pl.BlockSpec((1, 2, rows), lambda p: (p, 0, 0))
    return pl.pallas_call(
        body,
        out_shape=(Shape((rows, width), bf16), Shape(totals_shape(rows, width), f32)),
        grid=(width // PAIR,),
        in_specs=[block] * 3,
        out_specs=[block, total],
        cost_estimate=TINY,
        compiler_params=settings(),
        name="own_forward",
    )(*in_hbm(query, keys, values))


def lead_forward(query, keys, values, begun, begun_total, trailing):
    rows, width = query.shape

    def body(flag, q_ref, k_ref, v_ref, begun_ref, old_ref, out_ref, total_ref):
        @pl.when(flag[0] == 1)
        def _():
            begun = (begun_ref[...].T.astype(f32), old_ref)
            blocks = [(0, rows, 0, None)]
            forward_pair(q_ref, k_ref, v_ref, blocks, begun, out_ref, total_ref)

        @pl.when(flag[0] == 0)
        def _():
            out_ref[...] = begun_ref[...]
            total_ref[...] = old_ref[...]

    block = pl.BlockSpec((rows, PAIR), lambda p, flag: (0, p))
    total = pl.BlockSpec((1, 2, rows), lambda p, flag: (p, 0, 0))
    return pl.pallas_call(
        body,
        out_shape=(Shape((rows, width), bf16), Shape(totals_shape(rows, width), f32)),
        grid_spec=pltpu.PrefetchScalarGridSpec(
            num_scalar_prefetch=1,
            grid=(width // PAIR,),
            in_specs=[block] * 4 + [total],
            out_specs=[block, total],
        ),
        cost_estimate=TINY,
        compiler_params=settings(),
        name="lead_forward",
    )(trailing, *in_hbm(query, keys, values, begun, begun_total))


def slot_bias(filled_ref, slots):
    slot = lax.broadcasted_iota(jnp.int32, (slots, 1), 0)
    return jnp.where(slot < filled_ref[0], 0.0, NEG_FILL)


def cross_forward(query, keys, values, filled):
    rows, width = query.shape
    slots = keys.shape[0]

    def body(filled_ref, q_ref, k_ref, v_ref, out_ref, total_ref):
        blocks = [(0, slots, 0, slot_bias(filled_ref, slots))]
        forward_pair(q_ref, k_ref, v_ref, blocks, None, out_ref, total_ref)

    block = pl.BlockSpec((rows, PAIR), lambda p, f: (0, p))
    page = pl.BlockSpec((slots, PAIR), lambda p, f: (0, p))
    total = pl.BlockSpec((1, 2, rows), lambda p, f: (p, 0, 0))
    return pl.pallas_call(
        body,
        out_shape=(Shape((rows, width), bf16), Shape(totals_shape(rows, width), f32)),
        grid_spec=pltpu.PrefetchScalarGridSpec(
            num_scalar_prefetch=1,
            grid=(width // PAIR,),
            in_specs=[block, page, page],
            out_specs=[block, total],
        ),
        cost_estimate=TINY,
        compiler_params=settings(),
        name="cross_forward",
    )(filled, *in_hbm(query, keys, values))


def lead_backward(query, keys, values, out, total, grad, trailing, first, pairs, size=384):
    rows = query.shape[0]

    def body(flag, q_ref, k_ref, v_ref, out_ref, total_ref, g_ref, dq_ref, dk_ref, dv_ref):
        @pl.when(flag[0] == 1)
        def _():
            blocks = [(at, size, 0, None) for at in range(0, rows, size)]
            backward_pair(
                q_ref, k_ref, v_ref, out_ref, total_ref, g_ref, blocks, dq_ref, True, dk_ref, dv_ref
            )

        @pl.when(flag[0] == 0)
        def _():
            for ref in (dq_ref, dk_ref, dv_ref):
                ref[...] = jnp.zeros_like(ref)

    source = pl.BlockSpec((rows, PAIR), lambda p, flag: (0, p + first))
    target = pl.BlockSpec((rows, PAIR), lambda p, flag: (0, p))
    totals = pl.BlockSpec((1, 2, rows), lambda p, flag: (p + first, 0, 0))
    return pl.pallas_call(
        body,
        out_shape=[Shape((pairs * PAIR, rows), f32)] + [Shape((rows, pairs * PAIR), bf16)] * 2,
        grid_spec=pltpu.PrefetchScalarGridSpec(
            num_scalar_prefetch=1,
            grid=(pairs,),
            in_specs=[source] * 4 + [totals, source],
            out_specs=[pl.BlockSpec((PAIR, rows), lambda p, flag: (p, 0)), target, target],
        ),
        cost_estimate=TINY,
        compiler_params=settings(),
        name="lead_backward",
    )(trailing, *in_hbm(query, keys, values, out, total, grad))


def own_backward(query, keys, values, out, total, grad, begun, first, pairs):
    rows = query.shape[0]

    def body(q_ref, k_ref, v_ref, out_ref, total_ref, g_ref, begun_ref, dq_ref, dk_ref, dv_ref, acc):
        acc[...] = begun_ref[...]
        backward_pair(
            q_ref, k_ref, v_ref, out_ref, total_ref, g_ref, causal_blocks(rows), acc, False,
            dk_ref, dv_ref,
        )
        dq_ref[...] = (acc[...] * (HDIM**-0.5)).T.astype(bf16)

    source = pl.BlockSpec((rows, PAIR), lambda p: (0, p + first))
    target = pl.BlockSpec((rows, PAIR), lambda p: (0, p))
    totals = pl.BlockSpec((1, 2, rows), lambda p: (p + first, 0, 0))
    return pl.pallas_call(
        body,
        out_shape=[Shape((rows, pairs * PAIR), bf16)] * 3,
        grid=(pairs,),
        in_specs=[source] * 4 + [totals, source, pl.BlockSpec((PAIR, rows), lambda p: (p, 0))],
        out_specs=[target] * 3,
        scratch_shapes=[pltpu.VMEM((PAIR, rows), f32)],
        cost_estimate=TINY,
        compiler_params=settings(),
        name="own_backward",
    )(*in_hbm(query, keys, values, out, total, grad, begun))


def cross_backward(query, keys, values, out, total, grad, filled, first, pairs):
    rows, slots = query.shape[0], keys.shape[0]

    def body(
        filled_ref, q_ref, k_ref, v_ref, out_ref, total_ref, g_ref, dq_ref, dk_ref, dv_ref, acc
    ):
        blocks = [(0, slots, 0, slot_bias(filled_ref, slots))]
        backward_pair(
            q_ref, k_ref, v_ref, out_ref, total_ref, g_ref, blocks, acc, True, dk_ref, dv_ref
        )
        dq_ref[...] = (acc[...] * (HDIM**-0.5)).T.astype(bf16)

    source = pl.BlockSpec((rows, PAIR), lambda p, f: (0, p + first))
    page = pl.BlockSpec((slots, PAIR), lambda p, f: (0, p + first))
    target = pl.BlockSpec((rows, PAIR), lambda p, f: (0, p))
    page_target = pl.BlockSpec((slots, PAIR), lambda p, f: (0, p))
    totals = pl.BlockSpec((1, 2, rows), lambda p, f: (p + first, 0, 0))
    return pl.pallas_call(
        body,
        out_shape=[Shape((rows, pairs * PAIR), bf16)] + [Shape((slots, pairs * PAIR), bf16)] * 2,
        grid_spec=pltpu.PrefetchScalarGridSpec(
            num_scalar_prefetch=1,
            grid=(pairs,),
            in_specs=[source, page, page, source, totals, source],
            out_specs=[target, page_target, page_target],
            scratch_shapes=[pltpu.VMEM((PAIR, rows), f32)],
        ),
        cost_estimate=TINY,
        compiler_params=settings(),
        name="cross_backward",
    )(filled, *in_hbm(query, keys, values, out, total, grad))


def feed_forward(start_from, mixed, merge, cotangent, vectors, expand, bias, reduce, info, owners, begun):
    rows, width = start_from.shape
    hidden = expand.shape[1]
    block, tall = PIECE, 384
    steps, fine, others = hidden // block // 2, width // owners, owners // 2
    starts = range(0, rows, tall)
    final = begun is not None

    def body(info_ref, *refs):
        from_ref, mixed_ref, merge_ref, cot_ref, vec_ref, we_ref, be_ref, wr_ref = refs[:8]
        refs = refs[8:]
        if final:
            old_refs, refs = refs[:2], refs[2:]
            out_ref, two_ref, cross_ref, ms_ref, mo_ref = refs[:5]
            refs = refs[5:]
        else:
            new_refs, refs = refs[:3], refs[3:]
        rs_ref, ro_ref, es_ref, eo_ref, eb_ref, sums_ref = refs[:6]
        h, h_flip, g, branch, up, act, gp, sems = refs[6:14]
        after = from_ref if final else refs[14]
        step = pl.program_id(0)
        core, place, length = info_ref[0], info_ref[1], info_ref[2]

        def valid(start):
            row = lax.broadcasted_iota(jnp.int32, (tall, 1), 0) + (start + place)
            return (row < length).astype(f32)

        def copy(i):
            inside = (branch, up, after)[i]
            if final:
                return pltpu.make_async_copy(old_refs[i], inside, sems.at[i])
            return pltpu.make_async_copy(inside, new_refs[i], sems.at[i])

        @pl.when(step == 0)
        def _():
            if final:
                copy(0).start()
                copy(1).start()
            total = jnp.zeros((1, width), f32)
            for start in starts:
                at = pl.ds(start, tall)
                x = from_ref[at, :]
                if not final:
                    x = x + nn(mixed_ref[at, :], merge_ref[...]) + vec_ref[0:1, :]
                    after[at, :] = x
                    branch[at, :] = jnp.zeros((tall, width), f32)
                    up[at, :] = jnp.zeros((tall, width), f32)
                unit, _ = norm_unit(x)
                low = (unit * vec_ref[1:2, :] + vec_ref[2:3, :]).astype(bf16)
                h[at, :] = low
                h_flip[:, at] = low.T
                grad = (valid(start) * cot_ref[at, :].astype(f32)).astype(bf16)
                g[at, :] = grad
                total = total + column_sums(grad)
            sums_ref[...] = jnp.zeros_like(sums_ref)
            sums_ref[0:1, :] = total
            if final:
                copy(0).wait()
                copy(1).wait()
            else:
                copy(2).start()

        we, wr = we_ref[...], wr_ref[...]
        for start in starts:
            at = pl.ds(start, tall)
            low, slope = gelu_pair(nn(h[at, :], we) + be_ref[...])
            low = low.astype(bf16)
            act[at, :] = low
            branch[at, :] += nn(low, wr)
            grad = (nt(g[at, :], wr) * slope).astype(bf16)
            gp[at, :] = grad
            up[at, :] += nt(grad, we)
        if not final:
            @pl.when(step == steps - 1)
            def _():
                copy(0).start()
                copy(1).start()

        each = hidden // owners // fine
        for ref, one in zip(
            (rs_ref, ro_ref), by_core(core, tn(act[...], g[...]), hidden // owners, fine)
        ):
            ref[0], ref[1] = one[:, :each], one[:, each:]
        es_ref[...], eo_ref[...] = by_core(core, nn(h_flip[...], gp[...]), fine, fine)
        eb_ref[...] = nn(jnp.ones((8, rows), bf16), gp[...])

        @pl.when(step == steps - 1)
        def _():
            if not final:
                for i in range(3):
                    copy(i).wait()
                return
            gains = jnp.zeros((1, width), f32)
            shifts, merges = gains, gains
            for start in starts:
                at = pl.ds(start, tall)
                x, ok = after[at, :], valid(start)
                out_ref[at, :] = (ok * (x + branch[at, :] + vec_ref[3:4, :])).astype(bf16)
                unit, inverse = norm_unit(x)
                upstream = up[at, :]
                gains = gains + jnp.sum(upstream * unit, axis=0, keepdims=True)
                shifts = shifts + jnp.sum(upstream, axis=0, keepdims=True)
                pulled = norm_pull(upstream, unit, inverse, vec_ref[1:2, :])
                two = ok * cot_ref[at, :].astype(f32) + pulled
                two_ref[at, :] = two
                low = two.astype(bf16)
                g[at, :] = low
                merges = merges + column_sums(low)
                cross_ref[at, :] = nt(low, merge_ref[...]).astype(bf16)
            ms_ref[...], mo_ref[...] = by_core(core, tn(mixed_ref[...], g[...]), fine, fine)
            sums_ref[1:2, :], sums_ref[2:3, :], sums_ref[3:4, :] = gains, shifts, merges

    base = steps if final else 0

    def once(shape):
        return pl.BlockSpec(shape, lambda i, info: (0, 0), pipeline_mode=pl.Buffered(1))

    def fixed(shape):
        return pl.BlockSpec(shape, lambda i, info: (0,) * len(shape))

    each = hidden // owners // fine
    pairs = others // 2 // steps
    by_row = pl.BlockSpec((2, pairs, each, fine, PIECE), lambda i, info: (0, i, 0, 0, 0))
    by_column = pl.BlockSpec((others, 1, fine, PIECE), lambda i, info: (0, i, 0, 0))
    merged = (others, width // PIECE, fine, PIECE)
    hbm = pl.BlockSpec(memory_space=pltpu.HBM)
    full = (rows, width)
    shared_shapes = [
        *[Shape((2, others // 2, each, fine, PIECE), bf16)] * 2,
        *[Shape((others, steps, fine, PIECE), bf16)] * 2,
        Shape((8, hidden // 2), f32), Shape((8, width), f32),
    ]
    shared_specs = [
        by_row, by_row, by_column, by_column,
        pl.BlockSpec((8, block), lambda i, info: (0, i)), fixed((8, width)),
    ]
    if final:
        shapes = [Shape(full, bf16), Shape(full, f32), Shape(full, bf16), Shape(merged, bf16), Shape(merged, bf16)]
        specs = [fixed(full)] * 3 + [fixed(merged)] * 2
    else:
        shapes, specs = [Shape(full, f32)] * 3, [hbm] * 3
    return pl.pallas_call(
        body,
        out_shape=shapes + shared_shapes,
        grid_spec=pltpu.PrefetchScalarGridSpec(
            num_scalar_prefetch=1,
            grid=(steps,),
            in_specs=[
                once(full), once(full), once((width, width)), once(full), once((8, width)),
                pl.BlockSpec((width, block), lambda i, info: (0, base + i)),
                pl.BlockSpec((1, block), lambda i, info: (0, base + i)),
                pl.BlockSpec((block, width), lambda i, info: (base + i, 0)),
            ] + ([hbm] * 2 if final else []),
            out_specs=specs + shared_specs,
            scratch_shapes=[
                pltpu.VMEM(full, bf16), pltpu.VMEM((width, rows), bf16), pltpu.VMEM(full, bf16),
                pltpu.VMEM(full, f32), pltpu.VMEM(full, f32),
                pltpu.VMEM((rows, block), bf16), pltpu.VMEM((rows, block), bf16),
                pltpu.SemaphoreType.DMA((3,)),
            ] + ([] if final else [pltpu.VMEM(full, f32)]),
        ),
        cost_estimate=TINY,
        compiler_params=settings(60),
        name="feed_forward",
    )(
        info, *in_hbm(start_from, mixed, merge, cotangent), vectors,
        *in_hbm(expand), bias, *in_hbm(reduce), *(begun if final else ()),
    )


def streamed(name, body, info, inputs, outs, scratch=()):
    n, m = len(inputs), len(outs)

    def kernel(info_ref, *refs):
        ins, dests = refs[:n], refs[n : n + m]
        refs = refs[n + m :]
        held, made, refs = refs[:n], refs[n : n + m], refs[n + m :]
        in_sem, out_sem, *rest = refs
        loads = [pltpu.make_async_copy(ins[i], held[i], in_sem.at[i]) for i in range(n)]
        for load in loads:
            load.start()
        waited, stores = set(), {}

        def need(i):
            if i not in waited:
                loads[i].wait()
                waited.add(i)
            return held[i]

        def give(i, send=False):
            if send:
                stores[i] = pltpu.make_async_copy(made[i], dests[i], out_sem.at[i])
                stores[i].start()
            return made[i]

        body(info_ref, need, give, *rest)
        for i in range(m):
            stores[i].wait()

    anywhere = pl.BlockSpec(memory_space=pltpu.HBM)
    return pl.pallas_call(
        kernel,
        out_shape=[Shape(shape, kind) for shape, kind in outs],
        grid_spec=pltpu.PrefetchScalarGridSpec(
            num_scalar_prefetch=1,
            grid=(1,),
            in_specs=[anywhere] * n,
            out_specs=[anywhere] * m,
            scratch_shapes=[pltpu.VMEM(value.shape, value.dtype) for value in inputs]
            + [pltpu.VMEM(shape, kind) for shape, kind in outs]
            + [pltpu.SemaphoreType.DMA((n,)), pltpu.SemaphoreType.DMA((m,))]
            + list(scratch),
        ),
        cost_estimate=TINY,
        compiler_params=settings(60),
        name=name,
    )(info, *inputs)


def norm_project(name, info, tokens, weights, ways, vectors, keep):
    rows, width = tokens.shape
    n = len(weights)

    def body(info_ref, need, give):
        vec = need(1)
        for start in range(0, rows, 256):
            at = pl.ds(start, 256)
            unit, _ = norm_unit(need(0)[at, :].astype(f32))
            low = (unit * vec[0:1, :] + vec[1:2, :]).astype(bf16)
            if keep:
                give(n)[at, :] = low
            for i, (row, factor) in enumerate(ways):
                made = nn(low, need(2 + i)[...])
                if row is not None:
                    made = made + vec[row : row + 1, :]
                give(i)[at, :] = (made * factor).astype(bf16)
        for i in range(n + keep):
            give(i, True)

    return streamed(
        name, body, info, [tokens, vectors, *weights], [((rows, width), bf16)] * (n + keep),
    )


def output_project(info, mixed, tokens, output_weight, probe_weight, vectors):
    rows, width = tokens.shape

    def body(info_ref, need, give):
        vec = need(2)
        for start in range(0, rows, 256):
            at = pl.ds(start, 256)
            x = need(1)[at, :].astype(f32) + nn(need(0)[at, :], need(3)[...]) + vec[0:1, :]
            give(0)[at, :] = x
            unit, _ = norm_unit(x)
            low = (unit * vec[1:2, :] + vec[2:3, :]).astype(bf16)
            made = nn(low, need(4)[...]) + vec[3:4, :]
            give(1)[at, :] = (made * (HDIM**-0.5)).astype(bf16)
        give(0, True)
        give(1, True)

    return streamed(
        "output_project", body, info, [mixed, tokens, vectors, output_weight, probe_weight],
        [((rows, width), f32), ((rows, width), bf16)],
    )


def probe_backward(info, probe_low, probe_high, probe_weight, after_one, two, output_weight, mixed, vectors, owners):
    rows, width = after_one.shape
    half, tall, fine = width // 2, 256, width // owners

    def body(info_ref, need, give, hidden, low_grad):
        core = info_ref[0]
        left, right = need(0), need(1)
        weight = need(2)
        vec = need(7)
        x_ref, two_ref = need(3), need(4)
        gains = jnp.zeros((1, width), f32)
        shifts, outs = gains, gains
        for start in range(0, rows, tall):
            at = pl.ds(start, tall)
            up = nt(left[at, :], weight[:, :half]) + nt(right[at, :], weight[:, half:])
            unit, inverse = norm_unit(x_ref[at, :])
            hidden[at, :] = (unit * vec[0:1, :] + vec[1:2, :]).astype(bf16)
            gains = gains + jnp.sum(up * unit, axis=0, keepdims=True)
            shifts = shifts + jnp.sum(up, axis=0, keepdims=True)
            one = two_ref[at, :] + norm_pull(up, unit, inverse, vec[0:1, :])
            give(0)[at, :] = one
            low = one.astype(bf16)
            low_grad[at, :] = low
            outs = outs + column_sums(low)
            if start == 0:
                need(5)
            give(1)[at, :] = nt(low, need(5)[...]).astype(bf16)
        give(0, True)
        give(1, True)
        sums = give(4)
        sums[...] = jnp.zeros_like(sums)
        sums[0:1, :], sums[1:2, :], sums[2:3, :] = gains, shifts, outs
        sums[3:4, :half] = column_sums(left[...])
        sums[3:4, half:] = column_sums(right[...])
        give(4, True)
        mixed_ref = need(6)
        columns = (
            (0, 1, hidden, left[...]),
            (1, 2, hidden, right[...]),
            (2, 4, mixed_ref, low_grad[...]),
        )
        for begin, end, source, grads in columns:
            pair = by_core(core, tn(source[...], grads), fine, fine)
            give(2)[:, begin:end], give(3)[:, begin:end] = pair
        give(2, True)
        give(3, True)

    return streamed(
        "probe_backward",
        body,
        info,
        [probe_low, probe_high, probe_weight, after_one, two, output_weight, mixed, vectors],
        [
            ((rows, width), f32), ((rows, width), bf16),
            ((owners // 2, 4, fine, PIECE), bf16), ((owners // 2, 4, fine, PIECE), bf16),
            ((8, width), f32),
        ],
        [pltpu.VMEM((rows, width), bf16), pltpu.VMEM((rows, width), bf16)],
    )


def page_backward(
    info, key_low, key_high, value_low, value_high, page_rows, key_weight, value_weight, owners,
    patch_total,
):
    slots, width = page_rows.shape
    half, fine = width // 2, width // owners
    pieces = patch_total // owners // fine * (width // PIECE)

    def body(info_ref, need, give):
        core, page = info_ref[0], info_ref[3]
        kl, kh, vl, vh = need(0)[...], need(1)[...], need(2)[...], need(3)[...]
        rows_ref = need(4)
        for i, grads in enumerate((kl, kh, vl, vh)):
            pair = by_core(core, tn(rows_ref[...], grads), fine, fine)
            give(0)[:, i : i + 1], give(1)[:, i : i + 1] = pair
        wk, wv = need(5), need(6)
        total = nt(kl, wk[:, :half]) + nt(kh, wk[:, half:])
        total = total + nt(vl, wv[:, :half]) + nt(vh, wv[:, half:])
        pair = by_core(core, total, patch_total // owners, fine)
        each = pair[0].shape[0]
        at = pl.ds(pl.multiple_of(page * each, each), each)
        for which in range(2):
            give(which)[:, 4:] = jnp.zeros((owners // 2, pieces, fine, PIECE), bf16)
            give(which)[at, 4:] = pair[which]
            give(which, True)
        sums = give(2)
        sums[...] = jnp.zeros_like(sums)
        sums[0:1, :half] = column_sums(vl)
        sums[0:1, half:] = column_sums(vh)
        give(2, True)

    return streamed(
        "page_backward",
        body,
        info,
        [key_low, key_high, value_low, value_high, page_rows, key_weight, value_weight],
        [
            *[((owners // 2, 4 + pieces, fine, PIECE), bf16)] * 2, ((8, width), f32),
        ],
    )


def lead_upstream(info, keys, values, key_weight, value_weight, lead_tokens, vectors):
    rows, width = lead_tokens.shape
    half, tall = width // 2, 256

    def body(info_ref, need, give, hidden):
        kl, kh, vl, vh = need(0), need(1), need(2), need(3)
        wk, wv = need(4), need(5)
        x_ref, vec = need(6), need(7)
        gains = jnp.zeros((1, width), f32)
        shifts = gains
        for start in range(0, rows, tall):
            at = pl.ds(start, tall)
            up = nt(kl[at, :], wk[:, :half]) + nt(kh[at, :], wk[:, half:])
            up = up + nt(vl[at, :], wv[:, :half]) + nt(vh[at, :], wv[:, half:])
            give(0)[at, :] = up.astype(bf16)
            unit, _ = norm_unit(x_ref[at, :].astype(f32))
            hidden[at, :] = (unit * vec[0:1, :] + vec[1:2, :]).astype(bf16)
            gains = gains + jnp.sum(up * unit, axis=0, keepdims=True)
            shifts = shifts + jnp.sum(up, axis=0, keepdims=True)
        give(0, True)
        sums = give(2)
        sums[...] = jnp.zeros_like(sums)
        sums[0:1, :], sums[1:2, :] = gains, shifts
        sums[2:3, :half], sums[2:3, half:] = column_sums(vl[...]), column_sums(vh[...])
        give(2, True)
        for i, ref in enumerate((kl, kh, vl, vh)):
            give(1)[:, i * half : (i + 1) * half] = tn(hidden[...], ref[...]).astype(bf16)
        give(1, True)

    return streamed(
        "lead_upstream",
        body,
        info,
        [*keys, *values, key_weight, value_weight, lead_tokens, vectors],
        [((rows, width), bf16), ((width, 2 * width), bf16), ((8, width), f32)],
        [pltpu.VMEM((rows, width), bf16)],
    )


def projection_grads(info, hidden, query_grad, key_grad, value_grad, lead_part, high, owners):
    rows, width = hidden.shape
    half, fine = width // 2, width // owners
    column = half if high else 0

    def body(info_ref, need, give):
        core = info_ref[0]
        h = need(0)
        for i in range(3):
            total = tn(h[...], need(1 + i)[...])
            if i:
                base = (i - 1) * width + column
                total = total + need(4)[:, base : base + half].astype(f32)
            pair = by_core(core, total, fine, fine)
            give(0)[:, i : i + 1], give(1)[:, i : i + 1] = pair
        give(0, True)
        give(1, True)

    return streamed(
        "projection_grads",
        body,
        info,
        [hidden, query_grad, key_grad, value_grad, lead_part],
        [((owners // 2, 3, fine, PIECE), bf16)] * 2,
    )


def first_norm_backward(info, queries, keys, values, weights, tokens, one, returned, vectors):
    rows, width = tokens.shape
    half, tall = width // 2, 256

    def body(info_ref, need, give):
        grads = [need(i) for i in range(6)]
        vec = need(10)
        gains = jnp.zeros((1, width), f32)
        shifts = gains
        for start in range(0, rows, tall):
            at = pl.ds(start, tall)
            up = 0.0
            for i in range(3):
                up = up + nt(grads[2 * i][at, :], need(6 + i)[:, :half])
                up = up + nt(grads[2 * i + 1][at, :], need(6 + i)[:, half:])
            unit, inverse = norm_unit(need(9)[at, :].astype(f32))
            gains = gains + jnp.sum(up * unit, axis=0, keepdims=True)
            shifts = shifts + jnp.sum(up, axis=0, keepdims=True)
            up = up + need(12)[at, :].astype(f32)
            give(0)[at, :] = need(11)[at, :] + norm_pull(up, unit, inverse, vec[0:1, :])
        give(0, True)
        sums = give(1)
        sums[...] = jnp.zeros_like(sums)
        sums[0:1, :], sums[1:2, :] = gains, shifts
        sums[2:3, :half], sums[2:3, half:] = column_sums(grads[0][...]), column_sums(grads[1][...])
        sums[3:4, :half], sums[3:4, half:] = column_sums(grads[4][...]), column_sums(grads[5][...])
        give(1, True)

    return streamed(
        "first_norm_backward", body, info,
        [*queries, *keys, *values, *weights, tokens, vectors, one, returned],
        [((rows, width), f32), ((8, width), f32)],
    )


def digit_axes():
    patch_bits = lax.axis_size("patch").bit_length() - 1
    return [("tok", 0)] + [("patch", bit) for bit in reversed(range(patch_bits))]


def my_digit(axis, bit):
    return (lax.axis_index(axis) >> bit) & 1


def tied(*values):
    return lax.optimization_barrier(values)


FIRST_DIGIT = 4


class Gather:
    def __init__(self, block):
        every = digit_axes()
        self.order = every[-2:0:-1] + every[:1] + every[-1:]
        self.held, self.at = block[None], 2
        one, two = self.order[:2]
        self.arrived = [hop(self.held, steps) for steps in ([one], [two], [one, two])]

    def step(self, chain):
        chain, arrived = tied(chain, self.arrived)
        self.held = jnp.concatenate([self.held, *arrived], axis=0)
        if self.at < len(self.order):
            chain, self.held = tied(chain, self.held)
            self.arrived = [hop(self.held, self.order[self.at : self.at + 1])]
        self.at += 1
        return chain

    def rest(self, chain):
        while self.at <= len(self.order):
            chain = self.step(chain)
        return chain

    def places(self, first, count):
        digits = digit_axes()
        device = first + jnp.arange(count, dtype=jnp.int32)
        place = jnp.zeros((count,), jnp.int32)
        for i, one in enumerate(self.order):
            theirs = (device >> (len(digits) - 1 - digits.index(one))) & 1
            place = place | ((theirs ^ my_digit(*one)) << i)
        return place.astype(jnp.int32)


def page_forward(places, blocks, key_weight, value_weight, value_bias):
    count, (each, width) = places.shape[0], blocks.shape[1:]
    slots = count * each

    def body(place_ref, blocks_ref, wk_ref, wv_ref, bias_ref, rows_out, k_out, v_out, rows, wk, wv, k, v, sems):
        copies = [
            pltpu.make_async_copy(
                blocks_ref.at[place_ref[i]], rows.at[pl.ds(i * each, each)], sems.at[i]
            )
            for i in range(count)
        ]
        copies.append(pltpu.make_async_copy(wk_ref, wk, sems.at[count]))
        copies.append(pltpu.make_async_copy(wv_ref, wv, sems.at[count + 1]))
        for copy in copies:
            copy.start()
        for copy in copies[:-1]:
            copy.wait()
        stores = [pltpu.make_async_copy(rows, rows_out, sems.at[count + 2])]
        stores[0].start()
        k[...] = nn(rows[...], wk[...]).astype(bf16)
        stores.append(pltpu.make_async_copy(k, k_out, sems.at[count + 3]))
        stores[1].start()
        copies[-1].wait()
        v[...] = (nn(rows[...], wv[...]) + bias_ref[...]).astype(bf16)
        stores.append(pltpu.make_async_copy(v, v_out, sems.at[count + 4]))
        stores[2].start()
        for store in stores:
            store.wait()

    hbm = pl.BlockSpec(memory_space=pltpu.HBM)
    return pl.pallas_call(
        body,
        out_shape=[Shape((slots, width), bf16)] * 3,
        grid_spec=pltpu.PrefetchScalarGridSpec(
            num_scalar_prefetch=1,
            grid=(1,),
            in_specs=[hbm] * 3 + [pl.BlockSpec((1, width), lambda i, places: (0, 0))],
            out_specs=[hbm] * 3,
            scratch_shapes=[
                pltpu.VMEM((slots, width), bf16), pltpu.VMEM((width, width), bf16),
                pltpu.VMEM((width, width), bf16), pltpu.VMEM((slots, width), bf16),
                pltpu.VMEM((slots, width), bf16), pltpu.SemaphoreType.DMA((count + 5,)),
            ],
        ),
        cost_estimate=TINY,
        compiler_params=settings(),
        name="page_forward",
    )(places, blocks, key_weight, value_weight, value_bias)


class Part:
    def __init__(self, kept, tok_first, place, start=0, pieces=None):
        self.tok_first, self.place = tok_first, place
        self.pieces = pieces or kept.shape[1]
        self.terms = [(kept, owner_digits(), start)]


def owner_digits():
    return digit_axes()[:-1]


def stages_of(tok_first, direct):
    every = digit_axes()
    bits = every[-2:0:-1]
    loose, last = bits[: max(len(bits) - 2, 0)], bits[max(len(bits) - 2, 0) :]
    singles = [[one] for one in loose]
    ends = [last] if direct else [[one] for one in last]
    return ([every[:1]] + singles if tok_first else singles + [every[:1]]) + ends


class Sum:
    def __init__(self, direct, *sent):
        self.direct = direct
        self.parts = [part for _, parts in sent for part in parts]
        self.at = 0
        self.leaving = [array for array, _ in sent]
        self.hops = [[("patch", 0)]] * len(sent)
        self.groups = [parts for _, parts in sent]
        self.mine = self.came = None

    def send(self):
        self.arrived = [hop(value, steps) for value, steps in zip(self.leaving, self.hops)]

    def free(self, part, at):
        settled = [one for stage in stages_of(part.tok_first, self.direct)[:at] for one in stage]
        return [one for one in owner_digits() if one not in settled]

    def absorb(self, arrived):
        if self.mine is not None:
            self.came = arrived
            self.leaving = None
            return []
        for value, group in zip(arrived, self.groups):
            start = 0
            for part in group:
                part.terms = part.terms + [(value, self.free(part, self.at), start)]
                start += part.pieces
        stages = [stages_of(part.tok_first, self.direct) for part in self.parts]
        last = self.at == len(stages[0]) - 1
        ways = [stage[self.at] for stage in stages]
        self.at += 1
        jobs, self.hops, self.groups = [], [], []
        for digits in [way for i, way in enumerate(ways) if way not in ways[:i]]:
            group = [part for part, way in zip(self.parts, ways) if way == digits]
            free = self.free(group[0], self.at)
            for flips in range(0 if last else 1, 1 << len(digits)):
                flipped = [one for i, one in enumerate(digits) if flips >> i & 1]
                choices = []
                for chunk in range(1 << len(free)):
                    bits = {one: chunk >> (len(free) - 1 - i) & 1 for i, one in enumerate(free)}
                    choices.append((bits, flipped))
                terms = [(part.terms, part.pieces) for part in group]
                jobs.append((terms, choices, bf16 if flips else f32))
                if flips:
                    self.hops.append(flipped)
                    self.groups.append(group)
        return jobs

    def take(self, made):
        if self.at == len(stages_of(True, self.direct)):
            self.mine = made[0]
            made = made[1:]
        self.leaving = list(made)


def hop(value, steps):
    axis = steps[0][0]
    flip = sum(1 << bit for _, bit in steps)
    return lax.ppermute(value, axis, [(i, i ^ flip) for i in range(lax.axis_size(axis))])


def finished(shapes, *totals):
    arrays = [one for total in totals for one in [total.mine, *total.came]]

    def body(*refs):
        refs, outs = list(refs[: len(arrays)]), refs[len(arrays) :]
        for total in totals:
            mine_ref, *came = refs[: 1 + len(total.came)]
            refs = refs[1 + len(total.came) :]
            piece = 0
            for part in total.parts:
                out, at_column = part.place
                fine = mine_ref.shape[2]
                tall = shapes[out][0] // fine
                for p in range(part.pieces):
                    sum_here = mine_ref[0, piece]
                    for ref in came:
                        sum_here = sum_here + ref[0, piece].astype(f32)
                    row, column = p % tall * fine, at_column + p // tall * PIECE
                    outs[out][row : row + fine, column : column + PIECE] = sum_here
                    piece += 1

    return pl.pallas_call(
        body,
        out_shape=[Shape(shape, f32) for shape in shapes],
        cost_estimate=TINY,
        compiler_params=pltpu.CompilerParams(vmem_limit_bytes=40 * MIB),
        name="finished",
    )(*arrays)


def added_up(info, jobs):
    digits = digit_axes()
    arrays, known = [], {}
    for parts, _, _ in jobs:
        for terms, _ in parts:
            for value, _, _ in terms:
                if id(value) not in known:
                    known[id(value)] = len(arrays)
                    arrays.append(value)
    fine = arrays[0].shape[2]
    units = [(job, part) for job in range(len(jobs)) for part in range(len(jobs[job][0]))]
    loads = sum(len(jobs[job][0][part][0]) * len(jobs[job][1]) for job, part in units)

    def body(info_ref, *refs):
        n, m, k = len(arrays), len(jobs), len(units)
        ins, dests = refs[:n], refs[n : n + m]
        held, made = refs[n + m : n + m + k], refs[n + m + k : n + 2 * m + k]
        in_sem, out_sem = refs[n + 2 * m + k :]
        mine = {one: info_ref[FIRST_DIGIT + i] for i, one in enumerate(digits)}
        copies, count = [], 0
        for unit, (job, part) in enumerate(units):
            terms, pieces = jobs[job][0][part]
            copies.append([])
            for t, (value, free, start) in enumerate(terms):
                for c, (bits, flipped) in enumerate(jobs[job][1]):
                    index = 0
                    for one in free:
                        digit = bits[one] if one in bits else mine[one]
                        digit = 1 - digit if one in flipped else digit
                        index = 2 * index + digit
                    copy = pltpu.make_async_copy(
                        ins[known[id(value)]].at[index, pl.ds(start, pieces)],
                        held[unit].at[t, c],
                        in_sem.at[count],
                    )
                    copy.start()
                    copies[-1].append(copy)
                    count += 1
        offsets = [0] * m
        left = [len(jobs[job][0]) for job in range(m)]
        stores = []
        for unit, (job, part) in enumerate(units):
            terms, pieces = jobs[job][0][part]
            for copy in copies[unit]:
                copy.wait()
            offset = offsets[job]

            batch = max(one for one in range(1, 9) if pieces % one == 0)
            per = pieces // batch

            def step(i, _, unit=unit, job=job, count=len(terms), per=per, batch=batch, offset=offset):
                chunk = i // per
                for p in range(batch):
                    piece = i % per * batch + p
                    total = held[unit][0, chunk, piece].astype(f32)
                    for t in range(1, count):
                        total = total + held[unit][t, chunk, piece].astype(f32)
                    made[job][chunk, offset + piece] = total.astype(jobs[job][2])
                return 0

            lax.fori_loop(0, len(jobs[job][1]) * per, step, 0)
            offsets[job] += pieces
            left[job] -= 1
            if not left[job]:
                stores.append(pltpu.make_async_copy(made[job], dests[job], out_sem.at[job]))
                stores[-1].start()
        for store in stores:
            store.wait()

    anywhere = pl.BlockSpec(memory_space=pltpu.HBM)
    shapes = [
        ((len(choices), sum(pieces for _, pieces in parts), fine, PIECE), kind)
        for parts, choices, kind in jobs
    ]
    held = [
        pltpu.VMEM(
            (len(jobs[job][0][part][0]), len(jobs[job][1]), jobs[job][0][part][1], fine, PIECE), bf16
        )
        for job, part in units
    ]
    return pl.pallas_call(
        body,
        out_shape=[Shape(shape, kind) for shape, kind in shapes],
        grid_spec=pltpu.PrefetchScalarGridSpec(
            num_scalar_prefetch=1,
            grid=(1,),
            in_specs=[anywhere] * len(arrays),
            out_specs=[pl.BlockSpec(memory_space=pltpu.HBM)] * len(jobs),
            scratch_shapes=held
            + [pltpu.VMEM(shape, kind) for shape, kind in shapes]
            + [pltpu.SemaphoreType.DMA((loads,)), pltpu.SemaphoreType.DMA((len(jobs),))],
        ),
        cost_estimate=TINY,
        compiler_params=settings(60),
        name="added_up",
    )(info, *arrays)


def advance(info, chain, moving=(), fresh=()):
    moving = [one for one in moving if one.leaving is not None]
    chain, arrived = tied(chain, [one.arrived for one in moving])
    jobs, owners = [], []
    for one, values in zip(moving, arrived):
        new = one.absorb(values)
        owners.append((one, len(new)))
        jobs += new
    if jobs:
        made = added_up(info, jobs)
        for one, count in owners:
            if count:
                one.take(made[:count])
                made = made[count:]
    going = [one for one in moving + list(fresh) if one.leaving is not None]
    chain, leaving = tied(chain, [one.leaving for one in going])
    for one, values in zip(going, leaving):
        one.leaving = values
        one.send()
    return chain


def vector_table(feed, expand_bias, probe, page, lead, first):
    width = feed.shape[1]

    def body(feed_ref, bias_ref, probe_ref, page_ref, lead_ref, first_ref, out):
        rows = [
            first_ref[0:1, :] + lead_ref[0:1, :],
            first_ref[1:2, :] + lead_ref[1:2, :],
            first_ref[2:3, :],
            first_ref[3:4, :] + lead_ref[2:3, :],
            probe_ref[2:3, :],
            probe_ref[0:1, :],
            probe_ref[1:2, :],
            probe_ref[3:4, :],
            page_ref[0:1, :],
            feed_ref[3:4, :],
            feed_ref[1:2, :],
            feed_ref[2:3, :],
            feed_ref[0:1, :],
        ]
        out[...] = jnp.zeros_like(out)
        for i, row in enumerate(rows):
            out[i : i + 1, :] = row
        out[16 : 16 + bias_ref.shape[0], :] = bias_ref[...]

    return pl.pallas_call(
        body,
        out_shape=jax.ShapeDtypeStruct((24, width), f32),
        cost_estimate=TINY,
        name="vector_table",
    )(feed, expand_bias, probe, page, lead, first)


def scatter_rows(table, width, first, last):
    digits = digit_axes()
    fine = width >> len(digits)
    for axis, bit in digits[first:last]:
        half = table.shape[1] // 2
        if half % LANES:
            table = table + hop(table, [(axis, bit)])
        else:
            digit = my_digit(axis, bit)
            keep = lax.dynamic_slice_in_dim(table, digit * half, half, 1)
            give = lax.dynamic_slice_in_dim(table, (1 - digit) * half, half, 1)
            table = keep + hop(give, [(axis, bit)])
    if last < len(digits):
        return table
    inside = 0
    for axis, bit in digits[(table.shape[1] // fine).bit_length() * -1 + 1 :]:
        inside = 2 * inside + my_digit(axis, bit)
    return lax.dynamic_slice_in_dim(table, inside * fine, fine, 1)


def pick_entry(table, position):
    indices = jnp.arange(table.shape[0], dtype=jnp.int32)
    return jnp.sum(jnp.where(indices == position, table, 0))


def rows_of(*vectors):
    rows = jnp.stack(vectors, axis=0)
    return jnp.pad(rows, ((0, 8 - len(vectors)), (0, 0)))


def local(
    tokens,
    patches,
    cotangent,
    lengths,
    page_of,
    page_counts,
    self_gain,
    self_shift,
    query_weight,
    query_bias,
    key_weight,
    value_weight,
    value_bias,
    output_weight,
    output_bias,
    cross_gain,
    cross_shift,
    probe_weight,
    probe_bias,
    source_key,
    source_value,
    source_bias,
    merge_weight,
    merge_bias,
    feed_gain,
    feed_shift,
    expand_weight,
    expand_bias,
    reduce_weight,
    reduce_bias,
):
    head_scale = HDIM ** (-0.5)
    tok_index = lax.axis_index("tok").astype(jnp.int32)
    sequence = lax.axis_index("patch")
    core = my_digit("patch", 0).astype(jnp.int32)
    row_count, model_width = tokens.shape[1:]
    lead_tokens = lax.ppermute(tokens[0], "tok", [(0, 1)])
    page_index = pick_entry(page_of, sequence)
    filled = pick_entry(page_counts, page_index).reshape(1)
    trailing = tok_index.reshape(1)
    page_start = page_index * PAGE_SLOTS
    digits = [my_digit(*one).astype(jnp.int32) for one in digit_axes()]
    owners = 1 << len(digits)
    info = jnp.stack(
        [core, tok_index * row_count, pick_entry(lengths, sequence), page_index] + digits
    )
    self_vectors = rows_of(self_gain, self_shift, query_bias, value_bias)
    cross_vectors = rows_of(cross_gain, cross_shift)
    output_vectors = rows_of(output_bias, cross_gain, cross_shift, probe_bias)
    feed_vectors = rows_of(merge_bias, feed_gain, feed_shift, reduce_bias)

    gather = Gather(patches)
    nothing = jnp.zeros((1,), jnp.int32)
    query, own_keys, own_values, hidden_one = norm_project(
        "own_project", nothing, tokens[0], [query_weight, key_weight, value_weight],
        [(2, head_scale), (None, 1.0), (3, 1.0)], self_vectors, True,
    )
    query = gather.step(query)
    own_mixed, own_total = own_forward(query, own_keys, own_values)
    small = (info, filled, cross_vectors, feed_vectors, output_vectors)
    lead_tokens, own_mixed, small = gather.step((lead_tokens, own_mixed, small))
    info, filled, cross_vectors, feed_vectors, output_vectors = small
    lead_keys, lead_values = norm_project(
        "lead_project", nothing, lead_tokens, [key_weight, value_weight],
        [(None, 1.0), (3, 1.0)], self_vectors, False,
    )
    self_mixed, self_total = lead_forward(
        query, lead_keys, lead_values, own_mixed, own_total, trailing
    )
    self_mixed = gather.step(self_mixed)
    after_one, probe = output_project(
        nothing, self_mixed, tokens[0], output_weight, probe_weight, output_vectors
    )
    probe = gather.rest(probe)
    page_rows, page_keys, page_values = page_forward(
        gather.places(page_start // patches.shape[0], PAGE_SLOTS // patches.shape[0]),
        gather.held, source_key, source_value, source_bias[None],
    )
    cross_mixed, cross_total = cross_forward(probe, page_keys, page_values, filled)

    feed_args = (
        cross_mixed, merge_weight, cotangent[0], feed_vectors, expand_weight, expand_bias[None],
        reduce_weight, info, owners,
    )
    branch, upstream, after_two, *fed = feed_forward(after_one, *feed_args, None)
    fine = model_width // owners
    deep = expand_weight.shape[1] // 2

    def by_owner(value):
        return value.reshape((-1,) + value.shape[2:])

    first = Sum(
        False,
        (fed[2], [Part(fed[3], True, (0, 0))]),
        (by_owner(fed[0]), [Part(by_owner(fed[1]), False, (1, 0))]),
    )
    low_bias, low_sums = fed[4:]
    after_two, branch, upstream = advance(info, (after_two, branch, upstream), [], [first])
    block_output, grad_two, grad_cross_out, *fed = feed_forward(
        after_two, *feed_args, (branch, upstream)
    )
    second = Sum(
        False,
        (fed[4], [Part(fed[5], True, (0, deep))]),
        (by_owner(fed[2]), [Part(by_owner(fed[3]), False, (2, 0))]),
        (fed[0], [Part(fed[1], False, (3, 0))]),
    )
    expand_bias_sums = jnp.concatenate([low_bias[0], fed[6][0]])
    feed_sums = fed[7]

    half_pairs = model_width // PAIR // 2
    cross_args = (probe, page_keys, page_values, cross_mixed, cross_total)
    grad_cross_out = advance(info, grad_cross_out, [first], [second])
    low = cross_backward(*cross_args, grad_cross_out, filled, 0, half_pairs)
    low, grad_cross_out = advance(info, (low, grad_cross_out), [second])
    high = cross_backward(*cross_args, grad_cross_out, filled, half_pairs, half_pairs)
    low, high = advance(info, (low, high), [first])
    patch_total = patches.shape[0] * lax.axis_size(("tok", "patch"))
    paged = page_backward(
        info, low[1], high[1], low[2], high[2], page_rows, source_key, source_value, owners,
        patch_total,
    )
    probed = probe_backward(
        info, low[0], high[0], probe_weight, after_one, grad_two, output_weight, self_mixed,
        cross_vectors, owners,
    )
    grad_one, grad_self_out, probe_sums = probed[0], probed[1], probed[4]
    third = Sum(
        False,
        (
            paged[0],
            [Part(paged[1], True, (0, 0), 0, 4), Part(paged[1], False, (1, 0), 4, paged[1].shape[1] - 4)],
        ),
        (probed[2], [Part(probed[3], False, (2, 0))]),
    )
    self_args = (query, lead_keys, lead_values, self_mixed, self_total)
    own_args = (query, own_keys, own_values, self_mixed, self_total)
    bias_rows = expand_bias_sums.reshape(owners, -1, fine)
    bias_rows = jnp.transpose(bias_rows, (1, 0, 2)).reshape(-1, model_width)
    grad_self_out, bias_rows = advance(
        info, (grad_self_out, bias_rows), [first, second], [third]
    )
    lead_low = lead_backward(*self_args, grad_self_out, trailing, 0, half_pairs)
    lead_low, grad_self_out = advance(info, (lead_low, grad_self_out), [first, second, third])
    lead_high = lead_backward(*self_args, grad_self_out, trailing, half_pairs, half_pairs)
    led_grad, led_part, lead_sums = lead_upstream(
        info, (lead_low[1], lead_high[1]), (lead_low[2], lead_high[2]), key_weight,
        value_weight, lead_tokens, self_vectors,
    )
    led_grad, led_part, grad_self_out = advance(
        info, (led_grad, led_part, grad_self_out), [first, second, third]
    )
    returned = lax.ppermute(led_grad, "tok", [(1, 0)])
    own_low = own_backward(*own_args, grad_self_out, lead_low[0], 0, half_pairs)
    own_low, grad_self_out = advance(info, (own_low, grad_self_out), [second, third])
    parts = projection_grads(info, hidden_one, *own_low, led_part, False, owners)
    half = model_width // 2
    fourth = Sum(False, (parts[0], [Part(parts[1], i == 1, (i, 0), i, 1) for i in range(3)]))
    own_low, grad_self_out = advance(info, (own_low, grad_self_out), [], [fourth])
    own_high = own_backward(*own_args, grad_self_out, lead_high[0], half_pairs, half_pairs)
    own_low, own_high, returned = advance(
        info, (own_low, own_high, returned), [third, fourth]
    )
    tokens_grad, first_sums = first_norm_backward(
        info, (own_low[0], own_high[0]), (own_low[1], own_high[1]), (own_low[2], own_high[2]),
        (query_weight, key_weight, value_weight), tokens[0], grad_one, returned, self_vectors,
    )
    first_sums, own_high, led_part = advance(
        info, (first_sums, own_high, led_part), [third, fourth]
    )
    parts = projection_grads(info, hidden_one, *own_high, led_part, True, owners)
    table = vector_table(feed_sums, bias_rows, probe_sums, paged[2], lead_sums, first_sums)
    table = scatter_rows(table, model_width, 0, 1)
    fifth = Sum(True, (parts[0], [Part(parts[1], i != 1, (i, half), i, 1) for i in range(3)]))
    table = advance(info, table, [fourth], [fifth])
    table = scatter_rows(table, model_width, 1, 2)
    table = advance(info, table, [fourth, fifth])
    table = scatter_rows(table, model_width, 2, 3)
    table = advance(info, table, [fourth, fifth])
    table = scatter_rows(table, model_width, 3, len(digits) - 1)
    table = advance(info, table, [fourth, fifth])
    sums = scatter_rows(table, model_width, len(digits) - 1, len(digits))
    totals = [first, second, third, fourth, fifth]
    while any(one.leaving is not None for one in totals):
        sums = advance(info, sums, totals)
    tall = expand_weight.shape[1] // owners
    model, half_reduce = (fine, model_width), (tall, half)
    expand_grad, reduce_low, reduce_high, merge_grad = finished(
        [(fine, expand_weight.shape[1]), half_reduce, half_reduce, model], first, second
    )
    is_first = tok_index == 0
    given = jnp.where(is_first, reduce_high, reduce_low).astype(bf16)
    taken = hop(given, [("tok", 0)]).astype(f32)
    reduce_grad = jnp.concatenate(
        [jnp.where(is_first, reduce_low, taken), jnp.where(is_first, taken, reduce_high)], axis=1
    )
    source_grads, patches_grad, middle_grads = finished(
        [(fine, 2 * model_width), (patches.shape[0], model_width), (fine, 2 * model_width)], third
    )
    projections = finished([model] * 3, fourth, fifth)
    return (
        block_output[None],
        tokens_grad[None],
        patches_grad,
        sums[0],
        sums[1],
        projections[0],
        sums[2],
        projections[1],
        projections[2],
        sums[3],
        middle_grads[:, model_width:],
        sums[4],
        sums[5],
        sums[6],
        middle_grads[:, :model_width],
        sums[7],
        source_grads[:, :model_width],
        source_grads[:, model_width:],
        sums[8],
        merge_grad,
        sums[9],
        sums[10],
        sums[11],
        expand_grad,
        sums[16 : 16 + expand_bias.shape[0] // model_width].reshape(-1),
        reduce_grad,
        sums[12],
    )


def solution(mesh):
    placed = (
        P("patch", "tok", None),
        P(("tok", "patch"), None),
        P("patch", "tok", None),
        P(),
        P(),
        P(),
        P(),
        P(),
        P(),
        P(),
        P(),
        P(),
        P(),
        P(),
        P(),
        P(),
        P(),
        P(),
        P(),
        P(),
        P(),
        P(),
        P(),
        P(),
        P(),
        P(),
        P(),
        P(),
        P(),
        P(),
    )
    return jax.shard_map(
        local,
        mesh=mesh,
        in_specs=placed,
        out_specs=(
            P("patch", "tok", None),
            P("patch", "tok", None),
            P(("tok", "patch"), None),
            P(("tok", "patch")),
            P(("tok", "patch")),
            P(("tok", "patch"), None),
            P(("tok", "patch")),
            P(("tok", "patch"), None),
            P(("tok", "patch"), None),
            P(("tok", "patch")),
            P(("tok", "patch"), None),
            P(("tok", "patch")),
            P(("tok", "patch")),
            P(("tok", "patch")),
            P(("tok", "patch"), None),
            P(("tok", "patch")),
            P(("tok", "patch"), None),
            P(("tok", "patch"), None),
            P(("tok", "patch")),
            P(("tok", "patch"), None),
            P(("tok", "patch")),
            P(("tok", "patch")),
            P(("tok", "patch")),
            P(("tok", "patch"), None),
            P(("tok", "patch")),
            P(("tok", "patch"), None),
            P(("tok", "patch")),
        ),
        check_vma=False,
    )
```
